32 devices in a mesh: nodes: 8 (over y, x, core), shard: 4 (over z).
Axes of the slice: x: 2, y: 2, z: 4, core: 2. Of those that a mesh axis runs over, the one named last changes fastest.
Arguments:
- node_feats: bfloat16 [65536, 512], P(('nodes', 'shard')), may hold values from -6 to 6
- cotangent: bfloat16 [65536, 512], P(('nodes', 'shard')), may hold values from -6 to 6
- batch_ids: int32 [65536], P(('nodes', 'shard')), may hold values from 0 to 3, as said below
- valid_counts: int32 [32], P(('nodes', 'shard')), may hold values from 1024 to 2048, as said below
- proj_master: float32 [512, 2048], P('shard'), may hold values from -0.25 to 0.25
- proj_moment: float32 [512, 2048], P('shard'), may hold values from -0.25 to 0.25
- proj_square: float32 [512, 2048], P('shard'), may hold values from 0.0001 to 0.002
- out_master: float32 [512, 512], P('shard'), may hold values from -0.25 to 0.25
- out_moment: float32 [512, 512], P('shard'), may hold values from -0.25 to 0.25
- out_square: float32 [512, 512], P('shard'), may hold values from 0.0001 to 0.002
- norm_master: float32 [2, 512], P(None, 'shard')
- norm_moment: float32 [2, 512], P(None, 'shard'), may hold values from -0.5 to 0.5
- norm_square: float32 [2, 512], P(None, 'shard'), may hold values from 0.0002 to 0.01
Outputs:
- block_out: float32 [65536, 512], P(('nodes', 'shard'))
- input_grad: float32 [65536, 512], P(('nodes', 'shard'))
- global_norm: float32 [1], replicated
- moment_proj: float32 [512, 2048], P('shard')
- square_proj: float32 [512, 2048], P('shard')
- updated_proj: float32 [512, 2048], P('shard')
- copy_proj: bfloat16 [512, 2048], P('shard')
- moment_out: float32 [512, 512], P('shard')
- square_out: float32 [512, 512], P('shard')
- updated_out: float32 [512, 512], P('shard')
- copy_out: bfloat16 [512, 512], P('shard')
- clipped_norm: float32 [2, 512], P(None, 'shard')
- moment_norm: float32 [2, 512], P(None, 'shard')
- square_norm: float32 [2, 512], P(None, 'shard')
- updated_norm: float32 [2, 512], P(None, 'shard')
The draws below stay inside these ranges and needn't reach their ends.
Inputs may be any that keep to these rules, and one draw needn't show every extreme that they name: `batch_ids`: slots 0 to 3 of every device hold mini-batches 0 to 3 in order. `valid_counts`: entry i counts the valid leading slots of device i in nodes+shard order; some device has all 2048 slots valid.
All inputs are finite; a program needn't handle non-finite values.
Results may differ from the reference program's by a relative error of at most 0.0073.
Values may be sent and summed in bfloat16 or wider, within the bound.
No kernel may reach another device: no remote copies, remote signals or barrier semaphores. Data moves between devices by JAX's collectives and lax.ppermute only.
A program may use at most 128 MiB of HBM per device.

```python
import math
import jax
import jax.numpy as jnp
from jax import lax

D = 512
HEADS = 8
HEAD_DIM = 64
NODE_DEV = 2048
CLUSTERS = 4
STEP = 10
TOKENS = 65536


def draw_batch_ids(key, part):
    drawn = jax.random.randint(key, (TOKENS,), 0, CLUSTERS, dtype=jnp.int32)
    slot_index = jnp.arange(TOKENS, dtype=jnp.int32) % NODE_DEV
    return jnp.where(slot_index < CLUSTERS, slot_index, drawn).astype(jnp.int32)


def draw_valid_counts(key, part):
    key_one, key_two = jax.random.split(key)
    device_total = TOKENS // NODE_DEV
    drawn = jax.random.randint(key_one, (device_total,), NODE_DEV // 2, NODE_DEV + 1, dtype=jnp.int32)
    fullest = jax.random.randint(key_two, (), 0, device_total, dtype=jnp.int32)
    return jnp.where(jnp.arange(device_total, dtype=jnp.int32) == fullest, NODE_DEV, drawn).astype(jnp.int32)


def draw_norm_master(key, part):
    key_one, key_two = jax.random.split(key)
    gains = jax.random.uniform(key_one, (D,), jnp.float32, 0.5, 1.5)
    shifts = 0.3 * jax.random.normal(key_two, (D,), jnp.float32)
    return jnp.stack([gains, shifts]).astype(jnp.float32)


def steps_of(own_key, extent, cuts, smallest, high):
    loudness = 1.0
    for dim, parts in cuts:
        heights = jax.random.uniform(jax.random.fold_in(jax.random.fold_in(own_key, 6), dim), (parts,), jnp.float32, smallest / len(cuts), high / len(cuts))
        loudness = loudness * jnp.repeat(jnp.exp(heights), extent[dim] // parts).reshape((-1,) + (1,) * (len(extent) - 1 - dim))
    return loudness


def noise(key, extent, deviation, limit, cuts=(), kind=jnp.bfloat16):
    loudness = steps_of(key, extent, cuts, -0.22, 0.18) if cuts else 1.0
    values = jax.random.normal(key, extent, jnp.float32) * deviation * loudness
    return jnp.minimum(jnp.maximum(values, -limit), limit).astype(kind)


def setup_inputs(seed: int = 0) -> dict:
    streams_of = jax.random.split(jax.random.key(seed), 14)
    node_feats = noise(streams_of[0], (TOKENS, D), 1.0, 6.0, ((0, 32),))
    cotangent = noise(streams_of[1], (TOKENS, D), 1.0, 6.0, ((0, 32),))
    batch_ids = draw_batch_ids(jax.random.fold_in(streams_of[13], 71), 0)
    valid_counts = draw_valid_counts(jax.random.fold_in(streams_of[13], 71), 0)
    proj_master = noise(streams_of[4], (D, 4 * D), D ** -0.5, 0.25, ((0, 4),), jnp.float32)
    proj_moment = noise(streams_of[5], (D, 4 * D), 0.05, 0.25, ((0, 4),), jnp.float32)
    proj_square = jnp.clip(jnp.exp(math.log(0.002) - 2.9957323 * jax.random.uniform(streams_of[6], (D, 4 * D), jnp.float32) ** steps_of(streams_of[6], (D, 4 * D), ((0, 4),), -0.2, 0.2)), 0.0001, 0.002)
    out_master = noise(streams_of[7], (D, D), D ** -0.5, 0.25, ((0, 4),), jnp.float32)
    out_moment = noise(streams_of[8], (D, D), 0.05, 0.25, ((0, 4),), jnp.float32)
    out_square = jnp.clip(jnp.exp(math.log(0.002) - 2.9957323 * jax.random.uniform(streams_of[9], (D, D), jnp.float32) ** steps_of(streams_of[9], (D, D), ((0, 4),), -0.2, 0.2)), 0.0001, 0.002)
    norm_master = draw_norm_master(jax.random.fold_in(streams_of[13], 71), 0)
    norm_moment = noise(streams_of[11], (2, D), 0.1, 0.5, ((1, 4),), jnp.float32)
    norm_square = jnp.clip(jnp.exp(math.log(0.01) - 3.912023 * jax.random.uniform(streams_of[12], (2, D), jnp.float32) ** steps_of(streams_of[12], (2, D), ((1, 4),), -0.2, 0.2)), 0.0002, 0.01)
    return dict(node_feats=node_feats, cotangent=cotangent, batch_ids=batch_ids, valid_counts=valid_counts, proj_master=proj_master, proj_moment=proj_moment, proj_square=proj_square, out_master=out_master, out_moment=out_moment, out_square=out_square, norm_master=norm_master, norm_moment=norm_moment, norm_square=norm_square)


@jax.custom_vjp
def low(v):
    return lax.optimization_barrier(v.astype(jnp.bfloat16)).astype(jnp.float32)

@jax.custom_vjp
def low_back(v):
    return v

def low_keep(v):
    return (low(v), None)

def low_pass(kept, grad):
    return (grad,)

def back_keep(v):
    return (v, None)

def back_low(kept, grad):
    return (low(grad),)
low.defvjp(low_keep, low_pass)
low_back.defvjp(back_keep, back_low)
norm_eps = 1e-05
beta_one = 0.9
beta_two = 0.999
learn_rate = 0.05
norm_rate = 0.5
decay_rate = 0.01
adam_eps = 1e-08
highest = lax.Precision.HIGHEST

def matmul(left, right):
    return jnp.dot(left, right, precision=highest, preferred_element_type=jnp.float32)

def adam_update(master_w, moment_old, square_old, grad_in, clip_scale, decay_coef, step_rate):
    clipped = grad_in * clip_scale
    moment_new = beta_one * moment_old + (1.0 - beta_one) * clipped
    square_new = beta_two * square_old + (1.0 - beta_two) * clipped * clipped
    moment_hat = moment_new / (1.0 - beta_one ** STEP)
    square_hat = square_new / (1.0 - beta_two ** STEP)
    master_new = master_w * (1.0 - step_rate * decay_coef) - step_rate * moment_hat / (jnp.sqrt(square_hat) + adam_eps)
    return (clipped, moment_new, square_new, master_new)

def reference(node_feats, cotangent, batch_ids, valid_counts, proj_master, proj_moment, proj_square, out_master, out_moment, out_square, norm_master, norm_moment, norm_square):
    token_count = node_feats.shape[0]
    block_rows = math.gcd(token_count, 4096)
    block_count = token_count // block_rows
    positions = jnp.arange(token_count, dtype=jnp.int32)
    owners = (positions // NODE_DEV).astype(jnp.int32)
    valid_mask = (positions % NODE_DEV < valid_counts[owners]).astype(jnp.float32)
    member_table = (batch_ids[:, None] == jnp.arange(CLUSTERS, dtype=jnp.int32)[None, :]).astype(jnp.float32)
    feats = node_feats.astype(jnp.float32)
    cot_full = cotangent.astype(jnp.float32)
    proj_low = proj_master.astype(jnp.bfloat16).astype(jnp.float32)
    out_low = out_master.astype(jnp.bfloat16).astype(jnp.float32)
    norm_low = norm_master.astype(jnp.bfloat16).astype(jnp.float32)
    mask_blocks = valid_mask.reshape(block_count, block_rows)
    table_blocks = member_table.reshape(block_count, block_rows, CLUSTERS)

    def forward(feat_all, w_proj, w_out, w_norm):
        feat_blocks = feat_all.reshape(block_count, block_rows, D)

        def summary_block(running, pieces):
            feat_blk, mask_blk, table_blk = pieces
            key_pre = low_back(matmul(feat_blk, w_proj[:, D:2 * D]))
            value_pre = low_back(matmul(feat_blk, w_proj[:, 2 * D:3 * D]))
            key_rows = low(jax.nn.sigmoid(key_pre) * mask_blk[:, None])
            value_rows = low(value_pre)
            key_groups = (key_rows[:, None, :] * table_blk[:, :, None]).reshape(block_rows, CLUSTERS, HEADS, HEAD_DIM)
            kv_part = jnp.einsum('nchk,nhv->chkv', key_groups, value_rows.reshape(block_rows, HEADS, HEAD_DIM), precision=highest)
            ks_part = matmul(table_blk.T, key_rows)
            return ((running[0] + kv_part, running[1] + ks_part), None)
        initial = (jnp.zeros((CLUSTERS, HEADS, HEAD_DIM, HEAD_DIM), jnp.float32), jnp.zeros((CLUSTERS, D), jnp.float32))
        (summary, key_sum), unused = lax.scan(jax.checkpoint(summary_block), initial, (feat_blocks, mask_blocks, table_blocks))
        summary_low = low(low_back(summary))

        def output_block(pieces):
            feat_blk, mask_blk, table_blk = pieces
            query_pre = low_back(matmul(feat_blk, w_proj[:, :D]))
            gate_pre = low_back(matmul(feat_blk, w_proj[:, 3 * D:]))
            queries = low(jax.nn.sigmoid(query_pre))
            query_groups = (queries[:, None, :] * table_blk[:, :, None]).reshape(block_rows, CLUSTERS, HEADS, HEAD_DIM)
            numer = low_back(jnp.einsum('nchk,chkv->nhv', query_groups, summary_low, precision=highest))
            key_pick = matmul(table_blk, key_sum).reshape(block_rows, HEADS, HEAD_DIM)
            denom = lax.optimization_barrier(jnp.sum(queries.reshape(block_rows, HEADS, HEAD_DIM) * key_pick, axis=-1))
            attended = (numer / denom[:, :, None]).reshape(block_rows, D)
            centered = attended - lax.optimization_barrier(jnp.mean(attended, axis=-1, keepdims=True))
            normed = centered * lax.rsqrt(lax.optimization_barrier(jnp.mean(centered * centered, axis=-1, keepdims=True)) + norm_eps)
            mixed = normed * w_norm[0] + w_norm[1]
            product = low(mixed * gate_pre)
            return feat_blk + mask_blk[:, None] * matmul(product, w_out)
        outputs = lax.map(jax.checkpoint(output_block), (feat_blocks, mask_blocks, table_blocks))
        return outputs.reshape(token_count, D)
    block_out, pullback = jax.vjp(forward, feats, proj_low, out_low, norm_low)
    input_grad, grad_proj, grad_out, grad_gain = pullback(cot_full)
    square_sum = jnp.sum(grad_proj * grad_proj) + jnp.sum(grad_out * grad_out) + jnp.sum(grad_gain * grad_gain)
    grad_size = jnp.sqrt(square_sum)
    clip_level = 0.5 * math.sqrt(5 * D * D + 2 * D)
    clip_scale = jnp.minimum(1.0, clip_level / grad_size)
    unused_one, proj_mnew, proj_snew, proj_wnew = adam_update(proj_master, proj_moment, proj_square, grad_proj, clip_scale, decay_rate, learn_rate)
    unused_two, out_mnew, out_snew, out_wnew = adam_update(out_master, out_moment, out_square, grad_out, clip_scale, decay_rate, learn_rate)
    norm_clip, norm_mnew, norm_snew, norm_wnew = adam_update(norm_master, norm_moment, norm_square, grad_gain, clip_scale, 0.0, norm_rate)
    return (block_out, input_grad, grad_size.reshape(1), proj_mnew, proj_snew, proj_wnew, proj_wnew.astype(jnp.bfloat16), out_mnew, out_snew, out_wnew, out_wnew.astype(jnp.bfloat16), norm_clip, norm_mnew, norm_snew, norm_wnew)
```

```python
import functools
import math

import jax
import jax.numpy as jnp
from jax import lax
from jax.experimental import pallas as pl
from jax.experimental.pallas import tpu as pltpu
from jax.sharding import PartitionSpec as P

HEADS = 8
CLUSTERS = 4
STEP = 10
AXES = ("nodes", "shard")

norm_eps = 1e-05
beta_one = 0.9
beta_two = 0.999
learn_rate = 0.05
norm_rate = 0.5
decay_rate = 0.01
adam_eps = 1e-08
bf_type = jnp.bfloat16
fl_type = jnp.float32

GROUPS = 2
CHUNKS = GROUPS * CLUSTERS
PAD = 16


def dot_nn(a, b):
    return lax.dot_general(a, b, (((1,), (0,)), ((), ())), preferred_element_type=fl_type)


def dot_nt(a, b):
    return lax.dot_general(a, b, (((1,), (1,)), ((), ())), preferred_element_type=fl_type)


def dot_tn(a, b):
    return lax.dot_general(a, b, (((0,), (0,)), ((), ())), preferred_element_type=fl_type)


def whole(shape):
    return pl.BlockSpec(shape, lambda *_: (0,) * len(shape))


def smem():
    return pl.BlockSpec(memory_space=pltpu.SMEM)


def call(kernel, grid, ins, in_specs, outs, out_specs, scratch, flops, name):
    moved = sum(math.prod(a.shape) * a.dtype.itemsize for a in (*ins, *outs))
    return pl.pallas_call(
        kernel,
        grid=grid,
        in_specs=in_specs,
        out_specs=out_specs,
        out_shape=outs,
        scratch_shapes=scratch,
        cost_estimate=pl.CostEstimate(flops=int(flops), transcendentals=0, bytes_accessed=int(moved)),
        compiler_params=pltpu.CompilerParams(
            dimension_semantics=("arbitrary",) * len(grid), vmem_limit_bytes=60 * 1024 * 1024
        ),
        name=name,
    )(*ins)


def out(shape, dtype):
    return jax.ShapeDtypeStruct(shape, dtype)


def prep_kernel(place, wp, wo, wn, kv_mine, kv_other, qo_mine, qo_other, kv_all, qo_all):
    core = place[0]
    width = wo.shape[1]
    shard = wo.shape[0]

    def turned(block):
        return block.T.astype(bf_type)

    qo_all[0:width] = turned(wp[:, 0:width])
    kv_all[0:width] = turned(wp[:, width : 2 * width])
    kv_all[width : 2 * width] = turned(wp[:, 2 * width : 3 * width])
    qo_all[width : 2 * width] = turned(wp[:, 3 * width : 4 * width])
    qo_all[2 * width : 3 * width] = turned(wo[...])
    rows = jnp.concatenate([wn[...], jnp.zeros((30, shard), fl_type)], axis=0)
    qo_all[3 * width : 3 * width + 32] = rows.astype(bf_type)
    for whole_ref, mine, other in ((kv_all, kv_mine, kv_other), (qo_all, qo_mine, qo_other)):
        half = mine.shape[0]
        mine[...] = whole_ref[pl.ds(pl.multiple_of(core * half, 16), half)]
        other[...] = whole_ref[pl.ds(pl.multiple_of((1 - core) * half, 16), half)]


def members(ids_ref):
    rows = ids_ref.shape[1]
    classes = lax.broadcasted_iota(jnp.int32, (PAD, rows), 0)
    return (classes == ids_ref[...]).astype(fl_type).astype(bf_type)


def valid_row(count, start, rows):
    slots = lax.broadcasted_iota(jnp.int32, (1, rows), 1) + start
    return slots < count


def put_chunks(acc, keep, send, node, extra):
    width = acc.shape[2]
    head = width // 4
    for g in range(GROUPS):
        for c in range(CLUSTERS):
            chunk = g * CLUSTERS + c
            distance = lax.bitwise_xor(node, chunk)
            slot = lax.shift_right_logical(distance, 1)
            lane_head = lax.broadcasted_iota(jnp.int32, (head, width), 1) // head
            body = jnp.zeros((head, width), fl_type)
            for h in range(4):
                rows = acc[g, c * width + h * head : c * width + (h + 1) * head, :]
                body = jnp.where(lane_head == h, rows, body)
            block = jnp.concatenate([body, extra(g, c)], axis=0)

            @pl.when(lax.bitwise_and(distance, 1) == 0)
            def _():
                keep[slot] = block

            @pl.when(lax.bitwise_and(distance, 1) == 1)
            def _():
                send[slot] = block.astype(bf_type)


def key_kernel(pieces, place, x, ids, *refs):
    mine, other = refs[:pieces], refs[pieces : 2 * pieces]
    sig_key, value_out, keep, send, weights, masked, keys, acc = refs[2 * pieces :]
    step = pl.program_id(0)
    core, node, count = place[0], place[1], place[3]
    width = x.shape[1]
    rows = x.shape[0]
    half = width // GROUPS

    @pl.when(step == 0)
    def _():
        span = mine[0].shape[1]
        height = mine[0].shape[0]
        for d in range(pieces):
            weights[pl.ds(pl.multiple_of(core * height, 16), height), d * span : (d + 1) * span] = mine[d][...]
            weights[pl.ds(pl.multiple_of((1 - core) * height, 16), height), d * span : (d + 1) * span] = other[d][...]
        acc[...] = jnp.zeros_like(acc)

    table = members(ids)
    valid = valid_row(count, step * rows, rows)
    for g in range(GROUPS):
        sig = jax.nn.sigmoid(dot_nt(weights[g * half : (g + 1) * half, :], x[...]))
        sig_key[g * half : (g + 1) * half, :] = sig
        keys[...] = jnp.where(valid, sig, 0.0).astype(bf_type)
        value = dot_nt(weights[width + g * half : width + (g + 1) * half, :], x[...]).astype(bf_type)
        value_out[g * half : (g + 1) * half, :] = value
        for c in range(CLUSTERS):
            masked[c * half : (c + 1) * half, :] = value * table[c : c + 1, :]
        masked[CLUSTERS * half :, :] = table
        acc[g] += dot_nt(masked[...], keys[...])

    @pl.when(step == pl.num_programs(0) - 1)
    def _():
        def extra(g, c):
            row = acc[g, CLUSTERS * half + c : CLUSTERS * half + c + 1, :]
            return jnp.concatenate([row, jnp.zeros((PAD - 1, half), fl_type)], axis=0)

        put_chunks(acc, keep, send, node, extra)


def weights_kernel(pieces, place, *refs):
    q_mine, q_other = refs[:pieces], refs[pieces : 2 * pieces]
    k_mine, k_other = refs[2 * pieces : 3 * pieces], refs[3 * pieces : 4 * pieces]
    query_gate, out_weight, gain, shift, full, stage_q, stage_k = refs[4 * pieces :]
    core, shard = place[0], place[2]
    width = out_weight.shape[0]
    span = q_mine[0].shape[1]
    for mine, other, stage in ((q_mine, q_other, stage_q), (k_mine, k_other, stage_k)):
        half = mine[0].shape[0]
        for d in range(pieces):
            stage[d, pl.ds(pl.multiple_of(core * half, 16), half), :] = mine[d][...]
            stage[d, pl.ds(pl.multiple_of((1 - core) * half, 16), half), :] = other[d][...]
    norm_rows = []
    for z in range(pieces):
        where = lax.bitwise_xor(shard, z)
        cols = slice(z * span, (z + 1) * span)
        query_gate[:, cols] = stage_q[z, 0 : 2 * width, :]
        full[0:width, cols] = stage_q[where, 0:width, :]
        full[width : 3 * width, cols] = stage_k[where]
        full[3 * width :, cols] = stage_q[where, width : 2 * width, :]
        out_weight[cols, :] = stage_q[where, 2 * width : 3 * width, :].T
        norm_rows.append(stage_q[where, 3 * width : 3 * width + 16, :])
    turned = jnp.concatenate(norm_rows, axis=1).astype(fl_type).T
    gain[...] = jnp.broadcast_to(turned[:, 0:1], gain.shape)
    shift[...] = jnp.broadcast_to(turned[:, 1:2], shift.shape)


def query_kernel(place, x, g, query_gate, out_weight, sig_query, query, gate, grad_prod):
    step = pl.program_id(0)
    count = place[3]
    rows, width = x.shape
    half = width // GROUPS
    valid = valid_row(count, step * rows, rows)
    for p in range(GROUPS):
        span = slice(p * half, (p + 1) * half)
        sig = jax.nn.sigmoid(dot_nt(query_gate[span, :], x[...]))
        sig_query[span, :] = sig
        query[span, :] = sig.astype(bf_type)
        gate[span, :] = dot_nt(query_gate[width + p * half : width + (p + 1) * half, :], x[...])
        grad_prod[span, :] = jnp.where(valid, dot_nt(out_weight[span, :], g[...]), 0.0)


def place_chunks(chunk_refs, place, stage):
    node = place[1]
    for d in range(CHUNKS):
        stage[lax.bitwise_xor(node, d)] = chunk_refs[d][...]


def head_rows(width, h, value):
    lane_head = lax.broadcasted_iota(jnp.int32, (1, width), 1) // (width // 4)
    return jnp.where(lane_head == h, value, jnp.zeros_like(value))


def middle_kernel(place, ids, query, gate, grad_prod, gain, shift, *refs):
    chunk_refs = refs[:CHUNKS]
    prod_out, dgate_out, dnum_out, dden_out, keep, send = refs[CHUNKS : CHUNKS + 6]
    stage, left, stack, num, normed, dnormed, den, dden, acc, dgain, dshift = refs[CHUNKS + 6 :]
    step = pl.program_id(0)
    node, count = place[1], place[3]
    width, rows = query.shape
    half = width // GROUPS
    head = half // 4
    lanes = 256

    @pl.when(step == 0)
    def _():
        place_chunks(chunk_refs, place, stage)
        for g in range(GROUPS):
            for c in range(CLUSTERS):
                chunk = stage[g * CLUSTERS + c].astype(fl_type)
                cols = slice(c * half, (c + 1) * half)
                for h in range(4):
                    left[g, h * head : (h + 1) * head, cols] = head_rows(half, h, chunk[:head]).astype(bf_type)
                sums = [head_rows(half, h, chunk[head : head + 1]) for h in range(4)]
                sums.append(jnp.zeros((PAD - 4, half), fl_type))
                left[g, half : half + PAD, cols] = jnp.concatenate(sums, axis=0).astype(bf_type)
        acc[...] = jnp.zeros_like(acc)
        dgain[...] = jnp.zeros_like(dgain)
        dshift[...] = jnp.zeros_like(dshift)

    table = members(ids)
    for g in range(GROUPS):
        part = query[g * half : (g + 1) * half, :]
        for c in range(CLUSTERS):
            stack[c * half : (c + 1) * half, :] = part * table[c : c + 1, :]
        both = dot_nn(left[g], stack[0 : CLUSTERS * half, :])
        num[g * half : (g + 1) * half, :] = both[:half]
        den[g * 8 : g * 8 + 8, :] = 1.0 / both[half : half + 8]

    for lane in range(rows // lanes):
        cols = slice(lane * lanes, (lane + 1) * lanes)
        valid = valid_row(count, step * rows + lane * lanes, lanes)
        total = jnp.zeros((1, lanes), fl_type)
        for h in range(HEADS):
            span = slice(h * head, (h + 1) * head)
            row = (h // 4) * 8 + h % 4
            att = num[span, cols] * den[row : row + 1, cols]
            num[span, cols] = att
            total = total + jnp.sum(att, axis=0, keepdims=True)
        mean = total * (1.0 / width)
        total = jnp.zeros((1, lanes), fl_type)
        for h in range(HEADS):
            centered = num[h * head : (h + 1) * head, cols] - mean
            total = total + jnp.sum(centered * centered, axis=0, keepdims=True)
        scale = lax.rsqrt(total * (1.0 / width) + norm_eps)
        first = jnp.zeros((1, lanes), fl_type)
        second = jnp.zeros((1, lanes), fl_type)
        for h in range(HEADS):
            span = slice(h * head, (h + 1) * head)
            ah = (num[span, cols] - mean) * scale
            gamma = jnp.concatenate([gain[span, :]] * (lanes // 128), axis=1)
            beta = jnp.concatenate([shift[span, :]] * (lanes // 128), axis=1)
            u = ah * gamma + beta
            zg = gate[span, cols]
            dp = grad_prod[span, cols]
            prod_out[span, cols] = jnp.where(valid, u * zg, 0.0).astype(bf_type)
            du = dp * zg
            dgate_out[span, cols] = (dp * u).astype(bf_type)
            du_ah = du * ah
            for part in range(lanes // 128):
                sub = slice(part * 128, (part + 1) * 128)
                dgain[span, :] += du_ah[:, sub]
                dshift[span, :] += du[:, sub]
            dah = gamma * du
            first = first + jnp.sum(dah, axis=0, keepdims=True)
            second = second + jnp.sum(dah * ah, axis=0, keepdims=True)
            normed[span, cols] = ah
            dnormed[span, cols] = dah
        first = first * (1.0 / width)
        second = second * (1.0 / width)
        for h in range(HEADS):
            span = slice(h * head, (h + 1) * head)
            row = (h // 4) * 8 + h % 4
            da = scale * (dnormed[span, cols] - first - normed[span, cols] * second)
            inverse = den[row : row + 1, cols]
            dnum_out[span, cols] = (da * inverse).astype(bf_type)
            dden[row : row + 1, cols] = -jnp.sum(da * num[span, cols], axis=0, keepdims=True) * inverse

    dden_out[...] = dden[...]
    for g in range(GROUPS):
        part = dnum_out[g * half : (g + 1) * half, :]
        for c in range(CLUSTERS):
            stack[c * half : (c + 1) * half, :] = part * table[c : c + 1, :]
        den_rows = dden[g * 8 : g * 8 + 4, :]
        high = den_rows.astype(bf_type)
        low = (den_rows - high.astype(fl_type)).astype(bf_type)
        four_high = jnp.concatenate([high * table[c : c + 1, :] for c in range(CLUSTERS)], axis=0)
        four_low = jnp.concatenate([low * table[c : c + 1, :] for c in range(CLUSTERS)], axis=0)
        stack[CLUSTERS * half :, :] = jnp.concatenate([four_high, four_low], axis=0)
        acc[g] += dot_nt(stack[...], query[g * half : (g + 1) * half, :])

    @pl.when(step == pl.num_programs(0) - 1)
    def _():
        gain_row = jnp.sum(dgain[...].T, axis=0, keepdims=True)
        shift_row = jnp.sum(dshift[...].T, axis=0, keepdims=True)

        def extra(g, c):
            base = CLUSTERS * half
            row = jnp.zeros((1, half), fl_type)
            for h in range(4):
                at = base + c * 4 + h
                row = row + head_rows(half, h, acc[g, at : at + 1, :] + acc[g, at + 16 : at + 17, :])
            cols = slice(g * half, (g + 1) * half)
            tail = [row]
            if c == 0:
                tail += [gain_row[:, cols], shift_row[:, cols]]
            tail.append(jnp.zeros((PAD - len(tail), half), fl_type))
            return jnp.concatenate(tail, axis=0)

        put_chunks(acc, keep, send, node, extra)


def write_pieces(pieces, node, shard, span, keep, send, blocks):
    for chunk in range(8):
        distance = lax.bitwise_xor(node, chunk)
        slot = lax.shift_right_logical(distance, 1)
        even = lax.bitwise_and(distance, 1) == 0
        for z in range(pieces):
            block = blocks(z, chunk)

            @pl.when(even)
            def _():
                keep[slot, z] = block

            @pl.when(jnp.logical_not(even))
            def _():
                send[slot, z] = block.astype(bf_type)


def query_back_kernel(pieces, place, ids, dnum, dden, dgate, sig_query, prod, x, g, *refs):
    chunk_refs = refs[:CHUNKS]
    dquery_out, keep, send = refs[CHUNKS : CHUNKS + 3]
    stage, left, sums, stack, acc, acc_out = refs[CHUNKS + 3 :]
    step = pl.program_id(0)
    node, shard = place[1], place[2]
    width, rows = dnum.shape
    half = width // GROUPS
    head = half // 4
    span = width // pieces

    @pl.when(step == 0)
    def _():
        place_chunks(chunk_refs, place, stage)
        for gr in range(GROUPS):
            for c in range(CLUSTERS):
                chunk = stage[gr * CLUSTERS + c].astype(fl_type)
                block = jnp.concatenate([head_rows(half, h, chunk[:head]) for h in range(4)], axis=0)
                left[gr, :, c * half : (c + 1) * half] = block.T.astype(bf_type)
                column = jnp.broadcast_to(chunk[head : head + 8], (8, half)).T
                sums[c, gr * half : (gr + 1) * half, :] = jnp.broadcast_to(column[:, 0:1], (half, 128))
        acc[...] = jnp.zeros_like(acc)
        acc_out[...] = jnp.zeros_like(acc_out)

    table = members(ids)
    for gr in range(GROUPS):
        part = dnum[gr * half : (gr + 1) * half, :]
        for c in range(CLUSTERS):
            stack[c * half : (c + 1) * half, :] = part * table[c : c + 1, :]
        dq = dot_nn(left[gr], stack[...])
        for h in range(4):
            at = slice(gr * half + h * head, gr * half + (h + 1) * head)
            pick = pick_rows(sums, at, ids, rows)
            row = gr * 8 + h
            full = dq[h * head : (h + 1) * head] + dden[row : row + 1, :] * pick
            sig = sig_query[at, :]
            dquery_out[at, :] = (full * (sig * (1.0 - sig))).astype(bf_type)
    acc[0:width] += dot_nn(dquery_out[...], x[...])
    acc[width : 2 * width] += dot_nn(dgate[...], x[...])
    acc_out[...] += dot_nn(prod[...], g[...])

    @pl.when(step == pl.num_programs(0) - 1)
    def _():
        tall = 2 * width // 8

        def blocks(z, chunk):
            top = acc[chunk * tall : (chunk + 1) * tall, z * span : (z + 1) * span]
            start = lax.bitwise_xor(shard, z) * span
            rows_out = span // 2
            start = pl.multiple_of(start + (chunk % 2) * rows_out, 8)
            lanes = width // 4
            bottom = acc_out[pl.ds(start, rows_out), (chunk // 2) * lanes : (chunk // 2 + 1) * lanes]
            bottom = bottom.reshape(-1, span) if lanes == span else fold(bottom, span)
            return jnp.concatenate([top, bottom], axis=0)

        write_pieces(pieces, node, shard, span, keep, send, blocks)


def fold(block, span):
    return jnp.concatenate(
        [block[:, i * span : (i + 1) * span] for i in range(block.shape[1] // span)], axis=0
    )


def pick_rows(sums, at, ids, rows):
    reps = rows // 128
    wide = [jnp.concatenate([sums[c, at, :]] * reps, axis=1) for c in range(CLUSTERS)]
    pick = wide[CLUSTERS - 1]
    for c in range(CLUSTERS - 1):
        pick = jnp.where(ids[...] == c, wide[c], pick)
    return pick


def output_kernel(place, x, prod, out_weight, result):
    result[...] = x[...].astype(fl_type) + dot_tn(prod[...], out_weight[...])


def key_back_kernel(pieces, place, ids, sig_key, value, x, *refs):
    chunk_refs = refs[:CHUNKS]
    dkey_out, dvalue_out, norm_out, keep, send = refs[CHUNKS : CHUNKS + 5]
    stage, left_key, left_value, sums, stack, acc = refs[CHUNKS + 5 :]
    step = pl.program_id(0)
    node, shard, count = place[1], place[2], place[3]
    width, rows = value.shape
    half = width // GROUPS
    head = half // 4
    span = width // pieces

    @pl.when(step == 0)
    def _():
        place_chunks(chunk_refs, place, stage)
        for gr in range(GROUPS):
            for c in range(CLUSTERS):
                chunk = stage[gr * CLUSTERS + c].astype(fl_type)
                block = jnp.concatenate([head_rows(half, h, chunk[:head]) for h in range(4)], axis=0)
                left_value[gr, :, c * half : (c + 1) * half] = block.astype(bf_type)
                left_key[gr, :, c * half : (c + 1) * half] = block.T.astype(bf_type)
                column = chunk[head : head + 8].T
                sums[c, gr * half : (gr + 1) * half, :] = jnp.broadcast_to(column[:, 0:1], (half, 128))
                if c == 0:
                    norm_out[:, gr * half : (gr + 1) * half] = chunk[head : head + 8]
        acc[...] = jnp.zeros_like(acc)

    table = members(ids)
    valid = valid_row(count, step * rows, rows)
    for gr in range(GROUPS):
        at = slice(gr * half, (gr + 1) * half)
        part = value[at, :]
        for c in range(CLUSTERS):
            stack[c * half : (c + 1) * half, :] = part * table[c : c + 1, :]
        dk = dot_nn(left_key[gr], stack[...])
        for h in range(4):
            sub = slice(gr * half + h * head, gr * half + (h + 1) * head)
            full = dk[h * head : (h + 1) * head] + pick_rows(sums, sub, ids, rows)
            sig = sig_key[sub, :]
            dkey_out[sub, :] = jnp.where(valid, full * (sig * (1.0 - sig)), 0.0).astype(bf_type)
        key = jnp.where(valid, sig_key[at, :], 0.0).astype(bf_type)
        for c in range(CLUSTERS):
            stack[c * half : (c + 1) * half, :] = key * table[c : c + 1, :]
        dvalue_out[at, :] = dot_nn(left_value[gr], stack[...]).astype(bf_type)
    acc[0:width] += dot_nn(dkey_out[...], x[...])
    acc[width : 2 * width] += dot_nn(dvalue_out[...], x[...])

    @pl.when(step == pl.num_programs(0) - 1)
    def _():
        tall = 2 * width // 8

        def blocks(z, chunk):
            return acc[chunk * tall : (chunk + 1) * tall, z * span : (z + 1) * span]

        write_pieces(pieces, node, shard, span, keep, send, blocks)


def input_kernel(dquery, dkey, dvalue, dgate, full, g, result):
    width = g.shape[1]
    total = g[...].astype(fl_type)
    for i, part in enumerate((dquery, dkey, dvalue, dgate)):
        total = total + dot_tn(part[...], full[i * width : (i + 1) * width, :])
    result[...] = total


def gather_kernel(place, *refs):
    parts = refs[:CHUNKS]
    grad_proj, grad_out, squares = refs[CHUNKS : CHUNKS + 3]
    stage_kv, stage_qg = refs[CHUNKS + 3 :]
    node = place[1]
    span, width = grad_out.shape
    tall = 2 * width // 8
    total = jnp.zeros((8, span), fl_type)
    for d in range(CHUNKS):
        chunk = lax.bitwise_xor(node, d)
        part = parts[d][...].astype(fl_type)
        stage_kv[chunk] = part[:tall]
        stage_qg[chunk] = part[tall : 2 * tall]
        square = part * part
        for r in range(part.shape[0] // 8):
            total = total + square[r * 8 : (r + 1) * 8]
        bottom = part[2 * tall :]
        lanes = width // 4
        folds = lanes // span
        rows = span // 2
        row_start = pl.multiple_of(lax.bitwise_and(chunk, 1) * rows, 8)
        quarter = lax.shift_right_logical(chunk, 1)
        for q in range(4):

            @pl.when(quarter == q)
            def _():
                for i in range(folds):
                    at = slice(q * lanes + i * span, q * lanes + (i + 1) * span)
                    grad_out[pl.ds(row_start, rows), at] = bottom[i * rows : (i + 1) * rows]

    for chunk in range(8):
        half = chunk % 4
        key_or_value = width if chunk < 4 else 2 * width
        grad_proj[:, key_or_value + half * tall : key_or_value + (half + 1) * tall] = stage_kv[chunk].T
        query_or_gate = 0 if chunk < 4 else 3 * width
        grad_proj[:, query_or_gate + half * tall : query_or_gate + (half + 1) * tall] = stage_qg[chunk].T
    squares[...] = total


def adam(master_w, moment_old, square_old, clipped, decay_coef, step_rate):
    moment_new = beta_one * moment_old + (1.0 - beta_one) * clipped
    square_new = beta_two * square_old + (1.0 - beta_two) * clipped * clipped
    moment_hat = moment_new * (1.0 / (1.0 - beta_one**STEP))
    square_hat = square_new * (1.0 / (1.0 - beta_two**STEP))
    master_new = master_w * (1.0 - step_rate * decay_coef) - step_rate * moment_hat / (
        jnp.sqrt(square_hat) + adam_eps
    )
    return moment_new, square_new, master_new


def update_kernel(scale, gp, go, gn, pw, pm, ps, ow, om, osq, nw, nm, ns, *outs):
    p_m, p_s, p_w, p_c, o_m, o_s, o_w, o_c, n_g, n_m, n_s, n_w = outs
    factor = scale[0]
    p_m[...], p_s[...], new = adam(pw[...], pm[...], ps[...], gp[...] * factor, decay_rate, learn_rate)
    p_w[...] = new
    p_c[...] = new.astype(bf_type)
    o_m[...], o_s[...], new = adam(ow[...], om[...], osq[...], go[...] * factor, decay_rate, learn_rate)
    o_w[...] = new
    o_c[...] = new.astype(bf_type)
    clipped = gn[...] * factor
    n_g[...] = clipped
    n_m[...], n_s[...], n_w[...] = adam(nw[...], nm[...], ns[...], clipped, 0.0, norm_rate)


def make_exchange(nodes, shards):
    count = nodes * shards

    def exchange(value, node_bits, shard_bits):
        pairs = [
            (i, ((i // shards) ^ node_bits) * shards + ((i % shards) ^ shard_bits)) for i in range(count)
        ]
        return lax.ppermute(value, AXES, pairs)

    return exchange


def tree_sum(parts):
    parts = list(parts)
    while len(parts) > 1:
        parts = [parts[i] + parts[i + 1] for i in range(0, len(parts), 2)]
    return parts[0]


def to_float(parts):
    return [p.astype(fl_type) for p in parts]


def local(nodes, shards, *args):
    (x, g, ids, counts, pw, pm, ps, ow, om, osq, nw, nm, ns) = args
    exchange = make_exchange(nodes, shards)
    outer = nodes // 8
    rows, width = x.shape
    half = width // GROUPS
    head = width // HEADS
    span = pw.shape[0]
    block = min(512, rows)
    steps = rows // block
    tall = 2 * width // 8

    node = lax.axis_index("nodes").astype(jnp.int32)
    shard = lax.axis_index("shard").astype(jnp.int32)
    chunk_node = lax.bitwise_and(node, 7)
    place = jnp.stack([lax.bitwise_and(node, 1), chunk_node, shard, counts[0]])
    ids = ids.reshape(1, rows)

    half_kv, half_qo = width, (3 * width + 32) // 2
    kv_mine, kv_other, qo_mine, qo_other = call(
        prep_kernel,
        (),
        (place, pw, ow, nw),
        [smem(), whole(pw.shape), whole(ow.shape), whole(nw.shape)],
        [out((half_kv, span), bf_type)] * 2 + [out((half_qo, span), bf_type)] * 2,
        [whole((half_kv, span))] * 2 + [whole((half_qo, span))] * 2,
        [pltpu.VMEM((2 * half_kv, span), bf_type), pltpu.VMEM((2 * half_qo, span), bf_type)],
        1e6,
        "prep",
    )
    kv_mine, kv_other, qo_mine, qo_other = [kv_mine], [kv_other], [qo_mine], [qo_other]
    for z in range(1, shards):
        kv_mine.append(exchange(kv_mine[0], 0, z))
    for z in range(1, shards):
        qo_mine.append(exchange(qo_mine[0], 0, z))
    for z in range(1, shards):
        kv_other.append(exchange(kv_mine[z], 1, 0))
    for z in range(1, shards):
        qo_other.append(exchange(qo_mine[z], 1, 0))
    x_turned = jnp.concatenate(
        [
            lax.dynamic_slice(x, (0, lax.bitwise_xor(shard, z) * span), (rows, span))
            for z in range(shards)
        ],
        axis=1,
    )

    by_row = pl.BlockSpec((block, width), lambda i: (i, 0))
    by_lane = pl.BlockSpec((width, block), lambda i: (0, i))
    id_lane = pl.BlockSpec((1, block), lambda i: (0, i))
    chunk_shape = (4, head + PAD, half)
    piece_shape = (4, shards, tall, span)
    chunk_specs = [whole((head + PAD, half))] * CHUNKS

    sig_key, value, keep, send = call(
        functools.partial(key_kernel, shards),
        (steps,),
        (place, x_turned, ids, *kv_mine, *kv_other),
        [smem(), by_row, id_lane] + [whole((half_kv, span))] * (2 * shards),
        [
            out((width, rows), fl_type),
            out((width, rows), bf_type),
            out(chunk_shape, fl_type),
            out(chunk_shape, bf_type),
        ],
        [by_lane, by_lane, whole(chunk_shape), whole(chunk_shape)],
        [
            pltpu.VMEM((2 * width, width), bf_type),
            pltpu.VMEM((CLUSTERS * half + PAD, block), bf_type),
            pltpu.VMEM((half, block), bf_type),
            pltpu.VMEM((GROUPS, CLUSTERS * half + PAD, half), fl_type),
        ],
        8 * rows * width * width,
        "keys",
    )

    def reduce_chunks(keep, send):
        mine = keep + exchange(send, 1, 0).astype(fl_type)
        got = [exchange(mine[e].astype(bf_type), 2 * e, 0) for e in range(1, 4)]
        mine = tree_sum([mine[0], *to_float(got)])
        own = mine.astype(bf_type)
        got = [own] + [exchange(own, 0, z) for z in range(1, shards)]
        own = tree_sum(to_float(got)).astype(bf_type)
        if outer > 1:
            got = [own] + [exchange(own, 8 * o, 0) for o in range(1, outer)]
            own = tree_sum(to_float(got)).astype(bf_type)
        return spread(own)

    def spread(own):
        chunks = [None] * 8
        chunks[0] = own
        for e in range(1, 4):
            chunks[2 * e] = exchange(own, 2 * e, 0)
        for e in range(4):
            chunks[2 * e + 1] = exchange(chunks[2 * e], 1, 0)
        return chunks

    chunks = reduce_chunks(keep, send)

    query_gate, out_weight, gain, shift, full = call(
        functools.partial(weights_kernel, shards),
        (),
        (place, *qo_mine, *qo_other, *kv_mine, *kv_other),
        [smem()] + [whole((half_qo, span))] * (2 * shards) + [whole((half_kv, span))] * (2 * shards),
        [
            out((2 * width, width), bf_type),
            out((width, width), bf_type),
            out((width, 128), fl_type),
            out((width, 128), fl_type),
            out((4 * width, width), bf_type),
        ],
        [
            whole((2 * width, width)),
            whole((width, width)),
            whole((width, 128)),
            whole((width, 128)),
            whole((4 * width, width)),
        ],
        [
            pltpu.VMEM((shards, 2 * half_qo, span), bf_type),
            pltpu.VMEM((shards, 2 * half_kv, span), bf_type),
        ],
        1e6,
        "weights",
    )

    sig_query, query, gate, grad_prod = call(
        query_kernel,
        (steps,),
        (place, x_turned, g, query_gate, out_weight),
        [smem(), by_row, by_row, whole((2 * width, width)), whole((width, width))],
        [
            out((width, rows), fl_type),
            out((width, rows), bf_type),
            out((width, rows), fl_type),
            out((width, rows), fl_type),
        ],
        [by_lane] * 4,
        [],
        6 * rows * width * width,
        "queries",
    )

    lane16 = pl.BlockSpec((16, block), lambda i: (0, i))
    prod, dgate, dnum, dden, keep, send = call(
        middle_kernel,
        (steps,),
        (place, ids, query, gate, grad_prod, gain, shift, *chunks),
        [smem(), id_lane, by_lane, by_lane, by_lane, whole((width, 128)), whole((width, 128))] + chunk_specs,
        [
            out((width, rows), bf_type),
            out((width, rows), bf_type),
            out((width, rows), bf_type),
            out((16, rows), fl_type),
            out(chunk_shape, fl_type),
            out(chunk_shape, bf_type),
        ],
        [by_lane, by_lane, by_lane, lane16, whole(chunk_shape), whole(chunk_shape)],
        [
            pltpu.VMEM((CHUNKS, head + PAD, half), bf_type),
            pltpu.VMEM((GROUPS, half + PAD, CLUSTERS * half), bf_type),
            pltpu.VMEM((CLUSTERS * half + 32, block), bf_type),
            pltpu.VMEM((width, block), fl_type),
            pltpu.VMEM((width, block), fl_type),
            pltpu.VMEM((width, block), fl_type),
            pltpu.VMEM((16, block), fl_type),
            pltpu.VMEM((16, block), fl_type),
            pltpu.VMEM((GROUPS, CLUSTERS * half + 32, half), fl_type),
            pltpu.VMEM((width, 128), fl_type),
            pltpu.VMEM((width, 128), fl_type),
        ],
        12 * rows * width * width,
        "middle",
    )

    back_chunks = reduce_chunks(keep, send)

    early = tall + tall // 2
    early_shape = (4, shards, early * 1, span)
    if width // 4 != span:
        early_shape = (4, shards, tall + (span // 2) * (width // 4 // span), span)
    early = early_shape[2]
    dquery, early_keep, early_send = call(
        functools.partial(query_back_kernel, shards),
        (steps,),
        (place, ids, dnum, dden, dgate, sig_query, prod, x_turned, g, *chunks),
        [smem(), id_lane, by_lane, lane16, by_lane, by_lane, by_lane, by_row, by_row] + chunk_specs,
        [out((width, rows), bf_type), out(early_shape, fl_type), out(early_shape, bf_type)],
        [by_lane, whole(early_shape), whole(early_shape)],
        [
            pltpu.VMEM((CHUNKS, head + PAD, half), bf_type),
            pltpu.VMEM((GROUPS, half, CLUSTERS * half), bf_type),
            pltpu.VMEM((CLUSTERS, width, 128), fl_type),
            pltpu.VMEM((CLUSTERS * half, block), bf_type),
            pltpu.VMEM((2 * width, width), fl_type),
            pltpu.VMEM((width, width), fl_type),
        ],
        10 * rows * width * width,
        "query_back",
    )
    block_out = call(
        output_kernel,
        (steps,),
        (place, x, prod, out_weight),
        [smem(), by_row, by_lane, whole((width, width))],
        [out((rows, width), fl_type)],
        [by_row],
        [],
        2 * rows * width * width,
        "output",
    )[0]

    dkey, dvalue, norm_grad, late_keep, late_send = call(
        functools.partial(key_back_kernel, shards),
        (steps,),
        (place, ids, sig_key, value, x_turned, *back_chunks),
        [smem(), id_lane, by_lane, by_lane, by_row] + chunk_specs,
        [
            out((width, rows), bf_type),
            out((width, rows), bf_type),
            out((8, width), fl_type),
            out(piece_shape, fl_type),
            out(piece_shape, bf_type),
        ],
        [by_lane, by_lane, whole((8, width)), whole(piece_shape), whole(piece_shape)],
        [
            pltpu.VMEM((CHUNKS, head + PAD, half), bf_type),
            pltpu.VMEM((GROUPS, half, CLUSTERS * half), bf_type),
            pltpu.VMEM((GROUPS, half, CLUSTERS * half), bf_type),
            pltpu.VMEM((CLUSTERS, width, 128), fl_type),
            pltpu.VMEM((CLUSTERS * half, block), bf_type),
            pltpu.VMEM((2 * width, width), fl_type),
        ],
        12 * rows * width * width,
        "key_back",
    )

    def reduce_pieces(keep, send):
        mine = keep + exchange(send, 1, 0).astype(fl_type)
        got = [exchange(mine[e].astype(bf_type), 2 * e, 0) for e in range(1, 4)]
        mine = tree_sum([mine[0], *to_float(got)])
        got = [exchange(mine[z].astype(bf_type), 0, z) for z in range(1, shards)]
        mine = tree_sum([mine[0], *to_float(got)])
        if outer > 1:
            own = mine.astype(bf_type)
            got = [own] + [exchange(own, 8 * o, 0) for o in range(1, outer)]
            mine = tree_sum(to_float(got))
        return mine.astype(bf_type)

    early_sum = reduce_pieces(early_keep, early_send)
    late_sum = reduce_pieces(late_keep, late_send)

    input_grad = call(
        input_kernel,
        (steps,),
        (dquery, dkey, dvalue, dgate, full, g),
        [by_lane] * 4 + [whole((4 * width, width)), by_row],
        [out((rows, width), fl_type)],
        [by_row],
        [],
        8 * rows * width * width,
        "inputs",
    )[0]

    parts = spread(jnp.concatenate([late_sum, early_sum], axis=0))
    grad_proj, grad_out, squares = call(
        gather_kernel,
        (),
        (place, *parts),
        [smem()] + [whole((tall + early, span))] * 8,
        [out((span, 4 * width), fl_type), out((span, width), fl_type), out((8, span), fl_type)],
        [whole((span, 4 * width)), whole((span, width)), whole((8, span))],
        [pltpu.VMEM((8, tall, span), fl_type), pltpu.VMEM((8, tall, span), fl_type)],
        1e6,
        "gather",
    )
    gain_grad = norm_grad[1:3]
    squares = jnp.broadcast_to(jnp.sum(squares), (8, 128))
    square_sum = tree_sum([squares] + [exchange(squares, 0, z) for z in range(1, shards)])[0, 0]
    grad_size = jnp.sqrt(square_sum + jnp.sum(gain_grad * gain_grad))
    clip_level = 0.5 * math.sqrt(5 * width * width + 2 * width)
    factor = jnp.minimum(1.0, clip_level / grad_size).reshape(1)
    mine_norm = lax.dynamic_slice_in_dim(gain_grad, shard * span, span, 1)
    states = (grad_proj, grad_out, mine_norm, pw, pm, ps, ow, om, osq, nw, nm, ns)
    like = [pw, pw, pw, pw, ow, ow, ow, ow, nw, nw, nw, nw]
    kinds = [fl_type] * 3 + [bf_type] + [fl_type] * 3 + [bf_type] + [fl_type] * 4
    new = call(
        update_kernel,
        (),
        (factor, *states),
        [smem()] + [whole(s.shape) for s in states],
        [out(s.shape, k) for s, k in zip(like, kinds)],
        [whole(s.shape) for s in like],
        [],
        1e6,
        "update",
    )
    return (block_out, input_grad, grad_size.reshape(1), *new)


def solution(mesh):
    nodes, shards = mesh.shape["nodes"], mesh.shape["shard"]
    by_node = P(AXES, None)
    rows = P("shard", None)
    cols = P(None, "shard")
    return jax.shard_map(
        functools.partial(local, nodes, shards),
        mesh=mesh,
        in_specs=(by_node, by_node, P(AXES), P(AXES)) + (rows,) * 6 + (cols,) * 3,
        out_specs=(by_node, by_node, P()) + (rows,) * 8 + (cols,) * 4,
        check_vma=False,
    )
```

```python
import functools
import math

import jax
import jax.numpy as jnp
from jax import lax
from jax.experimental import pallas as pl
from jax.experimental.pallas import tpu as pltpu
from jax.sharding import PartitionSpec as P

HEADS = 8
CLUSTERS = 4
STEP = 10
AXES = ("nodes", "shard")

norm_eps = 1e-05
beta_one = 0.9
beta_two = 0.999
learn_rate = 0.05
norm_rate = 0.5
decay_rate = 0.01
adam_eps = 1e-08
bf_type = jnp.bfloat16
fl_type = jnp.float32

GROUPS = 2
CHUNKS = GROUPS * CLUSTERS
PAD = 16


def dot_nn(a, b):
    return lax.dot_general(a, b, (((1,), (0,)), ((), ())), preferred_element_type=fl_type)


def dot_nt(a, b):
    return lax.dot_general(a, b, (((1,), (1,)), ((), ())), preferred_element_type=fl_type)


def dot_tn(a, b):
    return lax.dot_general(a, b, (((0,), (0,)), ((), ())), preferred_element_type=fl_type)


def whole(shape):
    return pl.BlockSpec(shape, lambda *_: (0,) * len(shape))


def smem():
    return pl.BlockSpec(memory_space=pltpu.SMEM)


def view(ref, kind, start, size):
    if kind == "lane":
        return ref.at[:, pl.ds(start, size)]
    if kind == "row":
        return ref.at[pl.ds(start, size), :]
    return ref


def call(kernel, steps, ins, in_kinds, outs, out_kinds, scratch, flops, name, block=0, vmem=16, piped=False):
    moved = sum(math.prod(a.shape) * a.dtype.itemsize for a in (*ins, *outs))
    arrays, kinds = [*ins, *outs], [*in_kinds, *out_kinds]

    def spec(array, kind):
        if kind == "smem":
            return smem()
        if isinstance(kind, pl.BlockSpec):
            return kind
        if piped and kind == "lane":
            return pl.BlockSpec((array.shape[0], block), lambda i: (0, i))
        if piped and kind == "row":
            return pl.BlockSpec((block, array.shape[1]), lambda i: (i, 0))
        return whole(array.shape)

    def body(*refs):
        if piped:
            kernel(pl.program_id(0), *refs)
            return
        if steps == 1:
            kernel(0, *refs)
            return

        def one(i, carry):
            start = pl.multiple_of(i * block, block)
            views = [view(r, k, start, block) for r, k in zip(refs, kinds)]
            kernel(i, *views, *refs[len(kinds) :])
            return carry

        lax.fori_loop(0, steps, one, 0)

    specs = [spec(a, k) for a, k in zip(arrays, kinds)]
    return pl.pallas_call(
        body,
        grid=(steps,) if piped else (),
        in_specs=specs[: len(ins)],
        out_specs=specs[len(ins) :],
        out_shape=outs,
        scratch_shapes=scratch,
        cost_estimate=pl.CostEstimate(flops=int(flops), transcendentals=0, bytes_accessed=int(moved)),
        compiler_params=pltpu.CompilerParams(vmem_limit_bytes=vmem * 1024 * 1024),
        name=name,
    )(*ins)


def out(shape, dtype):
    return jax.ShapeDtypeStruct(shape, dtype)


def prep_kernel(step, wp, wo, wn, message, other, query_all, stage):
    core = lax.bitwise_and(lax.axis_index("nodes"), 1)
    part = lax.bitwise_and(lax.axis_index("nodes"), 7)
    shard, width = wo.shape
    stage[0:width] = wp[:, width : 2 * width].T.astype(bf_type)
    stage[width : 2 * width] = wp[:, 2 * width : 3 * width].T.astype(bf_type)
    query_all[0:width] = wp[:, 0:width].T.astype(bf_type)
    query_all[width : 2 * width] = wp[:, 3 * width : 4 * width].T.astype(bf_type)
    query_all[2 * width : 3 * width] = wo[...].T.astype(bf_type)
    rest = query_all.shape[0] - 3 * width
    rows = jnp.concatenate([wn[...], jnp.zeros((rest - 2, shard), fl_type)], axis=0)
    query_all[3 * width :] = rows.astype(bf_type)
    message[0:width] = stage[pl.ds(pl.multiple_of(core * width, 16), width)]
    other[...] = stage[pl.ds(pl.multiple_of((1 - core) * width, 16), width)]
    height = query_all.shape[0] // 8
    message[width:] = query_all[pl.ds(pl.multiple_of(part * height, 16), height)]


def members(ids_ref):
    rows = ids_ref.shape[1]
    classes = lax.broadcasted_iota(jnp.int32, (PAD, rows), 0)
    return (classes == ids_ref[...]).astype(fl_type).astype(bf_type)


def valid_row(count, start, rows):
    slots = lax.broadcasted_iota(jnp.int32, (1, rows), 1) + start
    return slots < count


def put_chunks(acc, keep, send, node, extra):
    width = acc.shape[2]
    head = width // 4
    for g in range(GROUPS):
        for c in range(CLUSTERS):
            chunk = g * CLUSTERS + c
            distance = lax.bitwise_xor(node, chunk)
            slot = lax.shift_right_logical(distance, 1)
            lane_head = lax.broadcasted_iota(jnp.int32, (head, width), 1) // head
            body = jnp.zeros((head, width), fl_type)
            for h in range(4):
                rows = acc[g, c * width + h * head : c * width + (h + 1) * head, :]
                body = jnp.where(lane_head == h, rows, body)
            block = jnp.concatenate([body, extra(g, c)], axis=0)

            @pl.when(lax.bitwise_and(distance, 1) == 0)
            def _():
                keep[slot] = block

            @pl.when(lax.bitwise_and(distance, 1) == 1)
            def _():
                send[slot] = block.astype(bf_type)


def key_kernel(pieces, steps, step, place, x, ids, *refs):
    mine, other = refs[:pieces], refs[pieces : 2 * pieces]
    sig_key, value_out, keep, send, weights, masked, keys, acc = refs[2 * pieces :]
    core, node, count = place[0], place[1], place[3]
    width = x.shape[1]
    rows = x.shape[0]
    half = width // GROUPS

    @pl.when(step == 0)
    def _():
        span = mine[0].shape[1]
        for d in range(pieces):
            cols = slice(d * span, (d + 1) * span)
            weights[pl.ds(pl.multiple_of(core * width, 16), width), cols] = mine[d][0:width]
            weights[pl.ds(pl.multiple_of((1 - core) * width, 16), width), cols] = other[d][0:width]
        acc[...] = jnp.zeros_like(acc)

    table = members(ids)
    valid = valid_row(count, step * rows, rows)
    for g in range(GROUPS):
        sig = jax.nn.sigmoid(dot_nt(weights[g * half : (g + 1) * half, :], x[...]))
        sig_key[g * half : (g + 1) * half, :] = sig
        keys[...] = jnp.where(valid, sig, 0.0).astype(bf_type)
        value = dot_nt(weights[width + g * half : width + (g + 1) * half, :], x[...]).astype(bf_type)
        value_out[g * half : (g + 1) * half, :] = value
        for c in range(CLUSTERS):
            masked[c * half : (c + 1) * half, :] = value * table[c : c + 1, :]
        masked[CLUSTERS * half :, :] = table
        acc[g] += dot_nt(masked[...], keys[...])

    @pl.when(step == steps - 1)
    def _():
        def extra(g, c):
            row = acc[g, CLUSTERS * half + c : CLUSTERS * half + c + 1, :]
            return jnp.concatenate([row, jnp.zeros((PAD - 1, half), fl_type)], axis=0)

        put_chunks(acc, keep, send, node, extra)


def weights_kernel(pieces, step, place, own, *refs):
    near, far = refs[: 2 * (pieces - 1)], refs[2 * (pieces - 1) : 2 * (pieces - 1) + 6]
    query_weight, gate_weight, out_weight, gain, shift, full_query, full_gate, stage = refs[2 * (pieces - 1) + 6 :]
    node, shard = place[1], place[2]
    width = out_weight.shape[0]
    span = own.shape[1]
    height = own.shape[0] // 8

    def put(d, position, block):
        where = pl.multiple_of(lax.bitwise_xor(node, position) * height, 16)
        stage[d, pl.ds(where, height), :] = block

    stage[0] = own[...]
    for d in range(1, pieces):
        for core in range(2):
            put(d, core, near[core * (pieces - 1) + d - 1][width:])
            for e in range(3):
                put(d, 2 * (e + 1) + core, far[core * 3 + e][d - 1])
    norm_rows = []
    for z in range(pieces):
        where = lax.bitwise_xor(shard, z)
        cols = slice(z * span, (z + 1) * span)
        query_weight[:, cols] = stage[z, 0:width, :]
        gate_weight[:, cols] = stage[z, width : 2 * width, :]
        full_query[:, cols] = stage[where, 0:width, :]
        full_gate[:, cols] = stage[where, width : 2 * width, :]
        out_weight[cols, :] = stage[where, 2 * width : 3 * width, :].T
        norm_rows.append(stage[where, 3 * width : 3 * width + 16, :])
    turned = jnp.concatenate(norm_rows, axis=1).astype(fl_type).T
    gain[...] = jnp.broadcast_to(turned[:, 0:1], gain.shape)
    shift[...] = jnp.broadcast_to(turned[:, 1:2], shift.shape)


def key_weights_kernel(pieces, step, place, *refs):
    mine, other = refs[:pieces], refs[pieces : 2 * pieces]
    full, stage = refs[2 * pieces :]
    core = place[0]
    width, span = full.shape[1], mine[0].shape[1]
    for d in range(pieces):
        stage[d, pl.ds(pl.multiple_of(core * width, 16), width), :] = mine[d][0:width]
        stage[d, pl.ds(pl.multiple_of((1 - core) * width, 16), width), :] = other[d][0:width]
    for z in range(pieces):
        full[:, z * span : (z + 1) * span] = stage[lax.bitwise_xor(place[2], z)]


def query_kernel(step, place, x, weight, sig_query, query):
    sig = jax.nn.sigmoid(dot_nt(weight[...], x[...]))
    sig_query[...] = sig
    query[...] = sig.astype(bf_type)


def gate_kernel(step, place, x, weight, gate):
    gate[...] = dot_nt(weight[...], x[...])


def grad_prod_kernel(step, place, g, out_weight, grad_prod):
    rows = g.shape[0]
    valid = valid_row(place[3], step * rows, rows)
    grad_prod[...] = jnp.where(valid, dot_nt(out_weight[...], g[...]), 0.0)


def place_chunks(chunk_refs, place, stage):
    node = place[1]
    for d in range(CHUNKS):
        stage[lax.bitwise_xor(node, d)] = chunk_refs[d][...]


def head_rows(width, h, value):
    lane_head = lax.broadcasted_iota(jnp.int32, (1, width), 1) // (width // 4)
    return jnp.where(lane_head == h, value, jnp.zeros_like(value))


def middle_kernel(steps, lanes, step, place, ids, query, gate, grad_prod, gain, shift, *refs):
    chunk_refs = refs[:CHUNKS]
    prod_out, dgate_out, dnum_out, dden_out, keep, send = refs[CHUNKS : CHUNKS + 6]
    rest = refs[CHUNKS + 6 :]
    width, rows = query.shape
    parts = rows // lanes
    stage, left, acc, dgain, dshift = rest[:5]
    stacks, back_stacks, nums, normeds, dnormeds, dens, ddens = (
        rest[5 + i * parts : 5 + (i + 1) * parts] for i in range(7)
    )
    node, count = place[1], place[3]
    half = width // GROUPS
    head = half // 4

    @pl.when(step == 0)
    def _():
        place_chunks(chunk_refs, place, stage)
        for g in range(GROUPS):
            for c in range(CLUSTERS):
                chunk = stage[g * CLUSTERS + c].astype(fl_type)
                cols = slice(c * half, (c + 1) * half)
                for h in range(4):
                    left[g, h * head : (h + 1) * head, cols] = head_rows(half, h, chunk[:head]).astype(bf_type)
                sums = [head_rows(half, h, chunk[head : head + 1]) for h in range(4)]
                sums.append(jnp.zeros((PAD - 4, half), fl_type))
                left[g, half : half + PAD, cols] = jnp.concatenate(sums, axis=0).astype(bf_type)
        acc[...] = jnp.zeros_like(acc)
        dgain[...] = jnp.zeros_like(dgain)
        dshift[...] = jnp.zeros_like(dshift)

    def forward(part):
        cols = slice(part * lanes, (part + 1) * lanes)
        table = members(ids.at[:, cols])
        stack, num, den = stacks[part], nums[part], dens[part]
        for g in range(GROUPS):
            mine = query[g * half : (g + 1) * half, cols]
            for c in range(CLUSTERS):
                stack[g, c * half : (c + 1) * half, :] = mine * table[c : c + 1, :]
            both = dot_nn(left[g], stack[g])
            num[g * half : (g + 1) * half, :] = both[:half]
            den[g * 8 : g * 8 + 8, :] = 1.0 / both[half : half + 8]

    def norm(part):
        cols = slice(part * lanes, (part + 1) * lanes)
        num, normed, dnormed, den, dden = nums[part], normeds[part], dnormeds[part], dens[part], ddens[part]
        valid = valid_row(count, step * rows + part * lanes, lanes)
        total = jnp.zeros((8, lanes), fl_type)
        for h in range(HEADS):
            span = slice(h * head, (h + 1) * head)
            row = (h // 4) * 8 + h % 4
            att = num[span, :] * den[row : row + 1, :]
            num[span, :] = att
            total = total + fold_rows(att)
        mean = jnp.sum(total, axis=0, keepdims=True) * (1.0 / width)
        total = jnp.zeros((8, lanes), fl_type)
        for h in range(HEADS):
            centered = num[h * head : (h + 1) * head, :] - mean
            total = total + fold_rows(centered * centered)
        scale = lax.rsqrt(jnp.sum(total, axis=0, keepdims=True) * (1.0 / width) + norm_eps)
        first = jnp.zeros((8, lanes), fl_type)
        second = jnp.zeros((8, lanes), fl_type)
        for h in range(HEADS):
            span = slice(h * head, (h + 1) * head)
            ah = (num[span, :] - mean) * scale
            gamma = jnp.concatenate([gain[span, :]] * (lanes // 128), axis=1)
            beta = jnp.concatenate([shift[span, :]] * (lanes // 128), axis=1)
            u = ah * gamma + beta
            zg = gate[span, cols]
            dp = grad_prod[span, cols]
            prod_out[span, cols] = jnp.where(valid, u * zg, 0.0).astype(bf_type)
            du = dp * zg
            dgate_out[span, cols] = (dp * u).astype(bf_type)
            du_ah = du * ah
            dgain[span, :] += fold_lanes(du_ah)
            dshift[span, :] += fold_lanes(du)
            dah = gamma * du
            first = first + fold_rows(dah)
            second = second + fold_rows(dah * ah)
            normed[span, :] = ah
            dnormed[span, :] = dah
        first = jnp.sum(first, axis=0, keepdims=True) * (1.0 / width)
        second = jnp.sum(second, axis=0, keepdims=True) * (1.0 / width)
        for h in range(HEADS):
            span = slice(h * head, (h + 1) * head)
            row = (h // 4) * 8 + h % 4
            da = scale * (dnormed[span, :] - first - normed[span, :] * second)
            inverse = den[row : row + 1, :]
            dnum_out[span, cols] = (da * inverse).astype(bf_type)
            dden[row : row + 1, :] = -jnp.sum(da * num[span, :], axis=0, keepdims=True) * inverse
        dden_out[:, cols] = dden[...]

    def backward(part):
        cols = slice(part * lanes, (part + 1) * lanes)
        table = members(ids.at[:, cols])
        stack, dden = back_stacks[part], ddens[part]
        for g in range(GROUPS):
            mine = dnum_out[g * half : (g + 1) * half, cols]
            for c in range(CLUSTERS):
                stack[g, c * half : (c + 1) * half, :] = mine * table[c : c + 1, :]
            den_rows = dden[g * 8 : g * 8 + 4, :]
            high = den_rows.astype(bf_type)
            low = (den_rows - high.astype(fl_type)).astype(bf_type)
            four_high = jnp.concatenate([high * table[c : c + 1, :] for c in range(CLUSTERS)], axis=0)
            four_low = jnp.concatenate([low * table[c : c + 1, :] for c in range(CLUSTERS)], axis=0)
            stack[g, CLUSTERS * half :, :] = jnp.concatenate([four_high, four_low], axis=0)
            acc[g] += dot_nt(stack[g], query[g * half : (g + 1) * half, cols])

    for part in range(parts):
        forward(part)
    for part in range(parts):
        norm(part)
        backward(part)

    @pl.when(step == steps - 1)
    def _():
        gain_row = jnp.sum(dgain[...].T, axis=0, keepdims=True)
        shift_row = jnp.sum(dshift[...].T, axis=0, keepdims=True)

        def extra(g, c):
            base = CLUSTERS * half
            row = jnp.zeros((1, half), fl_type)
            for h in range(4):
                at = base + c * 4 + h
                row = row + head_rows(half, h, acc[g, at : at + 1, :] + acc[g, at + 16 : at + 17, :])
            cols = slice(g * half, (g + 1) * half)
            tail = [row]
            if c == 0:
                tail += [gain_row[:, cols], shift_row[:, cols]]
            tail.append(jnp.zeros((PAD - len(tail), half), fl_type))
            return jnp.concatenate(tail, axis=0)

        put_chunks(acc, keep, send, node, extra)


def fold_rows(block):
    return tree_sum([block[i * 8 : (i + 1) * 8] for i in range(block.shape[0] // 8)])


def fold_lanes(block):
    return tree_sum([block[:, i * 128 : (i + 1) * 128] for i in range(block.shape[1] // 128)])


def write_pieces(pieces, node, shard, span, keep, send, blocks):
    for chunk in range(8):
        distance = lax.bitwise_xor(node, chunk)
        slot = lax.shift_right_logical(distance, 1)
        even = lax.bitwise_and(distance, 1) == 0
        for z in range(pieces):
            block = blocks(z, chunk)

            @pl.when(even)
            def _():
                keep[slot, z] = block

            @pl.when(jnp.logical_not(even))
            def _():
                send[slot, z] = block.astype(bf_type)


def query_back_kernel(pieces, step, place, ids, dnum, dden, sig_query, x, *refs):
    chunk_refs = refs[:CHUNKS]
    dquery_out, grad_out = refs[CHUNKS : CHUNKS + 2]
    stage, left, sums, stack = refs[CHUNKS + 2 :]
    width, rows = dnum.shape
    half = width // GROUPS
    head = half // 4

    @pl.when(step == 0)
    def _():
        place_chunks(chunk_refs, place, stage)
        for gr in range(GROUPS):
            for c in range(CLUSTERS):
                chunk = stage[gr * CLUSTERS + c].astype(fl_type)
                block = jnp.concatenate([head_rows(half, h, chunk[:head]) for h in range(4)], axis=0)
                left[gr, :, c * half : (c + 1) * half] = block.T.astype(bf_type)
                column = chunk[head : head + 8].T
                sums[c, gr * half : (gr + 1) * half, :] = jnp.broadcast_to(column[:, 0:1], (half, 128))
        grad_out[...] = jnp.zeros_like(grad_out)

    table = members(ids)
    for gr in range(GROUPS):
        part = dnum[gr * half : (gr + 1) * half, :]
        for c in range(CLUSTERS):
            stack[c * half : (c + 1) * half, :] = part * table[c : c + 1, :]
        dq = dot_nn(left[gr], stack[...])
        for h in range(4):
            at = slice(gr * half + h * head, gr * half + (h + 1) * head)
            pick = pick_rows(sums, at, ids, rows)
            row = gr * 8 + h
            full = dq[h * head : (h + 1) * head] + dden[row : row + 1, :] * pick
            sig = sig_query[at, :]
            dquery_out[at, :] = (full * (sig * (1.0 - sig))).astype(bf_type)
    grad_out[...] += dot_nn(dquery_out[...], x[...])


def gate_back_kernel(step, place, dgate, prod, x, g, grad_gate, grad_out):
    @pl.when(step == 0)
    def _():
        grad_gate[...] = jnp.zeros_like(grad_gate)
        grad_out[...] = jnp.zeros_like(grad_out)

    grad_gate[...] += dot_nn(dgate[...], x[...])
    grad_out[...] += dot_nn(prod[...], g[...])


def fold(block, span):
    return jnp.concatenate(
        [block[:, i * span : (i + 1) * span] for i in range(block.shape[1] // span)], axis=0
    )


def pick_rows(sums, at, ids, rows):
    reps = rows // 128
    wide = [jnp.concatenate([sums[c, at, :]] * reps, axis=1) for c in range(CLUSTERS)]
    pick = wide[CLUSTERS - 1]
    for c in range(CLUSTERS - 1):
        pick = jnp.where(ids[...] == c, wide[c], pick)
    return pick


def output_kernel(step, place, x, prod, out_weight, result):
    result[...] = x[...].astype(fl_type) + dot_tn(prod[...], out_weight[...])


def key_back_kernel(pieces, steps, step, place, ids, sig_key, value, x, grad_query, grad_gate, grad_out, *refs):
    chunk_refs = refs[:CHUNKS]
    dkey_out, dvalue_out, norm_out, keep, send = refs[CHUNKS : CHUNKS + 5]
    stage, left_key, left_value, sums, stack, acc = refs[CHUNKS + 5 :]
    node, shard, count = place[1], place[2], place[3]
    width, rows = value.shape
    half = width // GROUPS
    head = half // 4
    span = width // pieces

    @pl.when(step == 0)
    def _():
        place_chunks(chunk_refs, place, stage)
        for gr in range(GROUPS):
            for c in range(CLUSTERS):
                chunk = stage[gr * CLUSTERS + c].astype(fl_type)
                block = jnp.concatenate([head_rows(half, h, chunk[:head]) for h in range(4)], axis=0)
                left_value[gr, :, c * half : (c + 1) * half] = block.astype(bf_type)
                left_key[gr, :, c * half : (c + 1) * half] = block.T.astype(bf_type)
                column = chunk[head : head + 8].T
                sums[c, gr * half : (gr + 1) * half, :] = jnp.broadcast_to(column[:, 0:1], (half, 128))
                if c == 0:
                    norm_out[:, gr * half : (gr + 1) * half] = chunk[head : head + 8]
        acc[...] = jnp.zeros_like(acc)

    table = members(ids)
    valid = valid_row(count, step * rows, rows)
    for gr in range(GROUPS):
        at = slice(gr * half, (gr + 1) * half)
        part = value[at, :]
        for c in range(CLUSTERS):
            stack[c * half : (c + 1) * half, :] = part * table[c : c + 1, :]
        dk = dot_nn(left_key[gr], stack[...])
        for h in range(4):
            sub = slice(gr * half + h * head, gr * half + (h + 1) * head)
            full = dk[h * head : (h + 1) * head] + pick_rows(sums, sub, ids, rows)
            sig = sig_key[sub, :]
            dkey_out[sub, :] = jnp.where(valid, full * (sig * (1.0 - sig)), 0.0).astype(bf_type)
        key = jnp.where(valid, sig_key[at, :], 0.0).astype(bf_type)
        for c in range(CLUSTERS):
            stack[c * half : (c + 1) * half, :] = key * table[c : c + 1, :]
        dvalue_out[at, :] = dot_nn(left_value[gr], stack[...]).astype(bf_type)
    acc[0:width] += dot_nn(dkey_out[...], x[...])
    acc[width : 2 * width] += dot_nn(dvalue_out[...], x[...])

    @pl.when(step == steps - 1)
    def _():
        tall = 2 * width // 8
        lanes = width // 4
        short = span // 2

        def blocks(z, chunk):
            cols = slice(z * span, (z + 1) * span)
            top = acc[chunk * tall : (chunk + 1) * tall, cols]
            source = grad_query if chunk < 4 else grad_gate
            center = source[(chunk % 4) * tall : (chunk % 4 + 1) * tall, cols]
            start = pl.multiple_of(lax.bitwise_xor(shard, z) * span + (chunk % 2) * short, 8)
            bottom = grad_out[pl.ds(start, short), (chunk // 2) * lanes : (chunk // 2 + 1) * lanes]
            return jnp.concatenate([top, center, fold(bottom, span)], axis=0)

        write_pieces(pieces, node, shard, span, keep, send, blocks)


def input_kernel(step, place, dquery, dkey, dvalue, dgate, full_query, full_key, full_gate, g, result):
    width = g.shape[1]
    total = g[...].astype(fl_type)
    total = total + dot_tn(dquery[...], full_query[...])
    total = total + dot_tn(dkey[...], full_key[0:width, :])
    total = total + dot_tn(dvalue[...], full_key[width:, :])
    total = total + dot_tn(dgate[...], full_gate[...])
    result[...] = total


def finish_kernel(step, *refs):
    parts, (sums, squares) = refs[:-2], refs[-2:]
    value = tree_sum([p[...].astype(fl_type) for p in parts]).astype(bf_type)
    sums[...] = value
    value = value.astype(fl_type)
    total = jnp.sum(value * value, axis=0, keepdims=True)
    squares[...] = jnp.broadcast_to(jnp.sum(total, axis=1, keepdims=True), squares.shape)


def with_squares_kernel(count, step, *refs):
    sums, squares, result = refs[0], refs[1 : 1 + count], refs[1 + count]
    span = sums.shape[1]
    result[0 : sums.shape[0]] = sums[...]
    value = tree_sum([q[...] for q in squares])[:, :span]
    high = value.astype(bf_type).astype(fl_type)
    rest = value - high
    middle = rest.astype(bf_type).astype(fl_type)
    low = rest - middle
    row = lax.broadcasted_iota(jnp.int32, value.shape, 0)
    terms = jnp.where(row == 0, high, jnp.where(row == 1, middle, jnp.where(row == 2, low, 0.0)))
    result[sums.shape[0] :] = jnp.concatenate([terms, jnp.zeros_like(terms)], axis=0).astype(bf_type)


def adam(master_w, moment_old, square_old, clipped, decay_coef, step_rate):
    moment_new = beta_one * moment_old + (1.0 - beta_one) * clipped
    square_new = beta_two * square_old + (1.0 - beta_two) * clipped * clipped
    moment_hat = moment_new * (1.0 / (1.0 - beta_one**STEP))
    square_hat = square_new * (1.0 / (1.0 - beta_two**STEP))
    master_new = master_w * (1.0 - step_rate * decay_coef) - step_rate * moment_hat / (
        jnp.sqrt(square_hat) + adam_eps
    )
    return moment_new, square_new, master_new


def update_kernel(pieces, step, place, *refs):
    parts, gn, pw, pm, ps, ow, om, osq, nw, nm, ns = refs[:CHUNKS], *refs[CHUNKS : CHUNKS + 10]
    size, p_m, p_s, p_w, p_c, o_m, o_s, o_w, o_c, n_g, n_m, n_s, n_w = refs[CHUNKS + 10 : CHUNKS + 23]
    stage, grad_out, factor = refs[CHUNKS + 23 :]
    node, shard = place[1], place[2]
    span, width = ow.shape
    tall = 2 * width // 8

    @pl.when(step == 0)
    def _():
        terms = []
        lanes = width // 4
        rows = span // 2
        for d in range(CHUNKS):
            chunk = lax.bitwise_xor(node, d)
            part = parts[d]
            stage[4 + chunk] = part[0:tall]
            stage[jnp.where(chunk < 4, chunk, chunk + 8)] = part[tall : 2 * tall]
            bottom = part[2 * tall : 2 * tall + rows * (lanes // span)].astype(fl_type)
            tail = part[2 * tall + rows * (lanes // span) :].astype(fl_type)
            terms.append((tail[2:3] + tail[1:2]) + tail[0:1])
            row_start = pl.multiple_of(lax.bitwise_and(chunk, 1) * rows, 8)
            quarter = lax.shift_right_logical(chunk, 1)
            for q in range(4):

                @pl.when(quarter == q)
                def _():
                    for i in range(lanes // span):
                        at = slice(q * lanes + i * span, q * lanes + (i + 1) * span)
                        grad_out[pl.ds(row_start, rows), at] = bottom[i * rows : (i + 1) * rows]

        norm_grad = gn[1:3, :]
        norm_square = jnp.sum(norm_grad * norm_grad, axis=0, keepdims=True)
        total = tree_sum(terms)[:, 0:1] + jnp.sum(norm_square, axis=1, keepdims=True)
        norm = jnp.sqrt(total)
        size[...] = norm
        clip_level = 0.5 * math.sqrt(5 * width * width + 2 * width)
        scale = jnp.minimum(1.0, clip_level / norm)
        factor[...] = jnp.broadcast_to(scale, factor.shape)
        o_m[...], o_s[...], new = adam(ow[...], om[...], osq[...], grad_out[...] * scale, decay_rate, learn_rate)
        o_w[...] = new
        o_c[...] = new.astype(bf_type)
        mine = norm_grad[:, 0:span]
        for z in range(1, pieces):
            mine = jnp.where(shard == z, norm_grad[:, z * span : (z + 1) * span], mine)
        clipped = mine * scale
        n_g[...] = clipped
        n_m[...], n_s[...], n_w[...] = adam(nw[...], nm[...], ns[...], clipped, 0.0, norm_rate)

    scale = factor[0:1, 0:1]
    for i in range(4):
        cols = slice(i * tall, (i + 1) * tall)
        grad = stage[step * 4 + i].astype(fl_type).T * scale
        p_m[:, cols], p_s[:, cols], new = adam(pw[:, cols], pm[:, cols], ps[:, cols], grad, decay_rate, learn_rate)
        p_w[:, cols] = new
        p_c[:, cols] = new.astype(bf_type)


def make_exchange(nodes, shards):
    count = nodes * shards

    def exchange(value, node_bits, shard_bits):
        pairs = [
            (i, ((i // shards) ^ node_bits) * shards + ((i % shards) ^ shard_bits)) for i in range(count)
        ]
        return lax.ppermute(value, AXES, pairs)

    return exchange


def tree_sum(parts):
    parts = list(parts)
    while len(parts) > 1:
        parts = [parts[i] + parts[i + 1] for i in range(0, len(parts), 2)]
    return parts[0]


def to_float(parts):
    return [p.astype(fl_type) for p in parts]


def tie(value, *others):
    return lax.optimization_barrier((value, *others))[0]


def tie(value, *others):
    return lax.optimization_barrier((value, *others))[0]


def local(nodes, shards, *args):
    (x, g, ids, counts, pw, pm, ps, ow, om, osq, nw, nm, ns) = args
    exchange = make_exchange(nodes, shards)
    outer = nodes // 8
    rows, width = x.shape
    half = width // GROUPS
    head = width // HEADS
    span = pw.shape[0]
    block = min(512, rows)
    steps = rows // block
    lanes = 256
    tall = 2 * width // 8
    part_rows = (3 * width + 2 + 127) // 128 * 16
    work = 2 * rows * width * width

    node = lax.axis_index("nodes").astype(jnp.int32)
    shard = lax.axis_index("shard").astype(jnp.int32)
    place = jnp.stack([lax.bitwise_and(node, 1), lax.bitwise_and(node, 7), shard, counts[0]])
    ids = ids.reshape(1, rows)
    chunk_shape = (4, head + PAD, half)

    def wide(dtype):
        return out((width, rows), dtype)

    def vmem(shape, dtype):
        return pltpu.VMEM(shape, dtype)

    message, kv_half, query_all = call(
        prep_kernel,
        1,
        (pw, ow, nw),
        [None] * 3,
        [
            out((width + part_rows, span), bf_type),
            out((width, span), bf_type),
            out((8 * part_rows, span), bf_type),
        ],
        [None] * 3,
        [vmem((2 * width, span), bf_type)],
        1e6,
        "prep",
    )
    mine, other = [message], [kv_half]
    for z in range(1, shards):
        mine.append(exchange(message, 0, z))
    for z in range(1, shards):
        other.append(exchange(mine[z], 1, 0))
    x_turned = jnp.concatenate(
        [
            lax.dynamic_slice(x, (0, lax.bitwise_xor(shard, z) * span), (rows, span))
            for z in range(shards)
        ],
        axis=1,
    )

    sig_key, value, keep, send = call(
        functools.partial(key_kernel, shards, steps),
        steps,
        (place, x_turned, ids, *mine, *other),
        ["smem", "row", "lane"] + [None] * (2 * shards),
        [wide(fl_type), wide(bf_type), out(chunk_shape, fl_type), out(chunk_shape, bf_type)],
        ["lane", "lane", None, None],
        [
            vmem((2 * width, width), bf_type),
            vmem((CLUSTERS * half + PAD, block), bf_type),
            vmem((half, block), bf_type),
            vmem((GROUPS, CLUSTERS * half + PAD, half), fl_type),
        ],
        4 * work,
        "keys",
        block,
    )

    def swap(pieces, peers, filler):
        got = [exchange(p, *at) for p, at in zip(pieces, peers)]
        if filler is not None:
            done = filler(pieces[0])
            got = list(tie(tuple(got), done))
        return to_float(got)

    plane = [(2 * e, 0) for e in range(1, 4)]
    along = [(0, z) for z in range(1, shards)]
    made = {}

    def reduce_chunks(keep, send, fillers):
        mine = keep + exchange(send, 1, 0).astype(fl_type)
        got = swap([mine[e].astype(bf_type) for e in range(1, 4)], plane, fillers[0])
        own = tree_sum([mine[0], *got]).astype(bf_type)
        got = swap([own] * (shards - 1), along, fillers[1])
        own = tree_sum([own.astype(fl_type), *got]).astype(bf_type)
        if outer > 1:
            got = swap([own] * (outer - 1), [(8 * o, 0) for o in range(1, outer)], None)
            own = tree_sum([own.astype(fl_type), *got]).astype(bf_type)
        return spread(own, fillers[2])

    def spread(own, filler=None):
        chunks = [own] + [None] * 7
        for e in range(1, 4):
            chunks[2 * e] = exchange(own, 2 * e, 0)
        chunks[1] = exchange(own, 1, 0)
        if filler is not None:
            done = filler(own)
            chunks[2], chunks[4], chunks[6] = tie((chunks[2], chunks[4], chunks[6]), done)
        for e in range(1, 4):
            chunks[2 * e + 1] = exchange(chunks[2 * e], 1, 0)
        return chunks

    def fill_weights(dep):
        made["weights"] = call(
            functools.partial(weights_kernel, shards),
            1,
            (tie(place, dep), query_all, *mine[1:], *other[1:], *far),
            ["smem", None] + [None] * (2 * (shards - 1) + 6),
            [
                out((width, width), bf_type),
                out((width, width), bf_type),
                out((width, width), bf_type),
                out((width, 128), fl_type),
                out((width, 128), fl_type),
                out((width, width), bf_type),
                out((width, width), bf_type),
            ],
            [None] * 7,
            [vmem((shards, 8 * part_rows, span), bf_type)],
            1e6,
            "weights",
        )
        return made["weights"][0]

    def fill_query(dep):
        made["query"] = call(
            query_kernel,
            steps,
            (tie(place, dep), x_turned, made["weights"][0]),
            ["smem", "row", None],
            [wide(fl_type), wide(bf_type)],
            ["lane"] * 2,
            [],
            work,
            "query",
            block,
            vmem=12,
        )
        return made["query"][1], fill_gate(dep)

    def fill_gate(dep):
        gate_weight = made["weights"][1]
        made["gate"] = call(
            gate_kernel,
            steps,
            (tie(place, dep), x_turned, gate_weight),
            ["smem", "row", None],
            [wide(fl_type)],
            ["lane"],
            [],
            work,
            "gate",
            block,
            vmem=12,
        )[0]
        return made["gate"]

    def fill_grad_prod(dep):
        out_weight = made["weights"][2]
        made["grad_prod"] = call(
            grad_prod_kernel,
            steps,
            (tie(place, dep), g, out_weight),
            ["smem", "row", None],
            [wide(fl_type)],
            ["lane"],
            [],
            work,
            "grad_prod",
            block,
            vmem=12,
        )[0]
        return made["grad_prod"]

    stack = jnp.stack([mine[z][width:] for z in range(1, shards)])
    far = [exchange(stack, *at) for at in plane]
    send = tie(send, *far)
    far = far + [exchange(f, 1, 0) for f in far]
    chunks = reduce_chunks(keep, send, (fill_weights, fill_query, fill_grad_prod))
    out_weight, gain, shift, full_query, full_gate = made["weights"][2:]
    sig_query, query = made["query"]

    parts = block // lanes
    prod, dgate, dnum, dden, keep, send = call(
        functools.partial(middle_kernel, steps, lanes),
        steps,
        (place, ids, query, made["gate"], made["grad_prod"], gain, shift, *chunks),
        ["smem", "lane", "lane", "lane", "lane", None, None] + [None] * CHUNKS,
        [
            wide(bf_type),
            wide(bf_type),
            wide(bf_type),
            out((16, rows), fl_type),
            out(chunk_shape, fl_type),
            out(chunk_shape, bf_type),
        ],
        ["lane", "lane", "lane", "lane", None, None],
        [
            vmem((CHUNKS, head + PAD, half), bf_type),
            vmem((GROUPS, half + PAD, CLUSTERS * half), bf_type),
            vmem((GROUPS, CLUSTERS * half + 32, half), fl_type),
            vmem((width, 128), fl_type),
            vmem((width, 128), fl_type),
        ]
        + [vmem((GROUPS, CLUSTERS * half, lanes), bf_type)] * parts
        + [vmem((GROUPS, CLUSTERS * half + 32, lanes), bf_type)] * parts
        + [vmem((width, lanes), fl_type)] * (3 * parts)
        + [vmem((16, lanes), fl_type)] * (2 * parts),
        6 * work,
        "middle",
        block,
    )

    def fill_gate_back(dep):
        made["gate_back"] = call(
            gate_back_kernel,
            steps,
            (tie(place, dep), dgate, prod, x_turned, g),
            ["smem", "lane", "lane", "row", "row"],
            [out((width, width), fl_type)] * 2,
            [None] * 2,
            [],
            2 * work,
            "gate_back",
            block,
            vmem=12,
        )
        return made["gate_back"][0]

    def fill_output(dep):
        made["output"] = call(
            output_kernel,
            steps,
            (tie(place, dep), x, prod, out_weight),
            ["smem", "row", "lane", None],
            [out((rows, width), fl_type)],
            ["row"],
            [],
            work,
            "output",
            block,
            piped=True,
        )[0]
        return made["output"]

    def fill_query_back(dep):
        made["query_back"] = call(
            functools.partial(query_back_kernel, shards),
            steps,
            (tie(place, dep), ids, dnum, dden, sig_query, x_turned, *chunks),
            ["smem", "lane", "lane", "lane", "lane", "row"] + [None] * CHUNKS,
            [wide(bf_type), out((width, width), fl_type)],
            ["lane", None],
            [
                vmem((CHUNKS, head + PAD, half), bf_type),
                vmem((GROUPS, half, CLUSTERS * half), bf_type),
                vmem((CLUSTERS, width, 128), fl_type),
                vmem((CLUSTERS * half, block), bf_type),
            ],
            3 * work,
            "query_back",
            block,
        )
        return made["query_back"][0]

    back_chunks = reduce_chunks(keep, send, (fill_gate_back, None, fill_query_back))
    dquery, grad_query = made["query_back"]

    height = 2 * tall + (span // 2) * (width // 4 // span)
    piece_shape = (4, shards, height, span)
    dkey, dvalue, norm_grad, keep, send = call(
        functools.partial(key_back_kernel, shards, steps),
        steps,
        (place, ids, sig_key, value, x_turned, grad_query, *made["gate_back"], *back_chunks),
        ["smem", "lane", "lane", "lane", "row"] + [None] * (3 + CHUNKS),
        [
            wide(bf_type),
            wide(bf_type),
            out((8, width), fl_type),
            out(piece_shape, fl_type),
            out(piece_shape, bf_type),
        ],
        ["lane", "lane", None, None, None],
        [
            vmem((CHUNKS, head + PAD, half), bf_type),
            vmem((GROUPS, half, CLUSTERS * half), bf_type),
            vmem((GROUPS, half, CLUSTERS * half), bf_type),
            vmem((CLUSTERS, width, 128), fl_type),
            vmem((CLUSTERS * half, block), bf_type),
            vmem((2 * width, width), fl_type),
        ],
        6 * work,
        "key_back",
        block,
    )

    full_key = call(
        functools.partial(key_weights_kernel, shards),
        1,
        (place, *mine, *other),
        ["smem"] + [None] * (2 * shards),
        [out((2 * width, width), bf_type)],
        [None],
        [vmem((shards, 2 * width, span), bf_type)],
        1e6,
        "key_weights",
        vmem=12,
    )[0]

    def fill_inputs(dep):
        made["inputs"] = call(
            input_kernel,
            steps,
            (tie(place, dep), dquery, dkey, dvalue, dgate, full_query, full_key, full_gate, g),
            ["smem"] + ["lane"] * 4 + [None] * 3 + ["row"],
            [out((rows, width), fl_type)],
            ["row"],
            [],
            4 * work,
            "inputs",
            block,
            piped=True,
        )[0]
        fill_output(dep)
        return made["inputs"], made["output"]

    mine_sum = keep + exchange(send, 1, 0).astype(fl_type)
    got = swap([mine_sum[e].astype(bf_type) for e in range(1, 4)], plane, fill_inputs)
    mine_sum = tree_sum([mine_sum[0], *got])
    got = [exchange(mine_sum[z].astype(bf_type), *along[z - 1]) for z in range(1, shards)]
    owned_parts = [mine_sum[0], *got]
    if outer > 1:
        own = tree_sum(to_float(owned_parts)).astype(bf_type)
        got = [own] + [exchange(own, 8 * o, 0) for o in range(1, outer)]
        owned_parts = [tree_sum(to_float(got))] + [jnp.zeros_like(own)] * (shards - 1)

    sums, squares = call(
        finish_kernel,
        1,
        owned_parts,
        [None] * shards,
        [out((height, span), bf_type), out((8, 128), fl_type)],
        [None] * 2,
        [],
        1e6,
        "finish",
        vmem=4,
    )
    squares = [squares] + [exchange(squares, 0, z) for z in range(1, shards)]
    owned = call(
        functools.partial(with_squares_kernel, shards),
        1,
        (sums, *squares),
        [None] * (1 + shards),
        [out((height + 16, span), bf_type)],
        [None],
        [],
        1e6,
        "with_squares",
        vmem=4,
    )[0]
    parts = spread(owned)
    states = (pw, pm, ps, ow, om, osq, nw, nm, ns)
    column = pl.BlockSpec((span, width), lambda i: (0, i))
    like = [pw] * 4 + [ow] * 4 + [nw] * 4
    kinds = [fl_type] * 3 + [bf_type] + [fl_type] * 3 + [bf_type] + [fl_type] * 4
    grad_size, *new = call(
        functools.partial(update_kernel, shards),
        4,
        (place, *parts, norm_grad, *states),
        ["smem"] + [None] * (CHUNKS + 1) + [column] * 3 + [None] * 6,
        [out((1, 1), fl_type)] + [out(s.shape, k) for s, k in zip(like, kinds)],
        [None] + [column] * 4 + [None] * 8,
        [
            vmem((16, tall, span), bf_type),
            vmem((span, width), fl_type),
            vmem((8, 128), fl_type),
        ],
        1e6,
        "update",
        piped=True,
    )
    return (made["output"], made["inputs"], grad_size.reshape(1), *new)


def solution(mesh):
    nodes, shards = mesh.shape["nodes"], mesh.shape["shard"]
    by_node = P(AXES, None)
    rows = P("shard", None)
    cols = P(None, "shard")
    return jax.shard_map(
        functools.partial(local, nodes, shards),
        mesh=mesh,
        in_specs=(by_node, by_node, P(AXES), P(AXES)) + (rows,) * 6 + (cols,) * 3,
        out_specs=(by_node, by_node, P()) + (rows,) * 8 + (cols,) * 4,
        check_vma=False,
    )
```

```python
import functools
import math

import jax
import jax.numpy as jnp
from jax import lax
from jax.experimental import pallas as pl
from jax.experimental.pallas import tpu as pltpu
from jax.sharding import PartitionSpec as P

HEADS = 8
CLUSTERS = 4
STEP = 10
AXES = ("nodes", "shard")

norm_eps = 1e-05
beta_one = 0.9
beta_two = 0.999
learn_rate = 0.05
norm_rate = 0.5
decay_rate = 0.01
adam_eps = 1e-08
bf_type = jnp.bfloat16
fl_type = jnp.float32

GROUPS = 2
PAIRS = HEADS // 2
CHUNKS = GROUPS * CLUSTERS
PAD = 16


def dot_nn(a, b):
    return lax.dot_general(a, b, (((1,), (0,)), ((), ())), preferred_element_type=fl_type)


def dot_nt(a, b):
    return lax.dot_general(a, b, (((1,), (1,)), ((), ())), preferred_element_type=fl_type)


def dot_tn(a, b):
    return lax.dot_general(a, b, (((0,), (0,)), ((), ())), preferred_element_type=fl_type)


def whole(shape):
    return pl.BlockSpec(shape, lambda *_: (0,) * len(shape))


def smem():
    return pl.BlockSpec(memory_space=pltpu.SMEM)


def view(ref, kind, start, size):
    if kind == "lane":
        return ref.at[:, pl.ds(start, size)]
    if kind == "row":
        return ref.at[pl.ds(start, size), :]
    return ref


def call(kernel, steps, ins, in_kinds, outs, out_kinds, scratch, flops, name, block=0, vmem=16, piped=False):
    moved = sum(math.prod(a.shape) * a.dtype.itemsize for a in (*ins, *outs))
    arrays, kinds = [*ins, *outs], [*in_kinds, *out_kinds]

    def spec(array, kind):
        if kind == "smem":
            return smem()
        if kind == "hbm":
            return pl.BlockSpec(memory_space=pltpu.HBM)
        if isinstance(kind, pl.BlockSpec):
            return kind
        if piped and kind == "lane":
            return pl.BlockSpec((array.shape[0], block), lambda i: (0, i))
        if piped and kind == "row":
            return pl.BlockSpec((block, array.shape[1]), lambda i: (i, 0))
        return whole(array.shape)

    def body(*refs):
        if piped:
            kernel(pl.program_id(0), *refs)
            return
        if steps == 1:
            kernel(0, *refs)
            return

        def one(i, carry):
            start = pl.multiple_of(i * block, block)
            views = [view(r, k, start, block) for r, k in zip(refs, kinds)]
            kernel(i, *views, *refs[len(kinds) :])
            return carry

        lax.fori_loop(0, steps, one, 0)

    specs = [spec(a, k) for a, k in zip(arrays, kinds)]
    return pl.pallas_call(
        body,
        grid=(steps,) if piped else (),
        in_specs=specs[: len(ins)],
        out_specs=specs[len(ins) :],
        out_shape=outs,
        scratch_shapes=scratch,
        cost_estimate=pl.CostEstimate(flops=int(flops), transcendentals=0, bytes_accessed=int(moved)),
        compiler_params=pltpu.CompilerParams(vmem_limit_bytes=vmem * 1024 * 1024),
        name=name,
    )(*ins)


def out(shape, dtype):
    return jax.ShapeDtypeStruct(shape, dtype)


def fetch(copies):
    copies = [pltpu.make_async_copy(*c) for c in copies]
    for c in copies:
        c.start()
    return copies


def prep_kernel(step, wp, wo, wn, key_message, key_other, message, query_all, block, rows, stage, sems):
    core = lax.bitwise_and(lax.axis_index("nodes"), 1)
    part = lax.bitwise_and(lax.axis_index("nodes"), 7)
    shard, width = wo.shape
    columns = [wp.at[:, i * width : (i + 1) * width] for i in (1, 2, 0, 3)]
    sources = [*columns, wo]
    copies = fetch(
        [(sources[i], block.at[i], sems.at[i]) for i in range(5)] + [(wn, rows, sems.at[5])]
    )
    for i in range(2):
        copies[i].wait()
        stage[i] = block[i].T.astype(bf_type)
    key_message[...] = stage[core]
    key_other[...] = stage[1 - core]
    for i in range(3):
        copies[2 + i].wait()
        query_all[i * width : (i + 1) * width] = block[2 + i].T.astype(bf_type)
    copies[5].wait()
    rest = query_all.shape[0] - 3 * width
    tail = jnp.concatenate([rows[...], jnp.zeros((rest - 2, shard), fl_type)], axis=0)
    query_all[3 * width :] = tail.astype(bf_type)
    height = query_all.shape[0] // 8
    message[...] = query_all[pl.ds(pl.multiple_of(part * height, 16), height)]


def members(ids_ref):
    rows = ids_ref.shape[1]
    classes = lax.broadcasted_iota(jnp.int32, (PAD, rows), 0)
    return (classes == ids_ref[...]).astype(fl_type).astype(bf_type)


def valid_row(count, start, rows):
    slots = lax.broadcasted_iota(jnp.int32, (1, rows), 1) + start
    return slots < count


def put_chunks(acc, keep, send, node, extra):
    width = acc.shape[2]
    head = width // 4
    for g in range(GROUPS):
        for c in range(CLUSTERS):
            chunk = g * CLUSTERS + c
            distance = lax.bitwise_xor(node, chunk)
            slot = lax.shift_right_logical(distance, 1)
            lane_head = lax.broadcasted_iota(jnp.int32, (head, width), 1) // head
            body = jnp.zeros((head, width), fl_type)
            for h in range(4):
                rows = acc[g, c * width + h * head : c * width + (h + 1) * head, :]
                body = jnp.where(lane_head == h, rows, body)
            block = jnp.concatenate([body, extra(g, c)], axis=0)

            @pl.when(lax.bitwise_and(distance, 1) == 0)
            def _():
                keep[slot] = block

            @pl.when(lax.bitwise_and(distance, 1) == 1)
            def _():
                send[slot] = block.astype(bf_type)


def key_kernel(pieces, steps, step, place, x, ids, *refs):
    mine, other = refs[:pieces], refs[pieces : 2 * pieces]
    key_slope, key_out, value_out, keep, send, weights, masked, acc = refs[2 * pieces :]
    core, node, count = place[0], place[1], place[3]
    width = x.shape[1]
    rows = x.shape[0]
    half = width // GROUPS

    @pl.when(step == 0)
    def _():
        span = mine[0].shape[1]
        for d in range(pieces):
            cols = slice(d * span, (d + 1) * span)
            weights[pl.ds(pl.multiple_of(core * width, 16), width), cols] = mine[d][0:width]
            weights[pl.ds(pl.multiple_of((1 - core) * width, 16), width), cols] = other[d][0:width]
        acc[...] = jnp.zeros_like(acc)

    table = members(ids)
    valid = valid_row(count, step * rows, rows)
    for g in range(GROUPS):
        sig = jax.nn.sigmoid(dot_nt(weights[g * half : (g + 1) * half, :], x[...]))
        kept = jnp.where(valid, sig, 0.0)
        key_slope[g * half : (g + 1) * half, :] = kept * (1.0 - sig)
        keys = kept.astype(bf_type)
        key_out[g * half : (g + 1) * half, :] = keys
        value = dot_nt(weights[width + g * half : width + (g + 1) * half, :], x[...]).astype(bf_type)
        value_out[g * half : (g + 1) * half, :] = value
        for c in range(CLUSTERS):
            masked[c * half : (c + 1) * half, :] = value * table[c : c + 1, :]
        masked[CLUSTERS * half :, :] = table
        acc[g] += dot_nt(masked[...], keys)

    @pl.when(step == steps - 1)
    def _():
        def extra(g, c):
            row = acc[g, CLUSTERS * half + c : CLUSTERS * half + c + 1, :]
            return jnp.concatenate([row, jnp.zeros((PAD - 1, half), fl_type)], axis=0)

        put_chunks(acc, keep, send, node, extra)


def weights_kernel(pieces, step, place, own, *refs):
    stacks = refs[:8]
    query_weight, gate_weight, out_weight, gain, shift, full_query, full_gate, stage = refs[8:]
    node, shard = place[1], place[2]
    width = out_weight.shape[0]
    span = own.shape[1]
    height = own.shape[0] // 8
    stage[0] = own[...]
    for position in range(8):
        where = pl.multiple_of(lax.bitwise_xor(node, position) * height, 16)
        for d in range(1, pieces):
            stage[d, pl.ds(where, height), :] = stacks[position][d - 1]
    norm_rows = []
    for z in range(pieces):
        where = lax.bitwise_xor(shard, z)
        cols = slice(z * span, (z + 1) * span)
        query_weight[:, cols] = stage[z, 0:width, :]
        gate_weight[:, cols] = stage[z, width : 2 * width, :]
        full_query[:, cols] = stage[where, 0:width, :]
        full_gate[:, cols] = stage[where, width : 2 * width, :]
        out_weight[cols, :] = stage[where, 2 * width : 3 * width, :].T
        norm_rows.append(stage[where, 3 * width : 3 * width + 16, :])
    turned = jnp.concatenate(norm_rows, axis=1).astype(fl_type).T
    gain[...] = jnp.broadcast_to(turned[:, 0:1], gain.shape)
    shift[...] = jnp.broadcast_to(turned[:, 1:2], shift.shape)


def key_weights_kernel(pieces, step, place, *refs):
    mine, other = refs[:pieces], refs[pieces : 2 * pieces]
    full, stage = refs[2 * pieces :]
    core = place[0]
    width, span = full.shape[1], mine[0].shape[1]
    for d in range(pieces):
        stage[d, pl.ds(pl.multiple_of(core * width, 16), width), :] = mine[d][0:width]
        stage[d, pl.ds(pl.multiple_of((1 - core) * width, 16), width), :] = other[d][0:width]
    for z in range(pieces):
        full[:, z * span : (z + 1) * span] = stage[lax.bitwise_xor(place[2], z)]


def query_kernel(step, place, x, weight, query_slope, query):
    sig = jax.nn.sigmoid(dot_nt(weight[...], x[...]))
    query_slope[...] = sig * (1.0 - sig)
    query[...] = sig.astype(bf_type)


def gate_kernel(step, place, x, weight, gate):
    rows = x.shape[0]
    valid = valid_row(place[3], step * rows, rows)
    gate[...] = jnp.where(valid, dot_nt(weight[...], x[...]), 0.0)


def grad_prod_kernel(step, place, g, out_weight, grad_prod):
    rows = g.shape[0]
    valid = valid_row(place[3], step * rows, rows)
    grad_prod[...] = jnp.where(valid, dot_nt(out_weight[...], g[...]), 0.0)


def place_chunks(chunk_refs, place, stage):
    node = place[1]
    for d in range(CHUNKS):
        stage[lax.bitwise_xor(node, d)] = chunk_refs[d][...]


def pair_rows(h, value):
    lane_head = lax.broadcasted_iota(jnp.int32, (1, value.shape[1]), 1) // (value.shape[1] // 2)
    return jnp.where(lane_head == h, value, jnp.zeros_like(value))


def pair_block(chunk, p, head):
    mine = chunk[:head, p * 2 * head : (p + 1) * 2 * head]
    return jnp.concatenate([pair_rows(0, mine), pair_rows(1, mine)], axis=0)


def head_rows(width, h, value):
    lane_head = lax.broadcasted_iota(jnp.int32, (1, width), 1) // (width // 4)
    return jnp.where(lane_head == h, value, jnp.zeros_like(value))


def middle_kernel(steps, lanes, step, place, ids, query, gate, grad_prod, gain, shift, *refs):
    chunk_refs = refs[:CHUNKS]
    prod_out, dgate_out, dnum_out, dden_out, keep, send = refs[CHUNKS : CHUNKS + 6]
    rest = refs[CHUNKS + 6 :]
    width, rows = query.shape
    parts = rows // lanes
    stage, left, acc, dgain, dshift = rest[:5]
    stacks, back_stacks, nums, normeds, dnormeds, dens, ddens = (
        rest[5 + i * parts : 5 + (i + 1) * parts] for i in range(7)
    )
    node, count = place[1], place[3]
    half = width // GROUPS
    head = half // 4

    @pl.when(step == 0)
    def _():
        place_chunks(chunk_refs, place, stage)
        for g in range(GROUPS):
            for c in range(CLUSTERS):
                chunk = stage[g * CLUSTERS + c].astype(fl_type)
                cols = slice(c * 2 * head, (c + 1) * 2 * head)
                for p in range(2):
                    mine = chunk[:, p * 2 * head : (p + 1) * 2 * head]
                    for h in range(2):
                        at = slice(h * head, (h + 1) * head)
                        left[g * 2 + p, at, cols] = pair_rows(h, mine[:head]).astype(bf_type)
                    sums = [pair_rows(h, mine[head : head + 1]) for h in range(2)]
                    sums.append(jnp.zeros((PAD - 2, 2 * head), fl_type))
                    left[g * 2 + p, 2 * head :, cols] = jnp.concatenate(sums, axis=0).astype(bf_type)
        acc[...] = jnp.zeros_like(acc)
        dgain[...] = jnp.zeros_like(dgain)
        dshift[...] = jnp.zeros_like(dshift)

    def forward(part):
        cols = slice(part * lanes, (part + 1) * lanes)
        table = members(ids.at[:, cols])
        stack, num, den = stacks[part], nums[part], dens[part]
        for p in range(PAIRS):
            at = slice(p * 2 * head, (p + 1) * 2 * head)
            mine = query[at, cols]
            for c in range(CLUSTERS):
                stack[p, c * 2 * head : (c + 1) * 2 * head, :] = mine * table[c : c + 1, :]
            both = dot_nn(left[p], stack[p])
            num[at, :] = both[: 2 * head]
            row = (p // 2) * 8 + (p % 2) * 2
            den[row : row + 2, :] = 1.0 / both[2 * head : 2 * head + 2]

    def norm(part):
        cols = slice(part * lanes, (part + 1) * lanes)
        num, dnormed, den, dden = nums[part], dnormeds[part], dens[part], ddens[part]
        spans = [slice(h * head, (h + 1) * head) for h in range(HEADS)]
        inverse = [den[(h // 4) * 8 + h % 4 : (h // 4) * 8 + h % 4 + 1, :] for h in range(HEADS)]

        def mean_of(blocks):
            return jnp.sum(tree_sum(blocks), axis=0, keepdims=True) * (1.0 / width)

        mean = mean_of([fold_rows(num[spans[h], :]) * inverse[h] for h in range(HEADS)])
        squares = []
        for h in range(HEADS):
            centered = num[spans[h], :] * inverse[h] - mean
            num[spans[h], :] = centered
            squares.append(fold_rows(centered * centered))
        scale = lax.rsqrt(mean_of(squares) + norm_eps)
        first, second = [], []
        for h in range(HEADS):
            span = spans[h]
            ah = num[span, :] * scale
            num[span, :] = ah
            gamma = jnp.concatenate([gain[span, :]] * (lanes // 128), axis=1)
            beta = jnp.concatenate([shift[span, :]] * (lanes // 128), axis=1)
            u = ah * gamma + beta
            zg = gate[span, cols]
            dp = grad_prod[span, cols]
            prod_out[span, cols] = (u * zg).astype(bf_type)
            du = dp * zg
            dgate_out[span, cols] = (dp * u).astype(bf_type)
            du_ah = du * ah
            dgain[span, :] += fold_lanes(du_ah)
            dshift[span, :] += fold_lanes(du)
            dah = gamma * du
            first.append(fold_rows(dah))
            second.append(fold_rows(gamma * du_ah))
            dnormed[span, :] = dah
        first = mean_of(first)
        second = mean_of(second)
        shifted = mean * scale
        for h in range(HEADS):
            span = spans[h]
            ah = num[span, :]
            rest = dnormed[span, :] - ah * second - first
            dnum_out[span, cols] = (rest * (scale * inverse[h])).astype(bf_type)
            inner = fold_rows(rest * ah) + shifted * fold_rows(rest)
            row = (h // 4) * 8 + h % 4
            dden[row : row + 1, :] = -jnp.sum(inner, axis=0, keepdims=True) * inverse[h]
        dden_out[:, cols] = dden[...]

    def backward(part):
        cols = slice(part * lanes, (part + 1) * lanes)
        table = members(ids.at[:, cols])
        stack, dden = back_stacks[part], ddens[part]
        for g in range(GROUPS):
            mine = dnum_out[g * half : (g + 1) * half, cols]
            for c in range(CLUSTERS):
                stack[g, c * half : (c + 1) * half, :] = mine * table[c : c + 1, :]
            den_rows = dden[g * 8 : g * 8 + 4, :]
            high = den_rows.astype(bf_type)
            low = (den_rows - high.astype(fl_type)).astype(bf_type)
            four_high = jnp.concatenate([high * table[c : c + 1, :] for c in range(CLUSTERS)], axis=0)
            four_low = jnp.concatenate([low * table[c : c + 1, :] for c in range(CLUSTERS)], axis=0)
            stack[g, CLUSTERS * half :, :] = jnp.concatenate([four_high, four_low], axis=0)
            acc[g] += dot_nt(stack[g], query[g * half : (g + 1) * half, cols])

    for part in range(parts):
        forward(part)
    for part in range(parts):
        norm(part)
        backward(part)

    @pl.when(step == steps - 1)
    def _():
        gain_row = jnp.sum(dgain[...].T, axis=0, keepdims=True)
        shift_row = jnp.sum(dshift[...].T, axis=0, keepdims=True)

        def extra(g, c):
            base = CLUSTERS * half
            row = jnp.zeros((1, half), fl_type)
            for h in range(4):
                at = base + c * 4 + h
                row = row + head_rows(half, h, acc[g, at : at + 1, :] + acc[g, at + 16 : at + 17, :])
            cols = slice(g * half, (g + 1) * half)
            tail = [row]
            if c == 0:
                tail += [gain_row[:, cols], shift_row[:, cols]]
            tail.append(jnp.zeros((PAD - len(tail), half), fl_type))
            return jnp.concatenate(tail, axis=0)

        put_chunks(acc, keep, send, node, extra)


def fold_rows(block):
    return tree_sum([block[i * 8 : (i + 1) * 8] for i in range(block.shape[0] // 8)])


def fold_lanes(block):
    return tree_sum([block[:, i * 128 : (i + 1) * 128] for i in range(block.shape[1] // 128)])


def write_pieces(pieces, node, shard, span, keep, send, blocks):
    for chunk in range(8):
        distance = lax.bitwise_xor(node, chunk)
        slot = lax.shift_right_logical(distance, 1)
        even = lax.bitwise_and(distance, 1) == 0
        for z in range(pieces):
            block = blocks(z, chunk)

            @pl.when(even)
            def _():
                keep[slot, z] = block

            @pl.when(jnp.logical_not(even))
            def _():
                send[slot, z] = block.astype(bf_type)


def query_back_kernel(step, place, ids, dnum, dden, query_slope, *refs):
    chunk_refs = refs[:CHUNKS]
    dquery_out = refs[CHUNKS]
    stage, left, sums, stack = refs[CHUNKS + 1 :]
    width, rows = dnum.shape
    half = width // GROUPS
    head = half // 4

    @pl.when(step == 0)
    def _():
        place_chunks(chunk_refs, place, stage)
        for gr in range(GROUPS):
            for c in range(CLUSTERS):
                chunk = stage[gr * CLUSTERS + c].astype(fl_type)
                for p in range(2):
                    cols = slice(c * 2 * head, (c + 1) * 2 * head)
                    left[gr * 2 + p, :, cols] = pair_block(chunk, p, head).T.astype(bf_type)
                column = chunk[head : head + 8].T
                sums[c, gr * half : (gr + 1) * half, :] = jnp.broadcast_to(column[:, 0:1], (half, 128))

    table = members(ids)
    for p in range(PAIRS):
        part = dnum[p * 2 * head : (p + 1) * 2 * head, :]
        for c in range(CLUSTERS):
            stack[p, c * 2 * head : (c + 1) * 2 * head, :] = part * table[c : c + 1, :]
        dq = dot_nn(left[p], stack[p])
        for h in range(2):
            at = slice((p * 2 + h) * head, (p * 2 + h + 1) * head)
            pick = pick_rows(sums, at, ids, rows)
            row = (p // 2) * 8 + (p % 2) * 2 + h
            full = dq[h * head : (h + 1) * head] + dden[row : row + 1, :] * pick
            dquery_out[at, :] = (full * query_slope[at, :]).astype(bf_type)


def grad_query_kernel(step, place, dquery, x, grad_query):
    @pl.when(step == 0)
    def _():
        grad_query[...] = jnp.zeros_like(grad_query)

    grad_query[...] += dot_nn(dquery[...], x[...])


def gate_back_kernel(step, place, dgate, prod, x, g, grad_gate, grad_out):
    @pl.when(step == 0)
    def _():
        grad_gate[...] = jnp.zeros_like(grad_gate)
        grad_out[...] = jnp.zeros_like(grad_out)

    grad_gate[...] += dot_nn(dgate[...], x[...])
    grad_out[...] += dot_nn(prod[...], g[...])


def fold(block, span):
    return jnp.concatenate(
        [block[:, i * span : (i + 1) * span] for i in range(block.shape[1] // span)], axis=0
    )


def pick_rows(sums, at, ids, rows):
    reps = rows // 128
    wide = [jnp.concatenate([sums[c, at, :]] * reps, axis=1) for c in range(CLUSTERS)]
    pick = wide[CLUSTERS - 1]
    for c in range(CLUSTERS - 1):
        pick = jnp.where(ids[...] == c, wide[c], pick)
    return pick


def output_kernel(step, place, x, prod, out_weight, result):
    result[...] = x[...].astype(fl_type) + dot_tn(prod[...], out_weight[...])


def key_back_kernel(pieces, steps, step, place, ids, key_slope, key, value, x, grad_query, grad_gate, grad_out, *refs):
    chunk_refs = refs[:CHUNKS]
    dkey_out, dvalue_out, norm_out, keep, send = refs[CHUNKS : CHUNKS + 5]
    stage, left_key, left_value, sums, stack, key_stack, acc = refs[CHUNKS + 5 :]
    node, shard, count = place[1], place[2], place[3]
    width, rows = value.shape
    half = width // GROUPS
    head = half // 4
    span = width // pieces

    @pl.when(step == 0)
    def _():
        place_chunks(chunk_refs, place, stage)
        for gr in range(GROUPS):
            for c in range(CLUSTERS):
                chunk = stage[gr * CLUSTERS + c].astype(fl_type)
                for p in range(2):
                    cols = slice(c * 2 * head, (c + 1) * 2 * head)
                    pair = pair_block(chunk, p, head)
                    left_value[gr * 2 + p, :, cols] = pair.astype(bf_type)
                    left_key[gr * 2 + p, :, cols] = pair.T.astype(bf_type)
                column = chunk[head : head + 8].T
                sums[c, gr * half : (gr + 1) * half, :] = jnp.broadcast_to(column[:, 0:1], (half, 128))
                if c == 0:
                    norm_out[:, gr * half : (gr + 1) * half] = chunk[head : head + 8]
        acc[...] = jnp.zeros_like(acc)

    table = members(ids)
    valid = valid_row(count, step * rows, rows)
    for p in range(PAIRS):
        at = slice(p * 2 * head, (p + 1) * 2 * head)
        part = value[at, :]
        for c in range(CLUSTERS):
            stack[p, c * 2 * head : (c + 1) * 2 * head, :] = part * table[c : c + 1, :]
        dk = dot_nn(left_key[p], stack[p])
        for h in range(2):
            sub = slice((p * 2 + h) * head, (p * 2 + h + 1) * head)
            full = dk[h * head : (h + 1) * head] + pick_rows(sums, sub, ids, rows)
            dkey_out[sub, :] = (full * key_slope[sub, :]).astype(bf_type)
        part = key[at, :]
        for c in range(CLUSTERS):
            key_stack[p, c * 2 * head : (c + 1) * 2 * head, :] = part * table[c : c + 1, :]
        dvalue_out[at, :] = dot_nn(left_value[p], key_stack[p]).astype(bf_type)
    acc[0:width] += dot_nn(dkey_out[...], x[...])
    acc[width : 2 * width] += dot_nn(dvalue_out[...], x[...])

    @pl.when(step == steps - 1)
    def _():
        tall = 2 * width // 8
        lanes = width // 4
        short = span // 2

        def blocks(z, chunk):
            cols = slice(z * span, (z + 1) * span)
            top = acc[chunk * tall : (chunk + 1) * tall, cols]
            source = grad_query if chunk < 4 else grad_gate
            center = source[(chunk % 4) * tall : (chunk % 4 + 1) * tall, cols]
            start = pl.multiple_of(lax.bitwise_xor(shard, z) * span + (chunk % 2) * short, 8)
            bottom = grad_out[pl.ds(start, short), (chunk // 2) * lanes : (chunk // 2 + 1) * lanes]
            return jnp.concatenate([top, center, fold(bottom, span)], axis=0)

        write_pieces(pieces, node, shard, span, keep, send, blocks)


def input_kernel(step, place, dquery, dkey, dvalue, dgate, full_query, full_key, full_gate, g, result):
    width = g.shape[1]
    total = g[...].astype(fl_type)
    total = total + dot_tn(dquery[...], full_query[...])
    total = total + dot_tn(dkey[...], full_key[0:width, :])
    total = total + dot_tn(dvalue[...], full_key[width:, :])
    total = total + dot_tn(dgate[...], full_gate[...])
    result[...] = total


def finish_kernel(step, *refs):
    parts, sums = refs[:-1], refs[-1]
    sums[...] = tree_sum([p[...].astype(fl_type) for p in parts]).astype(bf_type)


def squares_kernel(step, *refs):
    parts, squares = refs[:-1], refs[-1]
    totals = []
    for part in parts:
        value = part[...].astype(fl_type)
        totals.append(fold_rows(value * value))
    total = jnp.sum(tree_sum(totals), axis=0, keepdims=True)
    squares[...] = jnp.broadcast_to(jnp.sum(total, axis=1, keepdims=True), squares.shape)


def assemble_kernel(step, place, *refs):
    parts, (grad_proj, grad_out, stage) = refs[:CHUNKS], refs[CHUNKS:]
    node = place[1]
    span, width = grad_out.shape
    tall = 2 * width // 8
    lanes = width // 4
    rows = span // 2
    folds = lanes // span
    for d in range(CHUNKS):
        chunk = lax.bitwise_xor(node, d)
        stage[chunk] = parts[d][...].astype(fl_type)
    for chunk in range(CHUNKS):
        query_at = (0 if chunk < 4 else 3 * width) + (chunk % 4) * tall
        grad_proj[:, width + chunk * tall : width + (chunk + 1) * tall] = stage[chunk, 0:tall].T
        grad_proj[:, query_at : query_at + tall] = stage[chunk, tall : 2 * tall].T
        for i in range(folds):
            at = slice((chunk // 2) * lanes + i * span, (chunk // 2) * lanes + (i + 1) * span)
            block = stage[chunk, 2 * tall + i * rows : 2 * tall + (i + 1) * rows]
            grad_out[(chunk % 2) * rows : (chunk % 2 + 1) * rows, at] = block


def adam(master_w, moment_old, square_old, clipped, decay_coef, step_rate):
    moment_new = beta_one * moment_old + (1.0 - beta_one) * clipped
    square_new = beta_two * square_old + (1.0 - beta_two) * clipped * clipped
    moment_hat = moment_new * (1.0 / (1.0 - beta_one**STEP))
    square_hat = square_new * (1.0 / (1.0 - beta_two**STEP))
    master_new = master_w * (1.0 - step_rate * decay_coef) - step_rate * moment_hat / (
        jnp.sqrt(square_hat) + adam_eps
    )
    return moment_new, square_new, master_new


def update_kernel(pieces, step, place, *refs):
    squares, (gp, go, gn, pw, pm, ps, ow, om, osq, nw, nm, ns) = refs[:pieces], refs[pieces : pieces + 12]
    size, *results = refs[pieces + 12 : pieces + 25]
    p_out, o_out, n_out = results[0:4], results[4:8], results[8:12]
    new_p, new_pc, new_o, new_oc, new_n, sems = refs[pieces + 25 :]
    shard = place[2]
    span, width = ow.shape
    norm_grad = gn[1:3, :]
    norm_square = jnp.sum(norm_grad * norm_grad, axis=0, keepdims=True)
    total = tree_sum([q[0:1, 0:1] for q in squares]) + jnp.sum(norm_square, axis=1, keepdims=True)
    norm = jnp.sqrt(total)
    size[...] = norm
    clip_level = 0.5 * math.sqrt(5 * width * width + 2 * width)
    scale = jnp.minimum(1.0, clip_level / norm)
    copies = []

    def send(source, target):
        copies.append(pltpu.make_async_copy(source, target, sems.at[len(copies)]))
        copies[-1].start()

    scale = jnp.broadcast_to(scale, (1, width))

    def step_block(at, cols, w, m, s, grad, new, new_copy):
        results = adam(w[at, cols], m[at, cols], s[at, cols], grad[at, cols] * scale, decay_rate, learn_rate)
        for j, value in zip((2, 0, 1), (results[2], *results[:2])):
            new[j, at, :] = value
        new_copy[at, :] = results[2].astype(bf_type)

    blocks = [slice(r, r + 16) for r in range(0, span, 16)]
    for i in range(4):
        cols = slice(i * width, (i + 1) * width)
        for at in blocks:
            step_block(at, cols, pw, pm, ps, gp, new_p.at[:, i], new_pc.at[i])
        for j in range(3):
            send(new_p.at[j, i], p_out[j].at[:, cols])
        send(new_pc.at[i], p_out[3].at[:, cols])
    for at in blocks:
        step_block(at, slice(0, width), ow, om, osq, go, new_o, new_oc)
    for j in range(3):
        send(new_o.at[j], o_out[j])
    send(new_oc, o_out[3])
    mine = norm_grad[:, 0:span]
    for z in range(1, pieces):
        mine = jnp.where(shard == z, norm_grad[:, z * span : (z + 1) * span], mine)
    clipped = mine * scale[:, 0:span]
    for j, value in enumerate((clipped, *adam(nw[...], nm[...], ns[...], clipped, 0.0, norm_rate))):
        new_n[j] = value
        send(new_n.at[j], n_out[j])
    for copy in copies:
        copy.wait()


def make_exchange(nodes, shards):
    count = nodes * shards

    def exchange(value, node_bits, shard_bits):
        pairs = [
            (i, ((i // shards) ^ node_bits) * shards + ((i % shards) ^ shard_bits)) for i in range(count)
        ]
        return lax.ppermute(value, AXES, pairs)

    return exchange


def tree_sum(parts):
    parts = list(parts)
    while len(parts) > 1:
        pairs = [parts[i] + parts[i + 1] for i in range(0, len(parts) - 1, 2)]
        parts = pairs + parts[len(parts) - len(parts) % 2 :]
    return parts[0]


def to_float(parts):
    return [p.astype(fl_type) for p in parts]


def tie(value, *others):
    return lax.optimization_barrier((value, *others))[0]


def tie(value, *others):
    return lax.optimization_barrier((value, *others))[0]


def local(nodes, shards, *args):
    (x, g, ids, counts, pw, pm, ps, ow, om, osq, nw, nm, ns) = args
    exchange = make_exchange(nodes, shards)
    outer = nodes // 8
    rows, width = x.shape
    half = width // GROUPS
    head = width // HEADS
    span = pw.shape[0]
    block = min(1024, rows)
    steps = rows // block
    lanes = 256
    tall = 2 * width // 8
    part_rows = (3 * width + 2 + 127) // 128 * 16
    work = 2 * rows * width * width

    node = lax.axis_index("nodes").astype(jnp.int32)
    shard = lax.axis_index("shard").astype(jnp.int32)
    place = jnp.stack([lax.bitwise_and(node, 1), lax.bitwise_and(node, 7), shard, counts[0]])
    ids = ids.reshape(1, rows)
    chunk_shape = (4, head + PAD, half)

    def wide(dtype):
        return out((width, rows), dtype)

    def vmem(shape, dtype):
        return pltpu.VMEM(shape, dtype)

    message, kv_half, part, query_all = call(
        prep_kernel,
        1,
        (pw, ow, nw),
        ["hbm"] * 3,
        [
            out((width, span), bf_type),
            out((width, span), bf_type),
            out((part_rows, span), bf_type),
            out((8 * part_rows, span), bf_type),
        ],
        [None] * 4,
        [
            vmem((5, span, width), fl_type),
            vmem((2, span), fl_type),
            vmem((2, width, span), bf_type),
            pltpu.SemaphoreType.DMA((6,)),
        ],
        1e6,
        "prep",
        vmem=60,
    )
    mine, other = [message], [kv_half]
    for z in range(1, shards):
        mine.append(exchange(message, 0, z))
    stack = jnp.stack([exchange(part, 0, z) for z in range(1, shards)])
    stacks = [stack] + [None] * 7
    for e in range(1, 4):
        stacks[2 * e] = exchange(stack, 2 * e, 0)
    for z in range(1, shards):
        other.append(exchange(tie(mine[z], stack), 1, 0))
    x_turned = jnp.concatenate(
        [
            lax.dynamic_slice(x, (0, lax.bitwise_xor(shard, z) * span), (rows, span))
            for z in range(shards)
        ],
        axis=1,
    )

    key_slope, key, value, keep, send = call(
        functools.partial(key_kernel, shards, steps),
        steps,
        (place, x_turned, ids, *mine, *other),
        ["smem", "row", "lane"] + [None] * (2 * shards),
        [wide(fl_type), wide(bf_type), wide(bf_type), out(chunk_shape, fl_type), out(chunk_shape, bf_type)],
        ["lane", "lane", "lane", None, None],
        [
            vmem((2 * width, width), bf_type),
            vmem((CLUSTERS * half + PAD, block), bf_type),
            vmem((GROUPS, CLUSTERS * half + PAD, half), fl_type),
        ],
        1e3,
        "keys",
        block,
    )

    def swap(pieces, peers, filler):
        got = [exchange(p, *at) for p, at in zip(pieces, peers)]
        if filler is not None:
            done = filler(pieces[0])
            got = list(tie(tuple(got), done))
        return to_float(got)

    plane = [(2 * e, 0) for e in range(1, 4)]
    along = [(0, z) for z in range(1, shards)]
    made = {}

    def reduce_chunks(keep, send, fillers):
        mine = keep + exchange(send, 1, 0).astype(fl_type)
        got = swap([mine[e].astype(bf_type) for e in range(1, 4)], plane, fillers[0])
        own = tree_sum([mine[0], *got]).astype(bf_type)
        got = swap([own] * (shards - 1), along, fillers[1])
        own = tree_sum([own.astype(fl_type), *got]).astype(bf_type)
        if outer > 1:
            got = swap([own] * (outer - 1), [(8 * o, 0) for o in range(1, outer)], None)
            own = tree_sum([own.astype(fl_type), *got]).astype(bf_type)
        return spread(own, fillers[2])

    def spread(own, filler=None):
        chunks = [own] + [None] * 7
        for e in range(1, 4):
            chunks[2 * e] = exchange(own, 2 * e, 0)
        chunks[1] = exchange(own, 1, 0)
        if filler is not None:
            done = filler(own)
            chunks[2], chunks[4], chunks[6] = tie((chunks[2], chunks[4], chunks[6]), done)
        for e in range(1, 4):
            chunks[2 * e + 1] = exchange(chunks[2 * e], 1, 0)
        return chunks

    def fill_weights(dep):
        made["weights"] = call(
            functools.partial(weights_kernel, shards),
            1,
            (tie(place, dep), query_all, *stacks),
            ["smem", None] + [None] * 8,
            [
                out((width, width), bf_type),
                out((width, width), bf_type),
                out((width, width), bf_type),
                out((width, 128), fl_type),
                out((width, 128), fl_type),
                out((width, width), bf_type),
                out((width, width), bf_type),
            ],
            [None] * 7,
            [vmem((shards, 8 * part_rows, span), bf_type)],
            1e6,
            "weights",
        )
        return made["weights"][0]

    def fill_query(dep):
        made["query"] = call(
            query_kernel,
            1,
            (tie(place, dep), x_turned, made["weights"][0]),
            ["smem", "row", None],
            [wide(fl_type), wide(bf_type)],
            ["lane"] * 2,
            [],
            work,
            "query",
            rows,
            vmem=16,
        )
        return made["query"][1], fill_gate(dep)

    def fill_gate(dep):
        gate_weight = made["weights"][1]
        made["gate"] = call(
            gate_kernel,
            1,
            (tie(place, dep), x_turned, gate_weight),
            ["smem", "row", None],
            [wide(fl_type)],
            ["lane"],
            [],
            work,
            "gate",
            rows,
            vmem=16,
        )[0]
        return made["gate"]

    def fill_grad_prod(dep):
        out_weight = made["weights"][2]
        made["grad_prod"] = call(
            grad_prod_kernel,
            1,
            (tie(place, dep), g, out_weight),
            ["smem", "row", None],
            [wide(fl_type)],
            ["lane"],
            [],
            work,
            "grad_prod",
            rows,
            vmem=16,
        )[0]
        return made["grad_prod"]

    send = tie(send, *stacks[2::2])
    for e in range(4):
        stacks[2 * e + 1] = exchange(stacks[2 * e], 1, 0)
    chunks = reduce_chunks(keep, send, (fill_weights, fill_query, fill_grad_prod))
    out_weight, gain, shift, full_query, full_gate = made["weights"][2:]
    query_slope, query = made["query"]

    parts = block // lanes
    prod, dgate, dnum, dden, keep, send = call(
        functools.partial(middle_kernel, steps, lanes),
        steps,
        (place, ids, query, made["gate"], made["grad_prod"], gain, shift, *chunks),
        ["smem", "lane", "lane", "lane", "lane", None, None] + [None] * CHUNKS,
        [
            wide(bf_type),
            wide(bf_type),
            wide(bf_type),
            out((16, rows), fl_type),
            out(chunk_shape, fl_type),
            out(chunk_shape, bf_type),
        ],
        ["lane", "lane", "lane", "lane", None, None],
        [
            vmem((CHUNKS, head + PAD, half), bf_type),
            vmem((PAIRS, 2 * head + PAD, CLUSTERS * 2 * head), bf_type),
            vmem((GROUPS, CLUSTERS * half + 32, half), fl_type),
            vmem((width, 128), fl_type),
            vmem((width, 128), fl_type),
        ]
        + [vmem((PAIRS, CLUSTERS * 2 * head, lanes), bf_type)] * parts
        + [vmem((GROUPS, CLUSTERS * half + 32, lanes), bf_type)] * parts
        + [vmem((width, lanes), fl_type)] * (3 * parts)
        + [vmem((16, lanes), fl_type)] * (2 * parts),
        6 * work,
        "middle",
        block,
    )

    def fill_gate_back(dep):
        made["gate_back"] = call(
            gate_back_kernel,
            1,
            (tie(place, dep), dgate, prod, x_turned, g),
            ["smem", "lane", "lane", "row", "row"],
            [out((width, width), fl_type)] * 2,
            [None] * 2,
            [],
            2 * work,
            "gate_back",
            rows,
            vmem=16,
        )
        return made["gate_back"][0]

    def fill_output(dep):
        made["output"] = call(
            output_kernel,
            steps,
            (tie(place, dep), x, prod, out_weight),
            ["smem", "row", "lane", None],
            [out((rows, width), fl_type)],
            ["row"],
            [],
            work,
            "output",
            block,
            piped=True,
        )[0]
        return made["output"]

    def fill_query_back(dep):
        made["dquery"] = call(
            query_back_kernel,
            steps,
            (tie(place, dep), ids, dnum, dden, query_slope, *chunks),
            ["smem", "lane", "lane", "lane", "lane"] + [None] * CHUNKS,
            [wide(bf_type)],
            ["lane"],
            [
                vmem((CHUNKS, head + PAD, half), bf_type),
                vmem((PAIRS, 2 * head, CLUSTERS * 2 * head), bf_type),
                vmem((CLUSTERS, width, 128), fl_type),
                vmem((PAIRS, CLUSTERS * 2 * head, block), bf_type),
            ],
            2 * work,
            "query_back",
            block,
        )[0]
        return made["dquery"]

    def fill_grad_query(dep):
        made["grad_query"] = call(
            grad_query_kernel,
            1,
            (tie(place, dep), made["dquery"], x_turned),
            ["smem", None, None],
            [out((width, width), fl_type)],
            [None],
            [],
            work,
            "grad_query",
            vmem=12,
        )[0]
        return made["grad_query"]

    back_chunks = reduce_chunks(keep, send, (fill_gate_back, fill_query_back, fill_grad_query))
    dquery, grad_query = made["dquery"], made["grad_query"]

    height = 2 * tall + (span // 2) * (width // 4 // span)
    piece_shape = (4, shards, height, span)
    dkey, dvalue, norm_grad, keep, send = call(
        functools.partial(key_back_kernel, shards, steps),
        steps,
        (place, ids, key_slope, key, value, x_turned, grad_query, *made["gate_back"], *back_chunks),
        ["smem", "lane", "lane", "lane", "lane", "row"] + [None] * (3 + CHUNKS),
        [
            wide(bf_type),
            wide(bf_type),
            out((8, width), fl_type),
            out(piece_shape, fl_type),
            out(piece_shape, bf_type),
        ],
        ["lane", "lane", None, None, None],
        [
            vmem((CHUNKS, head + PAD, half), bf_type),
            vmem((PAIRS, 2 * head, CLUSTERS * 2 * head), bf_type),
            vmem((PAIRS, 2 * head, CLUSTERS * 2 * head), bf_type),
            vmem((CLUSTERS, width, 128), fl_type),
            vmem((PAIRS, CLUSTERS * 2 * head, block), bf_type),
            vmem((PAIRS, CLUSTERS * 2 * head, block), bf_type),
            vmem((2 * width, width), fl_type),
        ],
        6 * work,
        "key_back",
        block,
    )

    full_key = call(
        functools.partial(key_weights_kernel, shards),
        1,
        (place, *mine, *other),
        ["smem"] + [None] * (2 * shards),
        [out((2 * width, width), bf_type)],
        [None],
        [vmem((shards, 2 * width, span), bf_type)],
        1e6,
        "key_weights",
        vmem=12,
    )[0]

    def fill_inputs(dep):
        made["inputs"] = call(
            input_kernel,
            steps,
            (tie(place, dep), dquery, dkey, dvalue, dgate, full_query, full_key, full_gate, g),
            ["smem"] + ["lane"] * 4 + [None] * 3 + ["row"],
            [out((rows, width), fl_type)],
            ["row"],
            [],
            4 * work,
            "inputs",
            block,
            piped=True,
        )[0]
        fill_output(dep)
        return made["inputs"], made["output"]

    mine_sum = keep + exchange(send, 1, 0).astype(fl_type)
    got = swap([mine_sum[e].astype(bf_type) for e in range(1, 4)], plane, fill_inputs)
    mine_sum = tree_sum([mine_sum[0], *got])
    got = [exchange(mine_sum[z].astype(bf_type), *along[z - 1]) for z in range(1, shards)]
    owned_parts = [mine_sum[0], *got]
    if outer > 1:
        own = tree_sum(to_float(owned_parts)).astype(bf_type)
        got = [own] + [exchange(own, 8 * o, 0) for o in range(1, outer)]
        owned_parts = [tree_sum(to_float(got))] + [jnp.zeros_like(own)] * (shards - 1)

    sums = call(
        finish_kernel,
        1,
        owned_parts,
        [None] * shards,
        [out((height, span), bf_type)],
        [None],
        [],
        1e6,
        "finish",
        vmem=4,
    )[0]
    parts = spread(sums)
    squares = call(
        squares_kernel,
        1,
        parts,
        [None] * CHUNKS,
        [out((8, 128), fl_type)],
        [None],
        [],
        1e6,
        "squares",
        vmem=4,
    )[0]

    def fill_assemble(dep):
        made["grads"] = call(
            assemble_kernel,
            1,
            (tie(place, dep), *parts),
            ["smem"] + [None] * CHUNKS,
            [out((span, 4 * width), fl_type), out((span, width), fl_type)],
            [None] * 2,
            [vmem((CHUNKS, height, span), fl_type)],
            1e6,
            "assemble",
            vmem=8,
        )
        return made["grads"][0]

    squares = [squares, *swap([squares] * (shards - 1), along, fill_assemble)]
    states = (pw, pm, ps, ow, om, osq, nw, nm, ns)
    like = [pw] * 4 + [ow] * 4 + [nw] * 4
    kinds = [fl_type] * 3 + [bf_type] + [fl_type] * 3 + [bf_type] + [fl_type] * 4
    grad_size, *new = call(
        functools.partial(update_kernel, shards),
        1,
        (place, *squares, *made["grads"], norm_grad, *states),
        ["smem"] + [None] * (shards + 12),
        [out((1, 1), fl_type)] + [out(s.shape, k) for s, k in zip(like, kinds)],
        [None] + ["hbm"] * 12,
        [
            vmem((3, 4, span, width), fl_type),
            vmem((4, span, width), bf_type),
            vmem((3, span, width), fl_type),
            vmem((span, width), bf_type),
            vmem((4, 2, span), fl_type),
            pltpu.SemaphoreType.DMA((24,)),
        ],
        1e6,
        "update",
    )
    return (made["output"], made["inputs"], grad_size.reshape(1), *new)


def solution(mesh):
    nodes, shards = mesh.shape["nodes"], mesh.shape["shard"]
    by_node = P(AXES, None)
    rows = P("shard", None)
    cols = P(None, "shard")
    return jax.shard_map(
        functools.partial(local, nodes, shards),
        mesh=mesh,
        in_specs=(by_node, by_node, P(AXES), P(AXES)) + (rows,) * 6 + (cols,) * 3,
        out_specs=(by_node, by_node, P()) + (rows,) * 8 + (cols,) * 4,
        check_vma=False,
    )
```

```python
import functools
import math

import jax
import jax.numpy as jnp
from jax import lax
from jax.experimental import pallas as pl
from jax.experimental.pallas import tpu as pltpu
from jax.sharding import PartitionSpec as P

HEADS = 8
CLUSTERS = 4
STEP = 10
AXES = ("nodes", "shard")

norm_eps = 1e-05
beta_one = 0.9
beta_two = 0.999
learn_rate = 0.05
norm_rate = 0.5
decay_rate = 0.01
adam_eps = 1e-08
bf_type = jnp.bfloat16
fl_type = jnp.float32

GROUPS = 2
PAIRS = HEADS // 2
CHUNKS = GROUPS * CLUSTERS
PAD = 16


def dot_nn(a, b):
    return lax.dot_general(a, b, (((1,), (0,)), ((), ())), preferred_element_type=fl_type)


def dot_nt(a, b):
    return lax.dot_general(a, b, (((1,), (1,)), ((), ())), preferred_element_type=fl_type)


def dot_tn(a, b):
    return lax.dot_general(a, b, (((0,), (0,)), ((), ())), preferred_element_type=fl_type)


def whole(shape):
    return pl.BlockSpec(shape, lambda *_: (0,) * len(shape))


def smem():
    return pl.BlockSpec(memory_space=pltpu.SMEM)


def view(ref, kind, start, size):
    if kind == "lane":
        return ref.at[:, pl.ds(start, size)]
    if kind == "row":
        return ref.at[pl.ds(start, size), :]
    return ref


def call(kernel, steps, ins, in_kinds, outs, out_kinds, scratch, flops, name, block=0, vmem=16, piped=False):
    moved = sum(math.prod(a.shape) * a.dtype.itemsize for a in (*ins, *outs))
    arrays, kinds = [*ins, *outs], [*in_kinds, *out_kinds]

    def spec(array, kind):
        if kind == "smem":
            return smem()
        if kind == "hbm":
            return pl.BlockSpec(memory_space=pltpu.HBM)
        if isinstance(kind, pl.BlockSpec):
            return kind
        if piped and kind == "lane":
            return pl.BlockSpec((array.shape[0], block), lambda i: (0, i))
        if piped and kind == "row":
            return pl.BlockSpec((block, array.shape[1]), lambda i: (i, 0))
        return whole(array.shape)

    def body(*refs):
        if piped:
            kernel(pl.program_id(0), *refs)
            return
        if steps == 1:
            kernel(0, *refs)
            return

        def one(i, carry):
            start = pl.multiple_of(i * block, block)
            views = [view(r, k, start, block) for r, k in zip(refs, kinds)]
            kernel(i, *views, *refs[len(kinds) :])
            return carry

        lax.fori_loop(0, steps, one, 0)

    specs = [spec(a, k) for a, k in zip(arrays, kinds)]
    return pl.pallas_call(
        body,
        grid=(steps,) if piped else (),
        in_specs=specs[: len(ins)],
        out_specs=specs[len(ins) :],
        out_shape=outs,
        scratch_shapes=scratch,
        cost_estimate=pl.CostEstimate(flops=int(flops), transcendentals=0, bytes_accessed=int(moved)),
        compiler_params=pltpu.CompilerParams(vmem_limit_bytes=vmem * 1024 * 1024),
        name=name,
    )(*ins)


def out(shape, dtype):
    return jax.ShapeDtypeStruct(shape, dtype)


def fetch(copies):
    copies = [pltpu.make_async_copy(*c) for c in copies]
    for c in copies:
        c.start()
    return copies


def prep_kernel(step, wp, wo, wn, key_message, key_other, message, query_all, block, rows, stage, sems):
    core = lax.bitwise_and(lax.axis_index("nodes"), 1)
    part = lax.bitwise_and(lax.axis_index("nodes"), 7)
    shard, width = wo.shape
    columns = [wp.at[:, i * width : (i + 1) * width] for i in (1, 2, 0, 3)]
    sources = [*columns, wo]
    copies = fetch(
        [(sources[i], block.at[i], sems.at[i]) for i in range(5)] + [(wn, rows, sems.at[5])]
    )
    for i in range(2):
        copies[i].wait()
        stage[i] = block[i].T.astype(bf_type)
    key_message[...] = stage[core]
    key_other[...] = stage[1 - core]
    for i in range(3):
        copies[2 + i].wait()
        query_all[i * width : (i + 1) * width] = block[2 + i].T.astype(bf_type)
    copies[5].wait()
    rest = query_all.shape[0] - 3 * width
    tail = jnp.concatenate([rows[...], jnp.zeros((rest - 2, shard), fl_type)], axis=0)
    query_all[3 * width :] = tail.astype(bf_type)
    height = query_all.shape[0] // 8
    message[...] = query_all[pl.ds(pl.multiple_of(part * height, 16), height)]


def members(ids_ref):
    rows = ids_ref.shape[1]
    classes = lax.broadcasted_iota(jnp.int32, (PAD, rows), 0)
    return (classes == ids_ref[...]).astype(fl_type).astype(bf_type)


def valid_row(count, start, rows):
    slots = lax.broadcasted_iota(jnp.int32, (1, rows), 1) + start
    return slots < count


def put_chunks(acc, keep, send, node, extra):
    width = acc.shape[2]
    head = width // 4
    for g in range(GROUPS):
        for c in range(CLUSTERS):
            chunk = g * CLUSTERS + c
            distance = lax.bitwise_xor(node, chunk)
            slot = lax.shift_right_logical(distance, 1)
            lane_head = lax.broadcasted_iota(jnp.int32, (head, width), 1) // head
            body = jnp.zeros((head, width), fl_type)
            for h in range(4):
                rows = acc[g, c * width + h * head : c * width + (h + 1) * head, :]
                body = jnp.where(lane_head == h, rows, body)
            block = jnp.concatenate([body, extra(g, c)], axis=0)

            @pl.when(lax.bitwise_and(distance, 1) == 0)
            def _():
                keep[slot] = block

            @pl.when(lax.bitwise_and(distance, 1) == 1)
            def _():
                send[slot] = block.astype(bf_type)


def key_kernel(pieces, step, place, x, ids, *refs):
    mine, other = refs[:pieces], refs[pieces : 2 * pieces]
    key_slope, key_out, value_out, keep, send, weights, masked, acc = refs[2 * pieces :]
    core, node, count = place[0], place[1], place[3]
    width = x.shape[1]
    rows = x.shape[0]
    half = width // GROUPS

    span = mine[0].shape[1]
    for d in range(pieces):
        cols = slice(d * span, (d + 1) * span)
        weights[pl.ds(pl.multiple_of(core * width, 16), width), cols] = mine[d][...]
        weights[pl.ds(pl.multiple_of((1 - core) * width, 16), width), cols] = other[d][...]

    table = members(ids)
    valid = valid_row(count, step * rows, rows)
    for g in range(GROUPS):
        sig = jax.nn.sigmoid(dot_nt(weights[g * half : (g + 1) * half, :], x[...]))
        kept = jnp.where(valid, sig, 0.0)
        key_slope[g * half : (g + 1) * half, :] = kept * (1.0 - sig)
        keys = kept.astype(bf_type)
        key_out[g * half : (g + 1) * half, :] = keys
        value = dot_nt(weights[width + g * half : width + (g + 1) * half, :], x[...]).astype(bf_type)
        value_out[g * half : (g + 1) * half, :] = value
        for c in range(CLUSTERS):
            masked[c * half : (c + 1) * half, :] = value * table[c : c + 1, :]
        masked[CLUSTERS * half :, :] = table
        acc[g] = dot_nt(masked[...], keys)

    def extra(g, c):
        row = acc[g, CLUSTERS * half + c : CLUSTERS * half + c + 1, :]
        return jnp.concatenate([row, jnp.zeros((PAD - 1, half), fl_type)], axis=0)

    put_chunks(acc, keep, send, node, extra)


def weights_kernel(pieces, step, place, own, *refs):
    stacks = refs[:8]
    query_weight, gate_weight, out_weight, gain, shift, full_query, full_gate, stage = refs[8:]
    node, shard = place[1], place[2]
    width = out_weight.shape[0]
    span = own.shape[1]
    height = own.shape[0] // 8
    stage[0] = own[...]
    for position in range(8):
        where = pl.multiple_of(lax.bitwise_xor(node, position) * height, 16)
        for d in range(1, pieces):
            stage[d, pl.ds(where, height), :] = stacks[position][d - 1]
    norm_rows = []
    for z in range(pieces):
        where = lax.bitwise_xor(shard, z)
        cols = slice(z * span, (z + 1) * span)
        query_weight[:, cols] = stage[z, 0:width, :]
        gate_weight[:, cols] = stage[z, width : 2 * width, :]
        full_query[:, cols] = stage[where, 0:width, :]
        full_gate[:, cols] = stage[where, width : 2 * width, :]
        out_weight[cols, :] = stage[where, 2 * width : 3 * width, :].T
        norm_rows.append(stage[where, 3 * width : 3 * width + 16, :])
    turned = jnp.concatenate(norm_rows, axis=1).astype(fl_type).T
    gain[...] = jnp.broadcast_to(turned[:, 0:1], gain.shape)
    shift[...] = jnp.broadcast_to(turned[:, 1:2], shift.shape)


def key_weights_kernel(pieces, step, place, *refs):
    mine, other = refs[:pieces], refs[pieces : 2 * pieces]
    full, stage = refs[2 * pieces :]
    core = place[0]
    width, span = full.shape[1], mine[0].shape[1]
    for d in range(pieces):
        stage[d, pl.ds(pl.multiple_of(core * width, 16), width), :] = mine[d][0:width]
        stage[d, pl.ds(pl.multiple_of((1 - core) * width, 16), width), :] = other[d][0:width]
    for z in range(pieces):
        full[:, z * span : (z + 1) * span] = stage[lax.bitwise_xor(place[2], z)]


def query_kernel(step, place, x, weight, query_slope, query):
    sig = jax.nn.sigmoid(dot_nt(weight[...], x[...]))
    query_slope[...] = sig * (1.0 - sig)
    query[...] = sig.astype(bf_type)


def gate_kernel(step, place, x, weight, gate):
    rows = x.shape[0]
    valid = valid_row(place[3], step * rows, rows)
    gate[...] = jnp.where(valid, dot_nt(weight[...], x[...]), 0.0)


def grad_prod_kernel(step, place, g, out_weight, grad_prod):
    rows = g.shape[0]
    valid = valid_row(place[3], step * rows, rows)
    grad_prod[...] = jnp.where(valid, dot_nt(out_weight[...], g[...]), 0.0)


def place_chunks(chunk_refs, place, stage):
    node = place[1]
    for d in range(CHUNKS):
        stage[lax.bitwise_xor(node, d)] = chunk_refs[d][...]


def pair_rows(h, value):
    lane_head = lax.broadcasted_iota(jnp.int32, (1, value.shape[1]), 1) // (value.shape[1] // 2)
    return jnp.where(lane_head == h, value, jnp.zeros_like(value))


def pair_block(chunk, p, head):
    mine = chunk[:head, p * 2 * head : (p + 1) * 2 * head]
    return jnp.concatenate([pair_rows(0, mine), pair_rows(1, mine)], axis=0)


def head_rows(width, h, value):
    lane_head = lax.broadcasted_iota(jnp.int32, (1, width), 1) // (width // 4)
    return jnp.where(lane_head == h, value, jnp.zeros_like(value))


def middle_kernel(steps, lanes, step, place, ids, query, gate, grad_prod, gain, shift, *refs):
    chunk_refs = refs[:CHUNKS]
    prod_out, dgate_out, dnum_out, dden_out, keep, send = refs[CHUNKS : CHUNKS + 6]
    rest = refs[CHUNKS + 6 :]
    width, rows = query.shape
    parts = rows // lanes
    stage, left, acc, dgain, dshift = rest[:5]
    stacks, back_stacks, nums, normeds, dnormeds, dens, ddens = (
        rest[5 + i * parts : 5 + (i + 1) * parts] for i in range(7)
    )
    node, count = place[1], place[3]
    half = width // GROUPS
    head = half // 4

    @pl.when(step == 0)
    def _():
        place_chunks(chunk_refs, place, stage)
        for g in range(GROUPS):
            for c in range(CLUSTERS):
                chunk = stage[g * CLUSTERS + c].astype(fl_type)
                cols = slice(c * 2 * head, (c + 1) * 2 * head)
                for p in range(2):
                    mine = chunk[:, p * 2 * head : (p + 1) * 2 * head]
                    for h in range(2):
                        at = slice(h * head, (h + 1) * head)
                        left[g * 2 + p, at, cols] = pair_rows(h, mine[:head]).astype(bf_type)
                    sums = [pair_rows(h, mine[head : head + 1]) for h in range(2)]
                    sums.append(jnp.zeros((PAD - 2, 2 * head), fl_type))
                    left[g * 2 + p, 2 * head :, cols] = jnp.concatenate(sums, axis=0).astype(bf_type)
        acc[...] = jnp.zeros_like(acc)
        dgain[...] = jnp.zeros_like(dgain)
        dshift[...] = jnp.zeros_like(dshift)

    def forward(part):
        cols = slice(part * lanes, (part + 1) * lanes)
        table = members(ids.at[:, cols])
        stack, num, den = stacks[part], nums[part], dens[part]
        for p in range(PAIRS):
            at = slice(p * 2 * head, (p + 1) * 2 * head)
            mine = query[at, cols]
            for c in range(CLUSTERS):
                stack[p, c * 2 * head : (c + 1) * 2 * head, :] = mine * table[c : c + 1, :]
            both = dot_nn(left[p], stack[p])
            num[at, :] = both[: 2 * head]
            row = (p // 2) * 8 + (p % 2) * 2
            den[row : row + 2, :] = 1.0 / both[2 * head : 2 * head + 2]

    def norm(part):
        cols = slice(part * lanes, (part + 1) * lanes)
        num, dnormed, den, dden = nums[part], dnormeds[part], dens[part], ddens[part]
        spans = [slice(h * head, (h + 1) * head) for h in range(HEADS)]
        inverse = [den[(h // 4) * 8 + h % 4 : (h // 4) * 8 + h % 4 + 1, :] for h in range(HEADS)]

        def mean_of(blocks):
            return jnp.sum(tree_sum(blocks), axis=0, keepdims=True) * (1.0 / width)

        mean = mean_of([fold_rows(num[spans[h], :]) * inverse[h] for h in range(HEADS)])
        squares = []
        for h in range(HEADS):
            centered = num[spans[h], :] * inverse[h] - mean
            num[spans[h], :] = centered
            squares.append(fold_rows(centered * centered))
        scale = lax.rsqrt(mean_of(squares) + norm_eps)
        first, second = [], []
        for h in range(HEADS):
            span = spans[h]
            ah = num[span, :] * scale
            num[span, :] = ah
            gamma = jnp.concatenate([gain[span, :]] * (lanes // 128), axis=1)
            beta = jnp.concatenate([shift[span, :]] * (lanes // 128), axis=1)
            u = ah * gamma + beta
            zg = gate[span, cols]
            dp = grad_prod[span, cols]
            prod_out[span, cols] = (u * zg).astype(bf_type)
            du = dp * zg
            dgate_out[span, cols] = (dp * u).astype(bf_type)
            du_ah = du * ah
            dgain[span, :] += fold_lanes(du_ah)
            dshift[span, :] += fold_lanes(du)
            dah = gamma * du
            first.append(fold_rows(dah))
            second.append(fold_rows(gamma * du_ah))
            dnormed[span, :] = dah
        first = mean_of(first)
        second = mean_of(second)
        shifted = mean * scale
        for h in range(HEADS):
            span = spans[h]
            ah = num[span, :]
            rest = dnormed[span, :] - ah * second - first
            dnum_out[span, cols] = (rest * (scale * inverse[h])).astype(bf_type)
            inner = fold_rows(rest * ah) + shifted * fold_rows(rest)
            row = (h // 4) * 8 + h % 4
            dden[row : row + 1, :] = -jnp.sum(inner, axis=0, keepdims=True) * inverse[h]
        dden_out[:, cols] = dden[...]

    def backward(part):
        cols = slice(part * lanes, (part + 1) * lanes)
        table = members(ids.at[:, cols])
        stack, dden = back_stacks[part], ddens[part]
        for g in range(GROUPS):
            mine = dnum_out[g * half : (g + 1) * half, cols]
            for c in range(CLUSTERS):
                stack[g, c * half : (c + 1) * half, :] = mine * table[c : c + 1, :]
            den_rows = dden[g * 8 : g * 8 + 4, :]
            high = den_rows.astype(bf_type)
            low = (den_rows - high.astype(fl_type)).astype(bf_type)
            four_high = jnp.concatenate([high * table[c : c + 1, :] for c in range(CLUSTERS)], axis=0)
            four_low = jnp.concatenate([low * table[c : c + 1, :] for c in range(CLUSTERS)], axis=0)
            stack[g, CLUSTERS * half :, :] = jnp.concatenate([four_high, four_low], axis=0)
            acc[g] += dot_nt(stack[g], query[g * half : (g + 1) * half, cols])

    for part in range(parts):
        forward(part)
    for part in range(parts):
        norm(part)
        backward(part)

    @pl.when(step == steps - 1)
    def _():
        gain_row = jnp.sum(dgain[...].T, axis=0, keepdims=True)
        shift_row = jnp.sum(dshift[...].T, axis=0, keepdims=True)

        def extra(g, c):
            base = CLUSTERS * half
            row = jnp.zeros((1, half), fl_type)
            for h in range(4):
                at = base + c * 4 + h
                row = row + head_rows(half, h, acc[g, at : at + 1, :] + acc[g, at + 16 : at + 17, :])
            cols = slice(g * half, (g + 1) * half)
            tail = [row]
            if c == 0:
                tail += [gain_row[:, cols], shift_row[:, cols]]
            tail.append(jnp.zeros((PAD - len(tail), half), fl_type))
            return jnp.concatenate(tail, axis=0)

        put_chunks(acc, keep, send, node, extra)


def fold_rows(block):
    return tree_sum([block[i * 8 : (i + 1) * 8] for i in range(block.shape[0] // 8)])


def fold_lanes(block):
    return tree_sum([block[:, i * 128 : (i + 1) * 128] for i in range(block.shape[1] // 128)])


def write_pieces(pieces, node, shard, span, keep, send, blocks):
    for chunk in range(8):
        distance = lax.bitwise_xor(node, chunk)
        slot = lax.shift_right_logical(distance, 1)
        even = lax.bitwise_and(distance, 1) == 0
        for z in range(pieces):
            block = blocks(z, chunk)

            @pl.when(even)
            def _():
                keep[slot, z] = block

            @pl.when(jnp.logical_not(even))
            def _():
                send[slot, z] = block.astype(bf_type)


def query_back_kernel(step, place, ids, dnum, dden, query_slope, *refs):
    chunk_refs = refs[:CHUNKS]
    dquery_out = refs[CHUNKS]
    stage, left, sums, stack = refs[CHUNKS + 1 :]
    width, rows = dnum.shape
    half = width // GROUPS
    head = half // 4

    @pl.when(step == 0)
    def _():
        place_chunks(chunk_refs, place, stage)
        for gr in range(GROUPS):
            for c in range(CLUSTERS):
                chunk = stage[gr * CLUSTERS + c].astype(fl_type)
                for p in range(2):
                    cols = slice(c * 2 * head, (c + 1) * 2 * head)
                    left[gr * 2 + p, :, cols] = pair_block(chunk, p, head).T.astype(bf_type)
                column = chunk[head : head + 8].T
                sums[c, gr * half : (gr + 1) * half, :] = jnp.broadcast_to(column[:, 0:1], (half, 128))

    table = members(ids)
    for p in range(PAIRS):
        part = dnum[p * 2 * head : (p + 1) * 2 * head, :]
        for c in range(CLUSTERS):
            stack[p, c * 2 * head : (c + 1) * 2 * head, :] = part * table[c : c + 1, :]
        dq = dot_nn(left[p], stack[p])
        for h in range(2):
            at = slice((p * 2 + h) * head, (p * 2 + h + 1) * head)
            pick = pick_rows(sums, at, ids, rows)
            row = (p // 2) * 8 + (p % 2) * 2 + h
            full = dq[h * head : (h + 1) * head] + dden[row : row + 1, :] * pick
            dquery_out[at, :] = (full * query_slope[at, :]).astype(bf_type)


def grad_query_kernel(step, place, dquery, x, grad_query):
    @pl.when(step == 0)
    def _():
        grad_query[...] = jnp.zeros_like(grad_query)

    grad_query[...] += dot_nn(dquery[...], x[...])


def gate_back_kernel(step, place, dgate, prod, x, g, grad_gate, grad_out):
    @pl.when(step == 0)
    def _():
        grad_gate[...] = jnp.zeros_like(grad_gate)
        grad_out[...] = jnp.zeros_like(grad_out)

    grad_gate[...] += dot_nn(dgate[...], x[...])
    grad_out[...] += dot_nn(prod[...], g[...])


def early_kernel(pieces, step, place, grad_query, grad_gate, grad_out, keep, send):
    node, shard = place[1], place[2]
    width = grad_out.shape[1]
    span = width // pieces
    tall = 2 * width // 8
    lanes = width // 4
    short = span // 2

    def blocks(z, chunk):
        source = grad_query if chunk < 4 else grad_gate
        top = source[(chunk % 4) * tall : (chunk % 4 + 1) * tall, z * span : (z + 1) * span]
        start = pl.multiple_of(lax.bitwise_xor(shard, z) * span + (chunk % 2) * short, 8)
        bottom = grad_out[pl.ds(start, short), (chunk // 2) * lanes : (chunk // 2 + 1) * lanes]
        return jnp.concatenate([top, fold(bottom, span)], axis=0)

    write_pieces(pieces, node, shard, span, keep, send, blocks)


def fold(block, span):
    return jnp.concatenate(
        [block[:, i * span : (i + 1) * span] for i in range(block.shape[1] // span)], axis=0
    )


def pick_rows(sums, at, ids, rows):
    reps = rows // 128
    wide = [jnp.concatenate([sums[c, at, :]] * reps, axis=1) for c in range(CLUSTERS)]
    pick = wide[CLUSTERS - 1]
    for c in range(CLUSTERS - 1):
        pick = jnp.where(ids[...] == c, wide[c], pick)
    return pick


def output_kernel(step, place, x, prod, out_weight, result):
    result[...] = x[...].astype(fl_type) + dot_tn(prod[...], out_weight[...])


def key_back_kernel(pieces, step, place, ids, key_slope, key, value, x, *refs):
    chunk_refs = refs[:CHUNKS]
    dkey_out, dvalue_out, norm_out, keep, send = refs[CHUNKS : CHUNKS + 5]
    stage, left_key, left_value, sums, stack, key_stack, acc = refs[CHUNKS + 5 :]
    node, shard, count = place[1], place[2], place[3]
    width, rows = value.shape
    half = width // GROUPS
    head = half // 4
    span = width // pieces

    @pl.when(step == 0)
    def _():
        place_chunks(chunk_refs, place, stage)
        for gr in range(GROUPS):
            for c in range(CLUSTERS):
                chunk = stage[gr * CLUSTERS + c].astype(fl_type)
                for p in range(2):
                    cols = slice(c * 2 * head, (c + 1) * 2 * head)
                    pair = pair_block(chunk, p, head)
                    left_value[gr * 2 + p, :, cols] = pair.astype(bf_type)
                    left_key[gr * 2 + p, :, cols] = pair.T.astype(bf_type)
                column = chunk[head : head + 8].T
                sums[c, gr * half : (gr + 1) * half, :] = jnp.broadcast_to(column[:, 0:1], (half, 128))
                if c == 0:
                    norm_out[:, gr * half : (gr + 1) * half] = chunk[head : head + 8]

    table = members(ids)
    valid = valid_row(count, step * rows, rows)
    for p in range(PAIRS):
        at = slice(p * 2 * head, (p + 1) * 2 * head)
        part = value[at, :]
        for c in range(CLUSTERS):
            stack[p % 2, c * 2 * head : (c + 1) * 2 * head, :] = part * table[c : c + 1, :]
        dk = dot_nn(left_key[p], stack[p % 2])
        for h in range(2):
            sub = slice((p * 2 + h) * head, (p * 2 + h + 1) * head)
            full = dk[h * head : (h + 1) * head] + pick_rows(sums, sub, ids, rows)
            dkey_out[sub, :] = (full * key_slope[sub, :]).astype(bf_type)
        part = key[at, :]
        for c in range(CLUSTERS):
            key_stack[p % 2, c * 2 * head : (c + 1) * 2 * head, :] = part * table[c : c + 1, :]
        dvalue_out[at, :] = dot_nn(left_value[p], key_stack[p % 2]).astype(bf_type)
    acc[0:width] = dot_nn(dkey_out[...], x[...])
    acc[width : 2 * width] = dot_nn(dvalue_out[...], x[...])

    tall = 2 * width // 8

    def blocks(z, chunk):
        return acc[chunk * tall : (chunk + 1) * tall, z * span : (z + 1) * span]

    write_pieces(pieces, node, shard, span, keep, send, blocks)


def input_kernel(step, place, dquery, dkey, dvalue, dgate, full_query, full_key, full_gate, g, result):
    width = g.shape[1]
    total = g[...].astype(fl_type)
    total = total + dot_tn(dquery[...], full_query[...])
    total = total + dot_tn(dkey[...], full_key[0:width, :])
    total = total + dot_tn(dvalue[...], full_key[width:, :])
    total = total + dot_tn(dgate[...], full_gate[...])
    result[...] = total


def finish_kernel(step, *refs):
    parts, sums = refs[:-1], refs[-1]
    sums[...] = tree_sum([p[...].astype(fl_type) for p in parts]).astype(bf_type)


def squares_kernel(step, *refs):
    parts, squares = refs[:-1], refs[-1]
    totals = []
    for part in parts:
        value = part[...].astype(fl_type)
        totals.append(fold_rows(value * value))
    total = jnp.sum(tree_sum(totals), axis=0, keepdims=True)
    squares[...] = jnp.broadcast_to(jnp.sum(total, axis=1, keepdims=True), squares.shape)


def assemble_kernel(step, place, *refs):
    parts, (grad_proj, grad_out, stage) = refs[:CHUNKS], refs[CHUNKS:]
    node = place[1]
    span, width = grad_out.shape
    tall = 2 * width // 8
    lanes = width // 4
    rows = span // 2
    folds = lanes // span
    for d in range(CHUNKS):
        chunk = lax.bitwise_xor(node, d)
        stage[chunk] = parts[d][...].astype(fl_type)
    for chunk in range(CHUNKS):
        query_at = (0 if chunk < 4 else 3 * width) + (chunk % 4) * tall
        grad_proj[:, width + chunk * tall : width + (chunk + 1) * tall] = stage[chunk, 0:tall].T
        grad_proj[:, query_at : query_at + tall] = stage[chunk, tall : 2 * tall].T
        for i in range(folds):
            at = slice((chunk // 2) * lanes + i * span, (chunk // 2) * lanes + (i + 1) * span)
            block = stage[chunk, 2 * tall + i * rows : 2 * tall + (i + 1) * rows]
            grad_out[(chunk % 2) * rows : (chunk % 2 + 1) * rows, at] = block


def adam(master_w, moment_old, square_old, clipped, decay_coef, step_rate):
    moment_new = beta_one * moment_old + (1.0 - beta_one) * clipped
    square_new = beta_two * square_old + (1.0 - beta_two) * clipped * clipped
    moment_hat = moment_new * (1.0 / (1.0 - beta_one**STEP))
    square_hat = square_new * (1.0 / (1.0 - beta_two**STEP))
    master_new = master_w * (1.0 - step_rate * decay_coef) - step_rate * moment_hat / (
        jnp.sqrt(square_hat) + adam_eps
    )
    return moment_new, square_new, master_new


def update_kernel(pieces, step, place, *refs):
    squares, (gp, go, gn, pw, pm, ps, ow, om, osq, nw, nm, ns) = refs[:pieces], refs[pieces : pieces + 12]
    size, *results = refs[pieces + 12 : pieces + 25]
    p_out, o_out, n_out = results[0:4], results[4:8], results[8:12]
    new_p, new_pc, new_o, new_oc, new_n, sems = refs[pieces + 25 :]
    shard = place[2]
    span, width = ow.shape
    norm_grad = gn[1:3, :]
    norm_square = jnp.sum(norm_grad * norm_grad, axis=0, keepdims=True)
    total = tree_sum([q[0:1, 0:1] for q in squares]) + jnp.sum(norm_square, axis=1, keepdims=True)
    norm = jnp.sqrt(total)
    size[...] = norm
    clip_level = 0.5 * math.sqrt(5 * width * width + 2 * width)
    scale = jnp.minimum(1.0, clip_level / norm)
    copies = []

    def send(source, target):
        copies.append(pltpu.make_async_copy(source, target, sems.at[len(copies)]))
        copies[-1].start()

    scale = jnp.broadcast_to(scale, (1, width))

    def step_block(at, cols, w, m, s, grad, new, new_copy):
        results = adam(w[at, cols], m[at, cols], s[at, cols], grad[at, cols] * scale, decay_rate, learn_rate)
        for j, value in zip((2, 0, 1), (results[2], *results[:2])):
            new[j, at, :] = value
        new_copy[at, :] = results[2].astype(bf_type)

    blocks = [slice(r, r + 16) for r in range(0, span, 16)]
    for i in range(4):
        cols = slice(i * width, (i + 1) * width)
        for at in blocks:
            step_block(at, cols, pw, pm, ps, gp, new_p.at[:, i], new_pc.at[i])
        for j in range(3):
            send(new_p.at[j, i], p_out[j].at[:, cols])
        send(new_pc.at[i], p_out[3].at[:, cols])
    for at in blocks:
        step_block(at, slice(0, width), ow, om, osq, go, new_o, new_oc)
    for j in range(3):
        send(new_o.at[j], o_out[j])
    send(new_oc, o_out[3])
    mine = norm_grad[:, 0:span]
    for z in range(1, pieces):
        mine = jnp.where(shard == z, norm_grad[:, z * span : (z + 1) * span], mine)
    clipped = mine * scale[:, 0:span]
    for j, value in enumerate((clipped, *adam(nw[...], nm[...], ns[...], clipped, 0.0, norm_rate))):
        new_n[j] = value
        send(new_n.at[j], n_out[j])
    for copy in copies:
        copy.wait()


def make_exchange(nodes, shards):
    count = nodes * shards

    def exchange(value, node_bits, shard_bits):
        pairs = [
            (i, ((i // shards) ^ node_bits) * shards + ((i % shards) ^ shard_bits)) for i in range(count)
        ]
        return lax.ppermute(value, AXES, pairs)

    return exchange


def tree_sum(parts):
    parts = list(parts)
    while len(parts) > 1:
        pairs = [parts[i] + parts[i + 1] for i in range(0, len(parts) - 1, 2)]
        parts = pairs + parts[len(parts) - len(parts) % 2 :]
    return parts[0]


def to_float(parts):
    return [p.astype(fl_type) for p in parts]


def tie(value, *others):
    return lax.optimization_barrier((value, *others))[0]


def tie(value, *others):
    return lax.optimization_barrier((value, *others))[0]


def local(nodes, shards, *args):
    (x, g, ids, counts, pw, pm, ps, ow, om, osq, nw, nm, ns) = args
    exchange = make_exchange(nodes, shards)
    outer = nodes // 8
    rows, width = x.shape
    half = width // GROUPS
    head = width // HEADS
    span = pw.shape[0]
    block = min(1024, rows)
    steps = rows // block
    lanes = 256
    tall = 2 * width // 8
    part_rows = (3 * width + 2 + 127) // 128 * 16
    work = 2 * rows * width * width

    node = lax.axis_index("nodes").astype(jnp.int32)
    shard = lax.axis_index("shard").astype(jnp.int32)
    place = jnp.stack([lax.bitwise_and(node, 1), lax.bitwise_and(node, 7), shard, counts[0]])
    ids = ids.reshape(1, rows)
    chunk_shape = (4, head + PAD, half)

    def wide(dtype):
        return out((width, rows), dtype)

    def vmem(shape, dtype):
        return pltpu.VMEM(shape, dtype)

    message, kv_half, part, query_all = call(
        prep_kernel,
        1,
        (pw, ow, nw),
        ["hbm"] * 3,
        [
            out((width, span), bf_type),
            out((width, span), bf_type),
            out((part_rows, span), bf_type),
            out((8 * part_rows, span), bf_type),
        ],
        [None] * 4,
        [
            vmem((5, span, width), fl_type),
            vmem((2, span), fl_type),
            vmem((2, width, span), bf_type),
            pltpu.SemaphoreType.DMA((6,)),
        ],
        1e6,
        "prep",
        vmem=60,
    )
    x_turned = jnp.concatenate(
        [
            lax.dynamic_slice(x, (0, lax.bitwise_xor(shard, z) * span), (rows, span))
            for z in range(shards)
        ],
        axis=1,
    )
    mine, other = [message], [kv_half]
    for z in range(1, shards):
        late = z == 2
        mine.append(exchange(tie(message, x_turned) if late else message, 0, z))
    stack = jnp.stack([exchange(part, 0, z) for z in range(1, shards)])
    stacks = [stack] + [None] * 7
    for e in range(1, 4):
        stacks[2 * e] = exchange(stack, 2 * e, 0)
    for z in range(1, shards):
        other.append(exchange(tie(mine[z], stack), 1, 0))
    key_slope, key, value, keep, send = call(
        functools.partial(key_kernel, shards),
        1,
        (place, x_turned, ids, *mine, *other),
        ["smem", "row", "lane"] + [None] * (2 * shards),
        [wide(fl_type), wide(bf_type), wide(bf_type), out(chunk_shape, fl_type), out(chunk_shape, bf_type)],
        ["lane", "lane", "lane", None, None],
        [
            vmem((2 * width, width), bf_type),
            vmem((CLUSTERS * half + PAD, rows), bf_type),
            vmem((GROUPS, CLUSTERS * half + PAD, half), fl_type),
        ],
        1e3,
        "keys",
        rows,
        vmem=26,
    )

    def swap(pieces, peers, filler, cast=True):
        got = [exchange(p, *at) for p, at in zip(pieces, peers)]
        if filler is not None:
            done = filler(pieces[0])
            got = list(tie(tuple(got), done))
        return to_float(got) if cast else got

    plane = [(2 * e, 0) for e in range(1, 4)]
    along = [(0, z) for z in range(1, shards)]
    made = {}

    def reduce_chunks(keep, send, fillers):
        mine = keep + exchange(send, 1, 0).astype(fl_type)
        got = swap([mine[e].astype(bf_type) for e in range(1, 4)], plane, fillers[0])
        own = tree_sum([mine[0], *got]).astype(bf_type)
        got = swap([own] * (shards - 1), along, fillers[1])
        own = tree_sum([own.astype(fl_type), *got]).astype(bf_type)
        if outer > 1:
            got = swap([own] * (outer - 1), [(8 * o, 0) for o in range(1, outer)], None)
            own = tree_sum([own.astype(fl_type), *got]).astype(bf_type)
        return spread(own, fillers[2])

    def spread(own, filler=None):
        chunks = [own] + [None] * 7
        for e in range(1, 4):
            chunks[2 * e] = exchange(own, 2 * e, 0)
        chunks[1] = exchange(own, 1, 0)
        if filler is not None:
            done = filler(own)
            chunks[2], chunks[4], chunks[6] = tie((chunks[2], chunks[4], chunks[6]), done)
        for e in range(1, 4):
            chunks[2 * e + 1] = exchange(chunks[2 * e], 1, 0)
        return chunks

    def fill_weights(dep):
        made["weights"] = call(
            functools.partial(weights_kernel, shards),
            1,
            (tie(place, dep), query_all, *stacks),
            ["smem", None] + [None] * 8,
            [
                out((width, width), bf_type),
                out((width, width), bf_type),
                out((width, width), bf_type),
                out((width, 128), fl_type),
                out((width, 128), fl_type),
                out((width, width), bf_type),
                out((width, width), bf_type),
            ],
            [None] * 7,
            [vmem((shards, 8 * part_rows, span), bf_type)],
            1e6,
            "weights",
        )
        return made["weights"][0]

    def fill_query(dep):
        made["query"] = call(
            query_kernel,
            1,
            (tie(place, dep), x_turned, made["weights"][0]),
            ["smem", "row", None],
            [wide(fl_type), wide(bf_type)],
            ["lane"] * 2,
            [],
            work,
            "query",
            rows,
            vmem=16,
        )
        return made["query"][1], fill_gate(dep)

    def fill_gate(dep):
        gate_weight = made["weights"][1]
        made["gate"] = call(
            gate_kernel,
            1,
            (tie(place, dep), x_turned, gate_weight),
            ["smem", "row", None],
            [wide(fl_type)],
            ["lane"],
            [],
            work,
            "gate",
            rows,
            vmem=16,
        )[0]
        return made["gate"]

    def fill_grad_prod(dep):
        out_weight = made["weights"][2]
        made["grad_prod"] = call(
            grad_prod_kernel,
            1,
            (tie(place, dep), g, out_weight),
            ["smem", "row", None],
            [wide(fl_type)],
            ["lane"],
            [],
            work,
            "grad_prod",
            rows,
            vmem=16,
        )[0]
        return made["grad_prod"]

    send = tie(send, *stacks[2::2])
    for e in range(4):
        stacks[2 * e + 1] = exchange(stacks[2 * e], 1, 0)
    chunks = reduce_chunks(keep, send, (fill_weights, fill_query, fill_grad_prod))
    out_weight, gain, shift, full_query, full_gate = made["weights"][2:]
    query_slope, query = made["query"]

    parts = block // lanes
    prod, dgate, dnum, dden, keep, send = call(
        functools.partial(middle_kernel, steps, lanes),
        steps,
        (place, ids, query, made["gate"], made["grad_prod"], gain, shift, *chunks),
        ["smem", "lane", "lane", "lane", "lane", None, None] + [None] * CHUNKS,
        [
            wide(bf_type),
            wide(bf_type),
            wide(bf_type),
            out((16, rows), fl_type),
            out(chunk_shape, fl_type),
            out(chunk_shape, bf_type),
        ],
        ["lane", "lane", "lane", "lane", None, None],
        [
            vmem((CHUNKS, head + PAD, half), bf_type),
            vmem((PAIRS, 2 * head + PAD, CLUSTERS * 2 * head), bf_type),
            vmem((GROUPS, CLUSTERS * half + 32, half), fl_type),
            vmem((width, 128), fl_type),
            vmem((width, 128), fl_type),
        ]
        + [vmem((PAIRS, CLUSTERS * 2 * head, lanes), bf_type)] * parts
        + [vmem((GROUPS, CLUSTERS * half + 32, lanes), bf_type)] * parts
        + [vmem((width, lanes), fl_type)] * (3 * parts)
        + [vmem((16, lanes), fl_type)] * (2 * parts),
        6 * work,
        "middle",
        block,
    )

    short = tall + (span // 2) * (width // 4 // span)
    height = tall + short
    early_shape = (4, shards, short, span)
    late_shape = (4, shards, tall, span)

    def fill_gate_back(dep):
        made["gate_back"] = call(
            gate_back_kernel,
            1,
            (tie(place, dep), dgate, prod, x_turned, g),
            ["smem", "lane", "lane", "row", "row"],
            [out((width, width), fl_type)] * 2,
            [None] * 2,
            [],
            2 * work,
            "gate_back",
            rows,
            vmem=16,
        )
        return made["gate_back"][0]

    def fill_output(dep):
        made["output"] = call(
            output_kernel,
            steps,
            (tie(place, dep), x, prod, out_weight),
            ["smem", "row", "lane", None],
            [out((rows, width), fl_type)],
            ["row"],
            [],
            work,
            "output",
            block,
            piped=True,
        )[0]
        return made["output"]

    def fill_query_back(dep):
        made["dquery"] = call(
            query_back_kernel,
            1,
            (tie(place, dep), ids, dnum, dden, query_slope, *chunks),
            ["smem", "lane", "lane", "lane", "lane"] + [None] * CHUNKS,
            [wide(bf_type)],
            ["lane"],
            [
                vmem((CHUNKS, head + PAD, half), bf_type),
                vmem((PAIRS, 2 * head, CLUSTERS * 2 * head), bf_type),
                vmem((CLUSTERS, width, 128), fl_type),
                vmem((PAIRS, CLUSTERS * 2 * head, rows), bf_type),
            ],
            2 * work,
            "query_back",
            rows,
            vmem=26,
        )[0]
        return made["dquery"]

    def fill_grad_query(dep):
        made["grad_query"] = call(
            grad_query_kernel,
            1,
            (tie(place, dep), made["dquery"], x_turned),
            ["smem", None, None],
            [out((width, width), fl_type)],
            [None],
            [],
            work,
            "grad_query",
            vmem=12,
        )[0]
        made["early"] = call(
            functools.partial(early_kernel, shards),
            1,
            (place, made["grad_query"], *made["gate_back"]),
            ["smem"] + [None] * 3,
            [out(early_shape, fl_type), out(early_shape, bf_type)],
            [None] * 2,
            [],
            1e6,
            "early",
            vmem=8,
        )
        return made["early"][1]

    back_chunks = reduce_chunks(keep, send, (fill_gate_back, fill_query_back, fill_grad_query))
    dquery = made["dquery"]

    early_keep, early_send = made["early"]
    early_send = tie(early_send, *back_chunks[2::2])
    early_mine = early_keep + exchange(early_send, 1, 0).astype(fl_type)
    early_pieces = tie(tuple(early_mine[e].astype(bf_type) for e in range(1, 4)))
    early_got = [exchange(p, *at) for p, at in zip(early_pieces, plane)]
    dkey, dvalue, norm_grad, keep, send = call(
        functools.partial(key_back_kernel, shards),
        1,
        (place, ids, key_slope, key, value, x_turned, *back_chunks),
        ["smem", "lane", "lane", "lane", "lane", "row"] + [None] * CHUNKS,
        [
            wide(bf_type),
            wide(bf_type),
            out((8, width), fl_type),
            out(late_shape, fl_type),
            out(late_shape, bf_type),
        ],
        ["lane", "lane", None, None, None],
        [
            vmem((CHUNKS, head + PAD, half), bf_type),
            vmem((PAIRS, 2 * head, CLUSTERS * 2 * head), bf_type),
            vmem((PAIRS, 2 * head, CLUSTERS * 2 * head), bf_type),
            vmem((CLUSTERS, width, 128), fl_type),
            vmem((2, CLUSTERS * 2 * head, rows), bf_type),
            vmem((2, CLUSTERS * 2 * head, rows), bf_type),
            vmem((2 * width, width), fl_type),
        ],
        6 * work,
        "key_back",
        rows,
        vmem=26,
    )

    full_key = call(
        functools.partial(key_weights_kernel, shards),
        1,
        (place, *mine, *other),
        ["smem"] + [None] * (2 * shards),
        [out((2 * width, width), bf_type)],
        [None],
        [vmem((shards, 2 * width, span), bf_type)],
        1e6,
        "key_weights",
        vmem=12,
    )[0]

    def fill_inputs(dep):
        made["inputs"] = call(
            input_kernel,
            steps,
            (tie(place, dep), dquery, dkey, dvalue, dgate, full_query, full_key, full_gate, g),
            ["smem"] + ["lane"] * 4 + [None] * 3 + ["row"],
            [out((rows, width), fl_type)],
            ["row"],
            [],
            4 * work,
            "inputs",
            block,
            piped=True,
        )[0]
        return made["inputs"]

    send = tie(send, *early_got)
    mine_sum = keep + exchange(send, 1, 0).astype(fl_type)
    early_sum = tree_sum([early_mine[0], *to_float(early_got)])
    got = swap([mine_sum[e].astype(bf_type) for e in range(1, 4)], plane, fill_inputs)
    mine_sum = jnp.concatenate([tree_sum([mine_sum[0], *got]), early_sum], axis=1)
    pieces = tie(tuple(mine_sum[z].astype(bf_type) for z in range(1, shards)))
    owned_parts = [mine_sum[0], *swap(pieces, along, fill_output, cast=False)]
    if outer > 1:
        own = tree_sum(to_float(owned_parts)).astype(bf_type)
        got = [own] + [exchange(own, 8 * o, 0) for o in range(1, outer)]
        owned_parts = [tree_sum(to_float(got))] + [jnp.zeros_like(own)] * (shards - 1)

    sums = call(
        finish_kernel,
        1,
        owned_parts,
        [None] * shards,
        [out((height, span), bf_type)],
        [None],
        [],
        1e6,
        "finish",
        vmem=4,
    )[0]
    parts = spread(sums)
    squares = call(
        squares_kernel,
        1,
        parts,
        [None] * CHUNKS,
        [out((8, 128), fl_type)],
        [None],
        [],
        1e6,
        "squares",
        vmem=4,
    )[0]

    def fill_assemble(dep):
        made["grads"] = call(
            assemble_kernel,
            1,
            (tie(place, dep), *parts),
            ["smem"] + [None] * CHUNKS,
            [out((span, 4 * width), fl_type), out((span, width), fl_type)],
            [None] * 2,
            [vmem((CHUNKS, height, span), fl_type)],
            1e6,
            "assemble",
            vmem=8,
        )
        return made["grads"][0]

    squares = [squares, *swap([squares] * (shards - 1), along, fill_assemble)]
    states = (pw, pm, ps, ow, om, osq, nw, nm, ns)
    like = [pw] * 4 + [ow] * 4 + [nw] * 4
    kinds = [fl_type] * 3 + [bf_type] + [fl_type] * 3 + [bf_type] + [fl_type] * 4
    grad_size, *new = call(
        functools.partial(update_kernel, shards),
        1,
        (place, *squares, *made["grads"], norm_grad, *states),
        ["smem"] + [None] * (shards + 12),
        [out((1, 1), fl_type)] + [out(s.shape, k) for s, k in zip(like, kinds)],
        [None] + ["hbm"] * 12,
        [
            vmem((3, 4, span, width), fl_type),
            vmem((4, span, width), bf_type),
            vmem((3, span, width), fl_type),
            vmem((span, width), bf_type),
            vmem((4, 2, span), fl_type),
            pltpu.SemaphoreType.DMA((24,)),
        ],
        1e6,
        "update",
    )
    return (made["output"], made["inputs"], grad_size.reshape(1), *new)


def solution(mesh):
    nodes, shards = mesh.shape["nodes"], mesh.shape["shard"]
    by_node = P(AXES, None)
    rows = P("shard", None)
    cols = P(None, "shard")
    return jax.shard_map(
        functools.partial(local, nodes, shards),
        mesh=mesh,
        in_specs=(by_node, by_node, P(AXES), P(AXES)) + (rows,) * 6 + (cols,) * 3,
        out_specs=(by_node, by_node, P()) + (rows,) * 8 + (cols,) * 4,
        check_vma=False,
    )
```

```python
import functools
import math

import jax
import jax.numpy as jnp
from jax import lax
from jax.experimental import pallas as pl
from jax.experimental.pallas import tpu as pltpu
from jax.sharding import PartitionSpec as P

HEADS = 8
CLUSTERS = 4
STEP = 10
AXES = ("nodes", "shard")

norm_eps = 1e-05
beta_one = 0.9
beta_two = 0.999
learn_rate = 0.05
norm_rate = 0.5
decay_rate = 0.01
adam_eps = 1e-08
bf_type = jnp.bfloat16
fl_type = jnp.float32

GROUPS = 2
PAIRS = HEADS // 2
CHUNKS = GROUPS * CLUSTERS
PAD = 16


def dot_nn(a, b):
    return lax.dot_general(a, b, (((1,), (0,)), ((), ())), preferred_element_type=fl_type)


def dot_nt(a, b):
    return lax.dot_general(a, b, (((1,), (1,)), ((), ())), preferred_element_type=fl_type)


def dot_tn(a, b):
    return lax.dot_general(a, b, (((0,), (0,)), ((), ())), preferred_element_type=fl_type)


def whole(shape):
    return pl.BlockSpec(shape, lambda *_: (0,) * len(shape))


def smem():
    return pl.BlockSpec(memory_space=pltpu.SMEM)


def view(ref, kind, start, size):
    if kind == "lane":
        return ref.at[:, pl.ds(start, size)]
    if kind == "row":
        return ref.at[pl.ds(start, size), :]
    return ref


def call(kernel, steps, ins, in_kinds, outs, out_kinds, scratch, flops, name, block=0, vmem=16, piped=False):
    moved = sum(math.prod(a.shape) * a.dtype.itemsize for a in (*ins, *outs))
    arrays, kinds = [*ins, *outs], [*in_kinds, *out_kinds]

    def spec(array, kind):
        if kind == "smem":
            return smem()
        if kind == "hbm":
            return pl.BlockSpec(memory_space=pltpu.HBM)
        if isinstance(kind, pl.BlockSpec):
            return kind
        if piped and kind == "lane":
            return pl.BlockSpec((array.shape[0], block), lambda i: (0, i))
        if piped and kind == "row":
            return pl.BlockSpec((block, array.shape[1]), lambda i: (i, 0))
        return whole(array.shape)

    def body(*refs):
        if piped:
            kernel(pl.program_id(0), *refs)
            return
        if steps == 1:
            kernel(0, *refs)
            return

        def one(i, carry):
            start = pl.multiple_of(i * block, block)
            views = [view(r, k, start, block) for r, k in zip(refs, kinds)]
            kernel(i, *views, *refs[len(kinds) :])
            return carry

        lax.fori_loop(0, steps, one, 0)

    specs = [spec(a, k) for a, k in zip(arrays, kinds)]
    return pl.pallas_call(
        body,
        grid=(steps,) if piped else (),
        in_specs=specs[: len(ins)],
        out_specs=specs[len(ins) :],
        out_shape=outs,
        scratch_shapes=scratch,
        cost_estimate=pl.CostEstimate(flops=int(flops), transcendentals=0, bytes_accessed=int(moved)),
        compiler_params=pltpu.CompilerParams(vmem_limit_bytes=vmem * 1024 * 1024),
        name=name,
    )(*ins)


def out(shape, dtype):
    return jax.ShapeDtypeStruct(shape, dtype)


def fetch(copies):
    copies = [pltpu.make_async_copy(*c) for c in copies]
    for c in copies:
        c.start()
    return copies


def prep_kernel(step, wp, wo, wn, key_message, key_other, message, query_all, block, rows, stage, sems):
    core = lax.bitwise_and(lax.axis_index("nodes"), 1)
    part = lax.bitwise_and(lax.axis_index("nodes"), 7)
    shard, width = wo.shape
    columns = [wp.at[:, i * width : (i + 1) * width] for i in (1, 2, 0, 3)]
    sources = [*columns, wo]
    copies = fetch(
        [(sources[i], block.at[i], sems.at[i]) for i in range(5)] + [(wn, rows, sems.at[5])]
    )
    for i in range(2):
        copies[i].wait()
        stage[i] = block[i].T.astype(bf_type)
    key_message[...] = stage[core]
    key_other[...] = stage[1 - core]
    for i in range(3):
        copies[2 + i].wait()
        query_all[i * width : (i + 1) * width] = block[2 + i].T.astype(bf_type)
    copies[5].wait()
    rest = query_all.shape[0] - 3 * width
    tail = jnp.concatenate([rows[...], jnp.zeros((rest - 2, shard), fl_type)], axis=0)
    query_all[3 * width :] = tail.astype(bf_type)
    height = query_all.shape[0] // 8
    message[...] = query_all[pl.ds(pl.multiple_of(part * height, 16), height)]


def members(ids_ref):
    rows = ids_ref.shape[1]
    classes = lax.broadcasted_iota(jnp.int32, (PAD, rows), 0)
    return (classes == ids_ref[...]).astype(fl_type).astype(bf_type)


def valid_row(count, start, rows):
    slots = lax.broadcasted_iota(jnp.int32, (1, rows), 1) + start
    return slots < count


def put_chunks(acc, keep, send, node, extra):
    width = acc.shape[2]
    head = width // 4
    for g in range(GROUPS):
        for c in range(CLUSTERS):
            chunk = g * CLUSTERS + c
            distance = lax.bitwise_xor(node, chunk)
            slot = lax.shift_right_logical(distance, 1)
            lane_head = lax.broadcasted_iota(jnp.int32, (head, width), 1) // head
            body = jnp.zeros((head, width), fl_type)
            for h in range(4):
                rows = acc[g, c * width + h * head : c * width + (h + 1) * head, :]
                body = jnp.where(lane_head == h, rows, body)
            block = jnp.concatenate([body, extra(g, c)], axis=0)

            @pl.when(lax.bitwise_and(distance, 1) == 0)
            def _():
                keep[slot] = block

            @pl.when(lax.bitwise_and(distance, 1) == 1)
            def _():
                send[slot] = block.astype(bf_type)


def key_kernel(pieces, step, place, x, ids, *refs):
    mine, other = refs[:pieces], refs[pieces : 2 * pieces]
    key_slope, key_out, value_out, keep, send, weights, masked, acc = refs[2 * pieces :]
    core, node, count = place[0], place[1], place[3]
    width = x.shape[1]
    rows = x.shape[0]
    half = width // GROUPS

    span = mine[0].shape[1]
    for d in range(pieces):
        cols = slice(d * span, (d + 1) * span)
        weights[pl.ds(pl.multiple_of(core * width, 16), width), cols] = mine[d][...]
        weights[pl.ds(pl.multiple_of((1 - core) * width, 16), width), cols] = other[d][...]

    table = members(ids)
    valid = valid_row(count, step * rows, rows)
    for g in range(GROUPS):
        sig = jax.nn.sigmoid(dot_nt(weights[g * half : (g + 1) * half, :], x[...]))
        kept = jnp.where(valid, sig, 0.0)
        key_slope[g * half : (g + 1) * half, :] = kept * (1.0 - sig)
        keys = kept.astype(bf_type)
        key_out[g * half : (g + 1) * half, :] = keys
        value = dot_nt(weights[width + g * half : width + (g + 1) * half, :], x[...]).astype(bf_type)
        value_out[g * half : (g + 1) * half, :] = value
        for c in range(CLUSTERS):
            masked[c * half : (c + 1) * half, :] = value * table[c : c + 1, :]
        masked[CLUSTERS * half :, :] = table
        acc[g] = dot_nt(masked[...], keys)

    def extra(g, c):
        row = acc[g, CLUSTERS * half + c : CLUSTERS * half + c + 1, :]
        return jnp.concatenate([row, jnp.zeros((PAD - 1, half), fl_type)], axis=0)

    put_chunks(acc, keep, send, node, extra)


def weights_kernel(pieces, step, place, own, *refs):
    stacks = refs[:8]
    query_weight, gate_weight, out_weight, gain, shift, full_query, full_gate, stage = refs[8:]
    node, shard = place[1], place[2]
    width = out_weight.shape[0]
    span = own.shape[1]
    height = own.shape[0] // 8
    stage[0] = own[...]
    for position in range(8):
        where = pl.multiple_of(lax.bitwise_xor(node, position) * height, 16)
        for d in range(1, pieces):
            stage[d, pl.ds(where, height), :] = stacks[position][d - 1]
    norm_rows = []
    for z in range(pieces):
        where = lax.bitwise_xor(shard, z)
        cols = slice(z * span, (z + 1) * span)
        query_weight[:, cols] = stage[z, 0:width, :]
        gate_weight[:, cols] = stage[z, width : 2 * width, :]
        full_query[:, cols] = stage[where, 0:width, :]
        full_gate[:, cols] = stage[where, width : 2 * width, :]
        out_weight[cols, :] = stage[where, 2 * width : 3 * width, :].T
        norm_rows.append(stage[where, 3 * width : 3 * width + 16, :])
    turned = jnp.concatenate(norm_rows, axis=1).astype(fl_type).T
    gain[...] = jnp.broadcast_to(turned[:, 0:1], gain.shape)
    shift[...] = jnp.broadcast_to(turned[:, 1:2], shift.shape)


def key_weights_kernel(pieces, step, place, *refs):
    mine, other = refs[:pieces], refs[pieces : 2 * pieces]
    full, stage = refs[2 * pieces :]
    core = place[0]
    width, span = full.shape[1], mine[0].shape[1]
    for d in range(pieces):
        stage[d, pl.ds(pl.multiple_of(core * width, 16), width), :] = mine[d][0:width]
        stage[d, pl.ds(pl.multiple_of((1 - core) * width, 16), width), :] = other[d][0:width]
    for z in range(pieces):
        full[:, z * span : (z + 1) * span] = stage[lax.bitwise_xor(place[2], z)]


def query_kernel(step, place, x, weight, query_slope, query):
    sig = jax.nn.sigmoid(dot_nt(weight[...], x[...]))
    query_slope[...] = sig * (1.0 - sig)
    query[...] = sig.astype(bf_type)


def gate_kernel(step, place, x, weight, gate):
    rows = x.shape[0]
    valid = valid_row(place[3], step * rows, rows)
    gate[...] = jnp.where(valid, dot_nt(weight[...], x[...]), 0.0)


def grad_prod_kernel(step, place, g, out_weight, grad_prod):
    rows = g.shape[0]
    valid = valid_row(place[3], step * rows, rows)
    grad_prod[...] = jnp.where(valid, dot_nt(out_weight[...], g[...]), 0.0)


def place_chunks(chunk_refs, place, stage):
    node = place[1]
    for d in range(CHUNKS):
        stage[lax.bitwise_xor(node, d)] = chunk_refs[d][...]


def pair_rows(h, value):
    lane_head = lax.broadcasted_iota(jnp.int32, (1, value.shape[1]), 1) // (value.shape[1] // 2)
    return jnp.where(lane_head == h, value, jnp.zeros_like(value))


def pair_block(chunk, p, head):
    mine = chunk[:head, p * 2 * head : (p + 1) * 2 * head]
    return jnp.concatenate([pair_rows(0, mine), pair_rows(1, mine)], axis=0)


def head_rows(width, h, value):
    lane_head = lax.broadcasted_iota(jnp.int32, (1, width), 1) // (width // 4)
    return jnp.where(lane_head == h, value, jnp.zeros_like(value))


def middle_kernel(steps, lanes, step, place, ids, query, gate, grad_prod, gain, shift, *refs):
    chunk_refs = refs[:CHUNKS]
    prod_out, dgate_out, dnum_out, dden_out, keep, send = refs[CHUNKS : CHUNKS + 6]
    rest = refs[CHUNKS + 6 :]
    width, rows = query.shape
    parts = rows // lanes
    stage, left, acc, dgain, dshift = rest[:5]
    stacks, back_stacks, nums, normeds, dnormeds, dens, ddens = (
        rest[5 + i * parts : 5 + (i + 1) * parts] for i in range(7)
    )
    node, count = place[1], place[3]
    half = width // GROUPS
    head = half // 4

    @pl.when(step == 0)
    def _():
        place_chunks(chunk_refs, place, stage)
        for g in range(GROUPS):
            for c in range(CLUSTERS):
                chunk = stage[g * CLUSTERS + c].astype(fl_type)
                cols = slice(c * 2 * head, (c + 1) * 2 * head)
                for p in range(2):
                    mine = chunk[:, p * 2 * head : (p + 1) * 2 * head]
                    for h in range(2):
                        at = slice(h * head, (h + 1) * head)
                        left[g * 2 + p, at, cols] = pair_rows(h, mine[:head]).astype(bf_type)
                    sums = [pair_rows(h, mine[head : head + 1]) for h in range(2)]
                    sums.append(jnp.zeros((PAD - 2, 2 * head), fl_type))
                    left[g * 2 + p, 2 * head :, cols] = jnp.concatenate(sums, axis=0).astype(bf_type)
        acc[...] = jnp.zeros_like(acc)
        dgain[...] = jnp.zeros_like(dgain)
        dshift[...] = jnp.zeros_like(dshift)

    def forward(part):
        cols = slice(part * lanes, (part + 1) * lanes)
        table = members(ids.at[:, cols])
        stack, num, den = stacks[part], nums[part], dens[part]
        for p in range(PAIRS):
            at = slice(p * 2 * head, (p + 1) * 2 * head)
            mine = query[at, cols]
            for c in range(CLUSTERS):
                stack[p, c * 2 * head : (c + 1) * 2 * head, :] = mine * table[c : c + 1, :]
            both = dot_nn(left[p], stack[p])
            num[at, :] = both[: 2 * head]
            row = (p // 2) * 8 + (p % 2) * 2
            den[row : row + 2, :] = 1.0 / both[2 * head : 2 * head + 2]

    def norm(part):
        cols = slice(part * lanes, (part + 1) * lanes)
        num, dnormed, den, dden = nums[part], dnormeds[part], dens[part], ddens[part]
        spans = [slice(h * head, (h + 1) * head) for h in range(HEADS)]
        inverse = [den[(h // 4) * 8 + h % 4 : (h // 4) * 8 + h % 4 + 1, :] for h in range(HEADS)]

        def mean_of(blocks):
            return jnp.sum(tree_sum(blocks), axis=0, keepdims=True) * (1.0 / width)

        mean = mean_of([fold_rows(num[spans[h], :]) * inverse[h] for h in range(HEADS)])
        squares = []
        for h in range(HEADS):
            centered = num[spans[h], :] * inverse[h] - mean
            num[spans[h], :] = centered
            squares.append(fold_rows(centered * centered))
        scale = lax.rsqrt(mean_of(squares) + norm_eps)
        first, second = [], []
        for h in range(HEADS):
            span = spans[h]
            ah = num[span, :] * scale
            num[span, :] = ah
            gamma = jnp.concatenate([gain[span, :]] * (lanes // 128), axis=1)
            beta = jnp.concatenate([shift[span, :]] * (lanes // 128), axis=1)
            u = ah * gamma + beta
            zg = gate[span, cols]
            dp = grad_prod[span, cols]
            prod_out[span, cols] = (u * zg).astype(bf_type)
            du = dp * zg
            dgate_out[span, cols] = (dp * u).astype(bf_type)
            du_ah = du * ah
            dgain[span, :] += fold_lanes(du_ah)
            dshift[span, :] += fold_lanes(du)
            dah = gamma * du
            first.append(fold_rows(dah))
            second.append(fold_rows(gamma * du_ah))
            dnormed[span, :] = dah
        first = mean_of(first)
        second = mean_of(second)
        shifted = mean * scale
        for h in range(HEADS):
            span = spans[h]
            ah = num[span, :]
            rest = dnormed[span, :] - ah * second - first
            dnum_out[span, cols] = (rest * (scale * inverse[h])).astype(bf_type)
            inner = fold_rows(rest * ah) + shifted * fold_rows(rest)
            row = (h // 4) * 8 + h % 4
            dden[row : row + 1, :] = -jnp.sum(inner, axis=0, keepdims=True) * inverse[h]
        dden_out[:, cols] = dden[...]

    def backward(part):
        cols = slice(part * lanes, (part + 1) * lanes)
        table = members(ids.at[:, cols])
        stack, dden = back_stacks[part], ddens[part]
        for g in range(GROUPS):
            mine = dnum_out[g * half : (g + 1) * half, cols]
            for c in range(CLUSTERS):
                stack[g, c * half : (c + 1) * half, :] = mine * table[c : c + 1, :]
            den_rows = dden[g * 8 : g * 8 + 4, :]
            high = den_rows.astype(bf_type)
            low = (den_rows - high.astype(fl_type)).astype(bf_type)
            four_high = jnp.concatenate([high * table[c : c + 1, :] for c in range(CLUSTERS)], axis=0)
            four_low = jnp.concatenate([low * table[c : c + 1, :] for c in range(CLUSTERS)], axis=0)
            stack[g, CLUSTERS * half :, :] = jnp.concatenate([four_high, four_low], axis=0)
            acc[g] += dot_nt(stack[g], query[g * half : (g + 1) * half, cols])

    for part in range(parts):
        forward(part)
    for part in range(parts):
        norm(part)
        backward(part)

    @pl.when(step == steps - 1)
    def _():
        gain_row = jnp.sum(dgain[...].T, axis=0, keepdims=True)
        shift_row = jnp.sum(dshift[...].T, axis=0, keepdims=True)

        def extra(g, c):
            base = CLUSTERS * half
            row = jnp.zeros((1, half), fl_type)
            for h in range(4):
                at = base + c * 4 + h
                row = row + head_rows(half, h, acc[g, at : at + 1, :] + acc[g, at + 16 : at + 17, :])
            cols = slice(g * half, (g + 1) * half)
            tail = [row]
            if c == 0:
                tail += [gain_row[:, cols], shift_row[:, cols]]
            tail.append(jnp.zeros((PAD - len(tail), half), fl_type))
            return jnp.concatenate(tail, axis=0)

        put_chunks(acc, keep, send, node, extra)


def fold_rows(block):
    return tree_sum([block[i * 8 : (i + 1) * 8] for i in range(block.shape[0] // 8)])


def fold_lanes(block):
    return tree_sum([block[:, i * 128 : (i + 1) * 128] for i in range(block.shape[1] // 128)])


def write_pieces(pieces, node, shard, span, keep, send, blocks):
    for chunk in range(8):
        distance = lax.bitwise_xor(node, chunk)
        slot = lax.shift_right_logical(distance, 1)
        even = lax.bitwise_and(distance, 1) == 0
        for z in range(pieces):
            block = blocks(z, chunk)

            @pl.when(even)
            def _():
                keep[slot, z] = block

            @pl.when(jnp.logical_not(even))
            def _():
                send[slot, z] = block.astype(bf_type)


def query_back_kernel(step, place, ids, dnum, dden, query_slope, *refs):
    chunk_refs = refs[:CHUNKS]
    dquery_out = refs[CHUNKS]
    stage, left, sums, stack = refs[CHUNKS + 1 :]
    width, rows = dnum.shape
    half = width // GROUPS
    head = half // 4

    @pl.when(step == 0)
    def _():
        place_chunks(chunk_refs, place, stage)
        for gr in range(GROUPS):
            for c in range(CLUSTERS):
                chunk = stage[gr * CLUSTERS + c].astype(fl_type)
                for p in range(2):
                    cols = slice(c * 2 * head, (c + 1) * 2 * head)
                    left[gr * 2 + p, :, cols] = pair_block(chunk, p, head).T.astype(bf_type)
                column = chunk[head : head + 8].T
                sums[c, gr * half : (gr + 1) * half, :] = jnp.broadcast_to(column[:, 0:1], (half, 128))

    table = members(ids)
    for p in range(PAIRS):
        part = dnum[p * 2 * head : (p + 1) * 2 * head, :]
        for c in range(CLUSTERS):
            stack[p, c * 2 * head : (c + 1) * 2 * head, :] = part * table[c : c + 1, :]
        dq = dot_nn(left[p], stack[p])
        for h in range(2):
            at = slice((p * 2 + h) * head, (p * 2 + h + 1) * head)
            pick = pick_rows(sums, at, ids, rows)
            row = (p // 2) * 8 + (p % 2) * 2 + h
            full = dq[h * head : (h + 1) * head] + dden[row : row + 1, :] * pick
            dquery_out[at, :] = (full * query_slope[at, :]).astype(bf_type)


def grad_query_kernel(step, place, dquery, x, grad_query):
    @pl.when(step == 0)
    def _():
        grad_query[...] = jnp.zeros_like(grad_query)

    grad_query[...] += dot_nn(dquery[...], x[...])


def gate_back_kernel(step, place, dgate, prod, x, g, grad_gate, grad_out):
    @pl.when(step == 0)
    def _():
        grad_gate[...] = jnp.zeros_like(grad_gate)
        grad_out[...] = jnp.zeros_like(grad_out)

    grad_gate[...] += dot_nn(dgate[...], x[...])
    grad_out[...] += dot_nn(prod[...], g[...])


def out_part(grad_out, shard, z, chunk, which, span):
    lanes = grad_out.shape[1] // 4
    quarter = span // 4
    start = lax.bitwise_xor(shard, z) * span + (chunk % 2) * 2 * quarter + which * quarter
    rows = grad_out[pl.ds(pl.multiple_of(start, 8), quarter), (chunk // 2) * lanes : (chunk // 2 + 1) * lanes]
    return fold(rows, span)


def early_kernel(pieces, step, place, grad_query, grad_gate, grad_out, keep, send):
    node, shard = place[1], place[2]
    width = grad_out.shape[1]
    span = width // pieces
    tall = 2 * width // 8

    def blocks(z, chunk):
        source = grad_query if chunk < 4 else grad_gate
        top = source[(chunk % 4) * tall : (chunk % 4 + 1) * tall, z * span : (z + 1) * span]
        return jnp.concatenate([top, out_part(grad_out, shard, z, chunk, 1, span)], axis=0)

    write_pieces(pieces, node, shard, span, keep, send, blocks)


def fold(block, span):
    return jnp.concatenate(
        [block[:, i * span : (i + 1) * span] for i in range(block.shape[1] // span)], axis=0
    )


def pick_rows(sums, at, ids, rows):
    reps = rows // 128
    wide = [jnp.concatenate([sums[c, at, :]] * reps, axis=1) for c in range(CLUSTERS)]
    pick = wide[CLUSTERS - 1]
    for c in range(CLUSTERS - 1):
        pick = jnp.where(ids[...] == c, wide[c], pick)
    return pick


def output_kernel(step, place, x, prod, out_weight, result):
    result[...] = x[...].astype(fl_type) + dot_tn(prod[...], out_weight[...])


def key_back_kernel(pieces, step, place, ids, key_slope, key, value, x, grad_out, *refs):
    chunk_refs = refs[:CHUNKS]
    dkey_out, dvalue_out, norm_out, keep, send = refs[CHUNKS : CHUNKS + 5]
    stage, left_key, left_value, sums, stack, key_stack, acc = refs[CHUNKS + 5 :]
    node, shard, count = place[1], place[2], place[3]
    width, rows = value.shape
    half = width // GROUPS
    head = half // 4
    span = width // pieces

    @pl.when(step == 0)
    def _():
        place_chunks(chunk_refs, place, stage)
        for gr in range(GROUPS):
            for c in range(CLUSTERS):
                chunk = stage[gr * CLUSTERS + c].astype(fl_type)
                for p in range(2):
                    cols = slice(c * 2 * head, (c + 1) * 2 * head)
                    pair = pair_block(chunk, p, head)
                    left_value[gr * 2 + p, :, cols] = pair.astype(bf_type)
                    left_key[gr * 2 + p, :, cols] = pair.T.astype(bf_type)
                column = chunk[head : head + 8].T
                sums[c, gr * half : (gr + 1) * half, :] = jnp.broadcast_to(column[:, 0:1], (half, 128))
                if c == 0:
                    norm_out[:, gr * half : (gr + 1) * half] = chunk[head : head + 8]

    table = members(ids)
    valid = valid_row(count, step * rows, rows)
    for p in range(PAIRS):
        at = slice(p * 2 * head, (p + 1) * 2 * head)
        part = value[at, :]
        for c in range(CLUSTERS):
            stack[p % 2, c * 2 * head : (c + 1) * 2 * head, :] = part * table[c : c + 1, :]
        dk = dot_nn(left_key[p], stack[p % 2])
        for h in range(2):
            sub = slice((p * 2 + h) * head, (p * 2 + h + 1) * head)
            full = dk[h * head : (h + 1) * head] + pick_rows(sums, sub, ids, rows)
            dkey_out[sub, :] = (full * key_slope[sub, :]).astype(bf_type)
        part = key[at, :]
        for c in range(CLUSTERS):
            key_stack[p % 2, c * 2 * head : (c + 1) * 2 * head, :] = part * table[c : c + 1, :]
        dvalue_out[at, :] = dot_nn(left_value[p], key_stack[p % 2]).astype(bf_type)
    acc[0:width] = dot_nn(dkey_out[...], x[...])
    acc[width : 2 * width] = dot_nn(dvalue_out[...], x[...])

    tall = 2 * width // 8

    def blocks(z, chunk):
        top = acc[chunk * tall : (chunk + 1) * tall, z * span : (z + 1) * span]
        return jnp.concatenate([top, out_part(grad_out, shard, z, chunk, 0, span)], axis=0)

    write_pieces(pieces, node, shard, span, keep, send, blocks)


def input_kernel(steps, step, place, dquery, dkey, dvalue, dgate, full_query, full_key, full_gate, g, result, blocks, sems):
    rows, width = g.shape
    total = g[...].astype(fl_type)
    total = total + dot_tn(dquery[...], full_query[...])
    total = total + dot_tn(dkey[...], full_key[0:width, :])
    total = total + dot_tn(dvalue[...], full_key[width:, :])
    total = total + dot_tn(dgate[...], full_gate[...])
    blocks[step] = total

    def copy(i):
        at = pl.ds(pl.multiple_of(i * rows, 8), rows)
        return pltpu.make_async_copy(blocks.at[i], result.at[at, :], sems.at[i])

    copy(step).start()

    @pl.when(step == steps - 1)
    def _():
        for i in range(steps):
            copy(i).wait()


def finish_kernel(step, *refs):
    parts, sums = refs[:-1], refs[-1]
    sums[...] = tree_sum([p[...].astype(fl_type) for p in parts]).astype(bf_type)


def squares_kernel(step, *refs):
    parts, squares = refs[:-1], refs[-1]
    totals = []
    for part in parts:
        value = part[...].astype(fl_type)
        totals.append(fold_rows(value * value))
    total = jnp.sum(tree_sum(totals), axis=0, keepdims=True)
    squares[...] = jnp.broadcast_to(jnp.sum(total, axis=1, keepdims=True), squares.shape)


def assemble_kernel(step, place, *refs):
    parts, (grad_proj, grad_out, stage) = refs[:CHUNKS], refs[CHUNKS:]
    node = place[1]
    span, width = grad_out.shape
    tall = 2 * width // 8
    lanes = width // 4
    rows = span // 2
    folds = lanes // span
    for d in range(CHUNKS):
        chunk = lax.bitwise_xor(node, d)
        stage[chunk] = parts[d][...].astype(fl_type)
    rows = rows // 2
    late = tall + rows * folds
    for chunk in range(CHUNKS):
        query_at = (0 if chunk < 4 else 3 * width) + (chunk % 4) * tall
        grad_proj[:, width + chunk * tall : width + (chunk + 1) * tall] = stage[chunk, 0:tall].T
        grad_proj[:, query_at : query_at + tall] = stage[chunk, late : late + tall].T
        for which in range(2):
            for i in range(folds):
                at = slice((chunk // 2) * lanes + i * span, (chunk // 2) * lanes + (i + 1) * span)
                start = which * late + tall + i * rows
                row = (chunk % 2 * 2 + which) * rows
                grad_out[row : row + rows, at] = stage[chunk, start : start + rows]


def adam(master_w, moment_old, square_old, clipped, decay_coef, step_rate):
    moment_new = beta_one * moment_old + (1.0 - beta_one) * clipped
    square_new = beta_two * square_old + (1.0 - beta_two) * clipped * clipped
    moment_hat = moment_new * (1.0 / (1.0 - beta_one**STEP))
    square_hat = square_new * (1.0 / (1.0 - beta_two**STEP))
    master_new = master_w * (1.0 - step_rate * decay_coef) - step_rate * moment_hat / (
        jnp.sqrt(square_hat) + adam_eps
    )
    return moment_new, square_new, master_new


def update_kernel(pieces, step, place, *refs):
    squares, (gp, go, gn, pw, pm, ps, ow, om, osq, nw, nm, ns) = refs[:pieces], refs[pieces : pieces + 12]
    size, *results = refs[pieces + 12 : pieces + 25]
    p_out, o_out, n_out = results[0:4], results[4:8], results[8:12]
    new_p, new_pc, new_o, new_oc, new_n, sems = refs[pieces + 25 :]
    shard = place[2]
    span, width = ow.shape
    norm_grad = gn[1:3, :]
    norm_square = jnp.sum(norm_grad * norm_grad, axis=0, keepdims=True)
    total = tree_sum([q[0:1, 0:1] for q in squares]) + jnp.sum(norm_square, axis=1, keepdims=True)
    norm = jnp.sqrt(total)
    size[...] = norm
    clip_level = 0.5 * math.sqrt(5 * width * width + 2 * width)
    scale = jnp.minimum(1.0, clip_level / norm)
    copies = []

    def send(source, target):
        copies.append(pltpu.make_async_copy(source, target, sems.at[len(copies)]))
        copies[-1].start()

    scale = jnp.broadcast_to(scale, (1, width))

    def step_block(at, cols, w, m, s, grad, new, new_copy):
        results = adam(w[at, cols], m[at, cols], s[at, cols], grad[at, cols] * scale, decay_rate, learn_rate)
        for j, value in zip((2, 0, 1), (results[2], *results[:2])):
            new[j, at, :] = value
        new_copy[at, :] = results[2].astype(bf_type)

    blocks = [slice(r, r + 16) for r in range(0, span, 16)]
    for i in range(4):
        cols = slice(i * width, (i + 1) * width)
        for at in blocks:
            step_block(at, cols, pw, pm, ps, gp, new_p.at[:, i], new_pc.at[i])
        for j in range(3):
            send(new_p.at[j, i], p_out[j].at[:, cols])
        send(new_pc.at[i], p_out[3].at[:, cols])
    for at in blocks:
        step_block(at, slice(0, width), ow, om, osq, go, new_o, new_oc)
    for j in range(3):
        send(new_o.at[j], o_out[j])
    send(new_oc, o_out[3])
    mine = norm_grad[:, 0:span]
    for z in range(1, pieces):
        mine = jnp.where(shard == z, norm_grad[:, z * span : (z + 1) * span], mine)
    clipped = mine * scale[:, 0:span]
    for j, value in enumerate((clipped, *adam(nw[...], nm[...], ns[...], clipped, 0.0, norm_rate))):
        new_n[j] = value
        send(new_n.at[j], n_out[j])
    for copy in copies:
        copy.wait()


def make_exchange(nodes, shards):
    count = nodes * shards

    def exchange(value, node_bits, shard_bits):
        pairs = [
            (i, ((i // shards) ^ node_bits) * shards + ((i % shards) ^ shard_bits)) for i in range(count)
        ]
        return lax.ppermute(value, AXES, pairs)

    return exchange


def tree_sum(parts):
    parts = list(parts)
    while len(parts) > 1:
        pairs = [parts[i] + parts[i + 1] for i in range(0, len(parts) - 1, 2)]
        parts = pairs + parts[len(parts) - len(parts) % 2 :]
    return parts[0]


def to_float(parts):
    return [p.astype(fl_type) for p in parts]


def tie(value, *others):
    return lax.optimization_barrier((value, *others))[0]


def tie(value, *others):
    return lax.optimization_barrier((value, *others))[0]


def local(nodes, shards, *args):
    (x, g, ids, counts, pw, pm, ps, ow, om, osq, nw, nm, ns) = args
    exchange = make_exchange(nodes, shards)
    outer = nodes // 8
    rows, width = x.shape
    half = width // GROUPS
    head = width // HEADS
    span = pw.shape[0]
    block = min(1024, rows)
    steps = rows // block
    lanes = 256
    tall = 2 * width // 8
    part_rows = (3 * width + 2 + 127) // 128 * 16
    work = 2 * rows * width * width

    node = lax.axis_index("nodes").astype(jnp.int32)
    shard = lax.axis_index("shard").astype(jnp.int32)
    place = jnp.stack([lax.bitwise_and(node, 1), lax.bitwise_and(node, 7), shard, counts[0]])
    ids = ids.reshape(1, rows)
    chunk_shape = (4, head + PAD, half)

    def wide(dtype):
        return out((width, rows), dtype)

    def vmem(shape, dtype):
        return pltpu.VMEM(shape, dtype)

    message, kv_half, part, query_all = call(
        prep_kernel,
        1,
        (pw, ow, nw),
        ["hbm"] * 3,
        [
            out((width, span), bf_type),
            out((width, span), bf_type),
            out((part_rows, span), bf_type),
            out((8 * part_rows, span), bf_type),
        ],
        [None] * 4,
        [
            vmem((5, span, width), fl_type),
            vmem((2, span), fl_type),
            vmem((2, width, span), bf_type),
            pltpu.SemaphoreType.DMA((6,)),
        ],
        1e6,
        "prep",
        vmem=60,
    )
    x_turned = jnp.concatenate(
        [
            lax.dynamic_slice(x, (0, lax.bitwise_xor(shard, z) * span), (rows, span))
            for z in range(shards)
        ],
        axis=1,
    )
    mine, other = [message], [kv_half]
    for z in range(1, shards):
        late = z == 2
        mine.append(exchange(tie(message, x_turned) if late else message, 0, z))
    stack = jnp.stack([exchange(part, 0, z) for z in range(1, shards)])
    stacks = [stack] + [None] * 7
    for e in range(1, 4):
        stacks[2 * e] = exchange(stack, 2 * e, 0)
    for z in range(1, shards):
        other.append(exchange(tie(mine[z], stack), 1, 0))
    key_slope, key, value, keep, send = call(
        functools.partial(key_kernel, shards),
        1,
        (place, x_turned, ids, *mine, *other),
        ["smem", "row", "lane"] + [None] * (2 * shards),
        [wide(fl_type), wide(bf_type), wide(bf_type), out(chunk_shape, fl_type), out(chunk_shape, bf_type)],
        ["lane", "lane", "lane", None, None],
        [
            vmem((2 * width, width), bf_type),
            vmem((CLUSTERS * half + PAD, rows), bf_type),
            vmem((GROUPS, CLUSTERS * half + PAD, half), fl_type),
        ],
        1e3,
        "keys",
        rows,
        vmem=26,
    )

    def swap(pieces, peers, filler, cast=True):
        got = [exchange(p, *at) for p, at in zip(pieces, peers)]
        if filler is not None:
            done = filler(pieces[0])
            got = list(tie(tuple(got), done))
        return to_float(got) if cast else got

    plane = [(2 * e, 0) for e in range(1, 4)]
    along = [(0, z) for z in range(1, shards)]
    made = {}

    def reduce_chunks(keep, send, fillers):
        mine = keep + exchange(send, 1, 0).astype(fl_type)
        got = swap([mine[e].astype(bf_type) for e in range(1, 4)], plane, fillers[0])
        own = tree_sum([mine[0], *got]).astype(bf_type)
        got = swap([own] * (shards - 1), along, fillers[1])
        own = tree_sum([own.astype(fl_type), *got]).astype(bf_type)
        if outer > 1:
            got = swap([own] * (outer - 1), [(8 * o, 0) for o in range(1, outer)], None)
            own = tree_sum([own.astype(fl_type), *got]).astype(bf_type)
        return spread(own, fillers[2])

    def spread(own, filler=None):
        chunks = [own] + [None] * 7
        for e in range(1, 4):
            chunks[2 * e] = exchange(own, 2 * e, 0)
        chunks[1] = exchange(own, 1, 0)
        if filler is not None:
            done = filler(own)
            chunks[2], chunks[4], chunks[6] = tie((chunks[2], chunks[4], chunks[6]), done)
        for e in range(1, 4):
            chunks[2 * e + 1] = exchange(chunks[2 * e], 1, 0)
        return chunks

    def fill_weights(dep):
        made["weights"] = call(
            functools.partial(weights_kernel, shards),
            1,
            (tie(place, dep), query_all, *stacks),
            ["smem", None] + [None] * 8,
            [
                out((width, width), bf_type),
                out((width, width), bf_type),
                out((width, width), bf_type),
                out((width, 128), fl_type),
                out((width, 128), fl_type),
                out((width, width), bf_type),
                out((width, width), bf_type),
            ],
            [None] * 7,
            [vmem((shards, 8 * part_rows, span), bf_type)],
            1e6,
            "weights",
        )
        return made["weights"][0]

    def fill_query(dep):
        made["query"] = call(
            query_kernel,
            1,
            (tie(place, dep), x_turned, made["weights"][0]),
            ["smem", "row", None],
            [wide(fl_type), wide(bf_type)],
            ["lane"] * 2,
            [],
            work,
            "query",
            rows,
            vmem=16,
        )
        return made["query"][1], fill_gate(dep)

    def fill_gate(dep):
        gate_weight = made["weights"][1]
        made["gate"] = call(
            gate_kernel,
            1,
            (tie(place, dep), x_turned, gate_weight),
            ["smem", "row", None],
            [wide(fl_type)],
            ["lane"],
            [],
            work,
            "gate",
            rows,
            vmem=16,
        )[0]
        return made["gate"]

    def fill_grad_prod(dep):
        out_weight = made["weights"][2]
        made["grad_prod"] = call(
            grad_prod_kernel,
            1,
            (tie(place, dep), g, out_weight),
            ["smem", "row", None],
            [wide(fl_type)],
            ["lane"],
            [],
            work,
            "grad_prod",
            rows,
            vmem=16,
        )[0]
        return made["grad_prod"]

    send = tie(send, *stacks[2::2])
    for e in range(4):
        stacks[2 * e + 1] = exchange(stacks[2 * e], 1, 0)
    chunks = reduce_chunks(keep, send, (fill_weights, fill_query, fill_grad_prod))
    out_weight, gain, shift, full_query, full_gate = made["weights"][2:]
    query_slope, query = made["query"]

    parts = block // lanes
    prod, dgate, dnum, dden, keep, send = call(
        functools.partial(middle_kernel, steps, lanes),
        steps,
        (place, ids, query, made["gate"], made["grad_prod"], gain, shift, *chunks),
        ["smem", "lane", "lane", "lane", "lane", None, None] + [None] * CHUNKS,
        [
            wide(bf_type),
            wide(bf_type),
            wide(bf_type),
            out((16, rows), fl_type),
            out(chunk_shape, fl_type),
            out(chunk_shape, bf_type),
        ],
        ["lane", "lane", "lane", "lane", None, None],
        [
            vmem((CHUNKS, head + PAD, half), bf_type),
            vmem((PAIRS, 2 * head + PAD, CLUSTERS * 2 * head), bf_type),
            vmem((GROUPS, CLUSTERS * half + 32, half), fl_type),
            vmem((width, 128), fl_type),
            vmem((width, 128), fl_type),
        ]
        + [vmem((PAIRS, CLUSTERS * 2 * head, lanes), bf_type)] * parts
        + [vmem((GROUPS, CLUSTERS * half + 32, lanes), bf_type)] * parts
        + [vmem((width, lanes), fl_type)] * (3 * parts)
        + [vmem((16, lanes), fl_type)] * (2 * parts),
        6 * work,
        "middle",
        block,
    )

    short = tall + (span // 4) * (width // 4 // span)
    height = 2 * short
    early_shape = late_shape = (4, shards, short, span)

    def fill_gate_back(dep):
        made["gate_back"] = call(
            gate_back_kernel,
            1,
            (tie(place, dep), dgate, prod, x_turned, g),
            ["smem", "lane", "lane", "row", "row"],
            [out((width, width), fl_type)] * 2,
            [None] * 2,
            [],
            2 * work,
            "gate_back",
            rows,
            vmem=16,
        )
        return made["gate_back"][0]

    def fill_output(dep):
        made["output"] = call(
            output_kernel,
            steps,
            (tie(place, dep), x, prod, out_weight),
            ["smem", "row", "lane", None],
            [out((rows, width), fl_type)],
            ["row"],
            [],
            work,
            "output",
            block,
            piped=True,
        )[0]
        return made["output"]

    def fill_query_back(dep):
        made["dquery"] = call(
            query_back_kernel,
            1,
            (tie(place, dep), ids, dnum, dden, query_slope, *chunks),
            ["smem", "lane", "lane", "lane", "lane"] + [None] * CHUNKS,
            [wide(bf_type)],
            ["lane"],
            [
                vmem((CHUNKS, head + PAD, half), bf_type),
                vmem((PAIRS, 2 * head, CLUSTERS * 2 * head), bf_type),
                vmem((CLUSTERS, width, 128), fl_type),
                vmem((PAIRS, CLUSTERS * 2 * head, rows), bf_type),
            ],
            2 * work,
            "query_back",
            rows,
            vmem=26,
        )[0]
        return made["dquery"]

    def fill_grad_query(dep):
        made["grad_query"] = call(
            grad_query_kernel,
            1,
            (tie(place, dep), made["dquery"], x_turned),
            ["smem", None, None],
            [out((width, width), fl_type)],
            [None],
            [],
            work,
            "grad_query",
            vmem=12,
        )[0]
        made["early"] = call(
            functools.partial(early_kernel, shards),
            1,
            (place, made["grad_query"], *made["gate_back"]),
            ["smem"] + [None] * 3,
            [out(early_shape, fl_type), out(early_shape, bf_type)],
            [None] * 2,
            [],
            1e6,
            "early",
            vmem=8,
        )
        return made["early"][1]

    back_chunks = reduce_chunks(keep, send, (fill_gate_back, fill_query_back, fill_grad_query))
    dquery = made["dquery"]

    early_keep, early_send = made["early"]
    early_send = tie(early_send, *back_chunks[2::2])
    early_mine = early_keep + exchange(early_send, 1, 0).astype(fl_type)
    early_pieces = tie(tuple(early_mine[e].astype(bf_type) for e in range(1, 4)))
    early_got = [exchange(p, *at) for p, at in zip(early_pieces, plane)]
    dkey, dvalue, norm_grad, keep, send = call(
        functools.partial(key_back_kernel, shards),
        1,
        (place, ids, key_slope, key, value, x_turned, made["gate_back"][1], *back_chunks),
        ["smem", "lane", "lane", "lane", "lane", "row", None] + [None] * CHUNKS,
        [
            wide(bf_type),
            wide(bf_type),
            out((8, width), fl_type),
            out(late_shape, fl_type),
            out(late_shape, bf_type),
        ],
        ["lane", "lane", None, None, None],
        [
            vmem((CHUNKS, head + PAD, half), bf_type),
            vmem((PAIRS, 2 * head, CLUSTERS * 2 * head), bf_type),
            vmem((PAIRS, 2 * head, CLUSTERS * 2 * head), bf_type),
            vmem((CLUSTERS, width, 128), fl_type),
            vmem((2, CLUSTERS * 2 * head, rows), bf_type),
            vmem((2, CLUSTERS * 2 * head, rows), bf_type),
            vmem((2 * width, width), fl_type),
        ],
        6 * work,
        "key_back",
        rows,
        vmem=26,
    )

    full_key = call(
        functools.partial(key_weights_kernel, shards),
        1,
        (place, *mine, *other),
        ["smem"] + [None] * (2 * shards),
        [out((2 * width, width), bf_type)],
        [None],
        [vmem((shards, 2 * width, span), bf_type)],
        1e6,
        "key_weights",
        vmem=12,
    )[0]

    def fill_inputs(dep):
        made["inputs"] = call(
            functools.partial(input_kernel, 2),
            2,
            (tie(place, dep), dquery, dkey, dvalue, dgate, full_query, full_key, full_gate, g),
            ["smem"] + ["lane"] * 4 + [None] * 3 + ["row"],
            [out((rows, width), fl_type)],
            ["hbm"],
            [vmem((2, rows // 2, width), fl_type), pltpu.SemaphoreType.DMA((2,))],
            4 * work,
            "inputs",
            rows // 2,
        )[0]
        return made["inputs"]

    send = tie(send, *early_got)
    mine_sum = keep + exchange(send, 1, 0).astype(fl_type)
    early_sum = tree_sum([early_mine[0], *to_float(early_got)])
    got = swap([mine_sum[e].astype(bf_type) for e in range(1, 4)], plane, fill_inputs)
    mine_sum = jnp.concatenate([tree_sum([mine_sum[0], *got]), early_sum], axis=1)
    pieces = tie(tuple(mine_sum[z].astype(bf_type) for z in range(1, shards)))
    owned_parts = [mine_sum[0], *swap(pieces, along, fill_output, cast=False)]
    if outer > 1:
        own = tree_sum(to_float(owned_parts)).astype(bf_type)
        got = [own] + [exchange(own, 8 * o, 0) for o in range(1, outer)]
        owned_parts = [tree_sum(to_float(got))] + [jnp.zeros_like(own)] * (shards - 1)

    sums = call(
        finish_kernel,
        1,
        owned_parts,
        [None] * shards,
        [out((height, span), bf_type)],
        [None],
        [],
        1e6,
        "finish",
        vmem=4,
    )[0]
    parts = spread(sums)
    squares = call(
        squares_kernel,
        1,
        parts,
        [None] * CHUNKS,
        [out((8, 128), fl_type)],
        [None],
        [],
        1e6,
        "squares",
        vmem=4,
    )[0]

    def fill_assemble(dep):
        made["grads"] = call(
            assemble_kernel,
            1,
            (tie(place, dep), *parts),
            ["smem"] + [None] * CHUNKS,
            [out((span, 4 * width), fl_type), out((span, width), fl_type)],
            [None] * 2,
            [vmem((CHUNKS, height, span), fl_type)],
            1e6,
            "assemble",
            vmem=8,
        )
        return made["grads"][0]

    squares = [squares, *swap([squares] * (shards - 1), along, fill_assemble)]
    states = (pw, pm, ps, ow, om, osq, nw, nm, ns)
    like = [pw] * 4 + [ow] * 4 + [nw] * 4
    kinds = [fl_type] * 3 + [bf_type] + [fl_type] * 3 + [bf_type] + [fl_type] * 4
    grad_size, *new = call(
        functools.partial(update_kernel, shards),
        1,
        (place, *squares, *made["grads"], norm_grad, *states),
        ["smem"] + [None] * (shards + 12),
        [out((1, 1), fl_type)] + [out(s.shape, k) for s, k in zip(like, kinds)],
        [None] + ["hbm"] * 12,
        [
            vmem((3, 4, span, width), fl_type),
            vmem((4, span, width), bf_type),
            vmem((3, span, width), fl_type),
            vmem((span, width), bf_type),
            vmem((4, 2, span), fl_type),
            pltpu.SemaphoreType.DMA((24,)),
        ],
        1e6,
        "update",
    )
    return (made["output"], made["inputs"], grad_size.reshape(1), *new)


def solution(mesh):
    nodes, shards = mesh.shape["nodes"], mesh.shape["shard"]
    by_node = P(AXES, None)
    rows = P("shard", None)
    cols = P(None, "shard")
    return jax.shard_map(
        functools.partial(local, nodes, shards),
        mesh=mesh,
        in_specs=(by_node, by_node, P(AXES), P(AXES)) + (rows,) * 6 + (cols,) * 3,
        out_specs=(by_node, by_node, P()) + (rows,) * 8 + (cols,) * 4,
        check_vma=False,
    )
```

```python
import functools
import math

import jax
import jax.numpy as jnp
from jax import lax
from jax.experimental import pallas as pl
from jax.experimental.pallas import tpu as pltpu
from jax.sharding import PartitionSpec as P

HEADS = 8
CLUSTERS = 4
STEP = 10
AXES = ("nodes", "shard")

norm_eps = 1e-05
beta_one = 0.9
beta_two = 0.999
learn_rate = 0.05
norm_rate = 0.5
decay_rate = 0.01
adam_eps = 1e-08
bf_type = jnp.bfloat16
fl_type = jnp.float32

GROUPS = 2
PAIRS = HEADS // 2
CHUNKS = GROUPS * CLUSTERS
PAD = 16


def dot_nn(a, b):
    return lax.dot_general(a, b, (((1,), (0,)), ((), ())), preferred_element_type=fl_type)


def dot_nt(a, b):
    return lax.dot_general(a, b, (((1,), (1,)), ((), ())), preferred_element_type=fl_type)


def dot_tn(a, b):
    return lax.dot_general(a, b, (((0,), (0,)), ((), ())), preferred_element_type=fl_type)


def whole(shape):
    return pl.BlockSpec(shape, lambda *_: (0,) * len(shape))


def smem():
    return pl.BlockSpec(memory_space=pltpu.SMEM)


def view(ref, kind, start, size):
    if kind == "lane":
        return ref.at[:, pl.ds(start, size)]
    if kind == "row":
        return ref.at[pl.ds(start, size), :]
    return ref


def call(kernel, steps, ins, in_kinds, outs, out_kinds, scratch, flops, name, block=0, vmem=16, piped=False):
    moved = sum(math.prod(a.shape) * a.dtype.itemsize for a in (*ins, *outs))
    arrays, kinds = [*ins, *outs], [*in_kinds, *out_kinds]

    def spec(array, kind):
        if kind == "smem":
            return smem()
        if kind == "hbm":
            return pl.BlockSpec(memory_space=pltpu.HBM)
        if isinstance(kind, pl.BlockSpec):
            return kind
        if piped and kind == "lane":
            return pl.BlockSpec((array.shape[0], block), lambda i: (0, i))
        if piped and kind == "row":
            return pl.BlockSpec((block, array.shape[1]), lambda i: (i, 0))
        return whole(array.shape)

    def body(*refs):
        if piped:
            kernel(pl.program_id(0), *refs)
            return
        if steps == 1:
            kernel(0, *refs)
            return

        def one(i, carry):
            start = pl.multiple_of(i * block, block)
            views = [view(r, k, start, block) for r, k in zip(refs, kinds)]
            kernel(i, *views, *refs[len(kinds) :])
            return carry

        lax.fori_loop(0, steps, one, 0)

    specs = [spec(a, k) for a, k in zip(arrays, kinds)]
    return pl.pallas_call(
        body,
        grid=(steps,) if piped else (),
        in_specs=specs[: len(ins)],
        out_specs=specs[len(ins) :],
        out_shape=outs,
        scratch_shapes=scratch,
        cost_estimate=pl.CostEstimate(flops=int(flops), transcendentals=0, bytes_accessed=int(moved)),
        compiler_params=pltpu.CompilerParams(vmem_limit_bytes=vmem * 1024 * 1024),
        name=name,
    )(*ins)


def out(shape, dtype):
    return jax.ShapeDtypeStruct(shape, dtype)


def fetch(copies):
    copies = [pltpu.make_async_copy(*c) for c in copies]
    for c in copies:
        c.start()
    return copies


def prep_kernel(step, wp, wo, wn, key_message, key_other, message, query_all, block, rows, stage, sems):
    core = lax.bitwise_and(lax.axis_index("nodes"), 1)
    part = lax.bitwise_and(lax.axis_index("nodes"), 7)
    shard, width = wo.shape
    columns = [wp.at[:, i * width : (i + 1) * width] for i in (1, 2, 0, 3)]
    sources = [*columns, wo]
    copies = fetch(
        [(sources[i], block.at[i], sems.at[i]) for i in range(5)] + [(wn, rows, sems.at[5])]
    )
    for i in range(2):
        copies[i].wait()
        stage[i] = block[i].T.astype(bf_type)
    key_message[...] = stage[core]
    key_other[...] = stage[1 - core]
    for i in range(3):
        copies[2 + i].wait()
        query_all[i * width : (i + 1) * width] = block[2 + i].T.astype(bf_type)
    copies[5].wait()
    rest = query_all.shape[0] - 3 * width
    tail = jnp.concatenate([rows[...], jnp.zeros((rest - 2, shard), fl_type)], axis=0)
    query_all[3 * width :] = tail.astype(bf_type)
    height = query_all.shape[0] // 8
    message[...] = query_all[pl.ds(pl.multiple_of(part * height, 16), height)]


def members(ids_ref):
    rows = ids_ref.shape[1]
    classes = lax.broadcasted_iota(jnp.int32, (PAD, rows), 0)
    return (classes == ids_ref[...]).astype(fl_type).astype(bf_type)


def valid_row(count, start, rows):
    slots = lax.broadcasted_iota(jnp.int32, (1, rows), 1) + start
    return slots < count


def put_chunks(acc, keep, send, node, extra):
    width = acc.shape[2]
    head = width // 4
    for g in range(GROUPS):
        for c in range(CLUSTERS):
            chunk = g * CLUSTERS + c
            distance = lax.bitwise_xor(node, chunk)
            slot = lax.shift_right_logical(distance, 1)
            lane_head = lax.broadcasted_iota(jnp.int32, (head, width), 1) // head
            body = jnp.zeros((head, width), fl_type)
            for h in range(4):
                rows = acc[g, c * width + h * head : c * width + (h + 1) * head, :]
                body = jnp.where(lane_head == h, rows, body)
            block = jnp.concatenate([body, extra(g, c)], axis=0)

            @pl.when(lax.bitwise_and(distance, 1) == 0)
            def _():
                keep[slot] = block

            @pl.when(lax.bitwise_and(distance, 1) == 1)
            def _():
                send[slot] = block.astype(bf_type)


def key_kernel(pieces, step, place, x, ids, *refs):
    mine, other = refs[:pieces], refs[pieces : 2 * pieces]
    key_slope, key_out, value_out, keep, send, weights, masked, acc = refs[2 * pieces :]
    core, node, count = place[0], place[1], place[3]
    width = x.shape[1]
    rows = x.shape[0]
    half = width // GROUPS

    span = mine[0].shape[1]
    for d in range(pieces):
        cols = slice(d * span, (d + 1) * span)
        weights[pl.ds(pl.multiple_of(core * width, 16), width), cols] = mine[d][...]
        weights[pl.ds(pl.multiple_of((1 - core) * width, 16), width), cols] = other[d][...]

    table = members(ids)
    valid = valid_row(count, step * rows, rows)
    for g in range(GROUPS):
        sig = jax.nn.sigmoid(dot_nt(weights[g * half : (g + 1) * half, :], x[...]))
        kept = jnp.where(valid, sig, 0.0)
        key_slope[g * half : (g + 1) * half, :] = kept * (1.0 - sig)
        keys = kept.astype(bf_type)
        key_out[g * half : (g + 1) * half, :] = keys
        value = dot_nt(weights[width + g * half : width + (g + 1) * half, :], x[...]).astype(bf_type)
        value_out[g * half : (g + 1) * half, :] = value
        for c in range(CLUSTERS):
            masked[c * half : (c + 1) * half, :] = value * table[c : c + 1, :]
        masked[CLUSTERS * half :, :] = table
        acc[g] = dot_nt(masked[...], keys)

    def extra(g, c):
        row = acc[g, CLUSTERS * half + c : CLUSTERS * half + c + 1, :]
        return jnp.concatenate([row, jnp.zeros((PAD - 1, half), fl_type)], axis=0)

    put_chunks(acc, keep, send, node, extra)


def weights_kernel(pieces, step, place, own, *refs):
    stacks = refs[:8]
    query_weight, gate_weight, out_weight, gain, shift, full_query, full_gate, stage = refs[8:]
    node, shard = place[1], place[2]
    width = out_weight.shape[0]
    span = own.shape[1]
    height = own.shape[0] // 8
    stage[0] = own[...]
    for position in range(8):
        where = pl.multiple_of(lax.bitwise_xor(node, position) * height, 16)
        for d in range(1, pieces):
            stage[d, pl.ds(where, height), :] = stacks[position][d - 1]
    norm_rows = []
    for z in range(pieces):
        where = lax.bitwise_xor(shard, z)
        cols = slice(z * span, (z + 1) * span)
        query_weight[:, cols] = stage[z, 0:width, :]
        gate_weight[:, cols] = stage[z, width : 2 * width, :]
        full_query[:, cols] = stage[where, 0:width, :]
        full_gate[:, cols] = stage[where, width : 2 * width, :]
        out_weight[cols, :] = stage[where, 2 * width : 3 * width, :].T
        norm_rows.append(stage[where, 3 * width : 3 * width + 16, :])
    turned = jnp.concatenate(norm_rows, axis=1).astype(fl_type).T
    gain[...] = jnp.broadcast_to(turned[:, 0:1], gain.shape)
    shift[...] = jnp.broadcast_to(turned[:, 1:2], shift.shape)


def key_weights_kernel(pieces, step, place, *refs):
    mine, other = refs[:pieces], refs[pieces : 2 * pieces]
    full, stage = refs[2 * pieces :]
    core = place[0]
    width, span = full.shape[1], mine[0].shape[1]
    for d in range(pieces):
        stage[d, pl.ds(pl.multiple_of(core * width, 16), width), :] = mine[d][0:width]
        stage[d, pl.ds(pl.multiple_of((1 - core) * width, 16), width), :] = other[d][0:width]
    for z in range(pieces):
        full[:, z * span : (z + 1) * span] = stage[lax.bitwise_xor(place[2], z)]


def query_kernel(step, place, x, weight, query_slope, query):
    sig = jax.nn.sigmoid(dot_nt(weight[...], x[...]))
    query_slope[...] = sig * (1.0 - sig)
    query[...] = sig.astype(bf_type)


def gate_kernel(step, place, x, weight, gate):
    rows = x.shape[0]
    valid = valid_row(place[3], step * rows, rows)
    gate[...] = jnp.where(valid, dot_nt(weight[...], x[...]), 0.0)


def grad_prod_kernel(step, place, g, out_weight, grad_prod):
    rows = g.shape[0]
    valid = valid_row(place[3], step * rows, rows)
    grad_prod[...] = jnp.where(valid, dot_nt(out_weight[...], g[...]), 0.0)


def place_chunks(chunk_refs, place, stage):
    node = place[1]
    for d in range(CHUNKS):
        stage[lax.bitwise_xor(node, d)] = chunk_refs[d][...]


def pair_rows(h, value):
    lane_head = lax.broadcasted_iota(jnp.int32, (1, value.shape[1]), 1) // (value.shape[1] // 2)
    return jnp.where(lane_head == h, value, jnp.zeros_like(value))


def pair_block(chunk, p, head):
    mine = chunk[:head, p * 2 * head : (p + 1) * 2 * head]
    return jnp.concatenate([pair_rows(0, mine), pair_rows(1, mine)], axis=0)


def head_rows(width, h, value):
    lane_head = lax.broadcasted_iota(jnp.int32, (1, width), 1) // (width // 4)
    return jnp.where(lane_head == h, value, jnp.zeros_like(value))


def middle_kernel(steps, lanes, step, place, ids, query, gate, grad_prod, gain, shift, *refs):
    chunk_refs = refs[:CHUNKS]
    prod_out, dgate_out, dnum_out, dden_out, keep, send = refs[CHUNKS : CHUNKS + 6]
    rest = refs[CHUNKS + 6 :]
    width, rows = query.shape
    parts = rows // lanes
    stage, left, acc, dgain, dshift = rest[:5]
    stacks, back_stacks, nums, normeds, dnormeds, dens, ddens = (
        rest[5 + i * parts : 5 + (i + 1) * parts] for i in range(7)
    )
    node, count = place[1], place[3]
    half = width // GROUPS
    head = half // 4

    @pl.when(step == 0)
    def _():
        place_chunks(chunk_refs, place, stage)
        for g in range(GROUPS):
            for c in range(CLUSTERS):
                chunk = stage[g * CLUSTERS + c].astype(fl_type)
                cols = slice(c * 2 * head, (c + 1) * 2 * head)
                for p in range(2):
                    mine = chunk[:, p * 2 * head : (p + 1) * 2 * head]
                    for h in range(2):
                        at = slice(h * head, (h + 1) * head)
                        left[g * 2 + p, at, cols] = pair_rows(h, mine[:head]).astype(bf_type)
                    sums = [pair_rows(h, mine[head : head + 1]) for h in range(2)]
                    sums.append(jnp.zeros((PAD - 2, 2 * head), fl_type))
                    left[g * 2 + p, 2 * head :, cols] = jnp.concatenate(sums, axis=0).astype(bf_type)
        acc[...] = jnp.zeros_like(acc)
        dgain[...] = jnp.zeros_like(dgain)
        dshift[...] = jnp.zeros_like(dshift)

    def forward(part):
        cols = slice(part * lanes, (part + 1) * lanes)
        table = members(ids.at[:, cols])
        stack, num, den = stacks[part], nums[part], dens[part]
        for p in range(PAIRS):
            at = slice(p * 2 * head, (p + 1) * 2 * head)
            mine = query[at, cols]
            for c in range(CLUSTERS):
                stack[p, c * 2 * head : (c + 1) * 2 * head, :] = mine * table[c : c + 1, :]
            both = dot_nn(left[p], stack[p])
            num[at, :] = both[: 2 * head]
            row = (p // 2) * 8 + (p % 2) * 2
            den[row : row + 2, :] = 1.0 / both[2 * head : 2 * head + 2]

    def norm(part):
        cols = slice(part * lanes, (part + 1) * lanes)
        num, dnormed, den, dden = nums[part], dnormeds[part], dens[part], ddens[part]
        spans = [slice(h * head, (h + 1) * head) for h in range(HEADS)]
        inverse = [den[(h // 4) * 8 + h % 4 : (h // 4) * 8 + h % 4 + 1, :] for h in range(HEADS)]

        def mean_of(blocks):
            return jnp.sum(tree_sum(blocks), axis=0, keepdims=True) * (1.0 / width)

        mean = mean_of([fold_rows(num[spans[h], :]) * inverse[h] for h in range(HEADS)])
        squares = []
        for h in range(HEADS):
            centered = num[spans[h], :] * inverse[h] - mean
            num[spans[h], :] = centered
            squares.append(fold_rows(centered * centered))
        scale = lax.rsqrt(mean_of(squares) + norm_eps)
        first, second = [], []
        for h in range(HEADS):
            span = spans[h]
            ah = num[span, :] * scale
            num[span, :] = ah
            gamma = jnp.concatenate([gain[span, :]] * (lanes // 128), axis=1)
            beta = jnp.concatenate([shift[span, :]] * (lanes // 128), axis=1)
            u = ah * gamma + beta
            zg = gate[span, cols]
            dp = grad_prod[span, cols]
            prod_out[span, cols] = (u * zg).astype(bf_type)
            du = dp * zg
            dgate_out[span, cols] = (dp * u).astype(bf_type)
            du_ah = du * ah
            dgain[span, :] += fold_lanes(du_ah)
            dshift[span, :] += fold_lanes(du)
            dah = gamma * du
            first.append(fold_rows(dah))
            second.append(fold_rows(gamma * du_ah))
            dnormed[span, :] = dah
        first = mean_of(first)
        second = mean_of(second)
        shifted = mean * scale
        for h in range(HEADS):
            span = spans[h]
            ah = num[span, :]
            rest = dnormed[span, :] - ah * second - first
            dnum_out[span, cols] = (rest * (scale * inverse[h])).astype(bf_type)
            inner = fold_rows(rest * ah) + shifted * fold_rows(rest)
            row = (h // 4) * 8 + h % 4
            dden[row : row + 1, :] = -jnp.sum(inner, axis=0, keepdims=True) * inverse[h]
        dden_out[:, cols] = dden[...]

    def backward(part):
        cols = slice(part * lanes, (part + 1) * lanes)
        table = members(ids.at[:, cols])
        stack, dden = back_stacks[part], ddens[part]
        for g in range(GROUPS):
            mine = dnum_out[g * half : (g + 1) * half, cols]
            for c in range(CLUSTERS):
                stack[g, c * half : (c + 1) * half, :] = mine * table[c : c + 1, :]
            den_rows = dden[g * 8 : g * 8 + 4, :]
            high = den_rows.astype(bf_type)
            low = (den_rows - high.astype(fl_type)).astype(bf_type)
            four_high = jnp.concatenate([high * table[c : c + 1, :] for c in range(CLUSTERS)], axis=0)
            four_low = jnp.concatenate([low * table[c : c + 1, :] for c in range(CLUSTERS)], axis=0)
            stack[g, CLUSTERS * half :, :] = jnp.concatenate([four_high, four_low], axis=0)
            acc[g] += dot_nt(stack[g], query[g * half : (g + 1) * half, cols])

    for part in range(parts):
        forward(part)
    for part in range(parts):
        norm(part)
        backward(part)

    @pl.when(step == steps - 1)
    def _():
        gain_row = jnp.sum(dgain[...].T, axis=0, keepdims=True)
        shift_row = jnp.sum(dshift[...].T, axis=0, keepdims=True)

        def extra(g, c):
            base = CLUSTERS * half
            row = jnp.zeros((1, half), fl_type)
            for h in range(4):
                at = base + c * 4 + h
                row = row + head_rows(half, h, acc[g, at : at + 1, :] + acc[g, at + 16 : at + 17, :])
            cols = slice(g * half, (g + 1) * half)
            tail = [row]
            if c == 0:
                tail += [gain_row[:, cols], shift_row[:, cols]]
            tail.append(jnp.zeros((PAD - len(tail), half), fl_type))
            return jnp.concatenate(tail, axis=0)

        put_chunks(acc, keep, send, node, extra)


def fold_rows(block):
    return tree_sum([block[i * 8 : (i + 1) * 8] for i in range(block.shape[0] // 8)])


def fold_lanes(block):
    return tree_sum([block[:, i * 128 : (i + 1) * 128] for i in range(block.shape[1] // 128)])


def write_pieces(pieces, node, shard, span, keep, send, blocks):
    for chunk in range(8):
        distance = lax.bitwise_xor(node, chunk)
        slot = lax.shift_right_logical(distance, 1)
        even = lax.bitwise_and(distance, 1) == 0
        for z in range(pieces):
            block = blocks(z, chunk)

            @pl.when(even)
            def _():
                keep[slot, z] = block

            @pl.when(jnp.logical_not(even))
            def _():
                send[slot, z] = block.astype(bf_type)


def query_back_kernel(step, place, ids, dnum, dden, query_slope, *refs):
    chunk_refs = refs[:CHUNKS]
    dquery_out = refs[CHUNKS]
    stage, left, sums, stack = refs[CHUNKS + 1 :]
    width, rows = dnum.shape
    half = width // GROUPS
    head = half // 4

    @pl.when(step == 0)
    def _():
        place_chunks(chunk_refs, place, stage)
        for gr in range(GROUPS):
            for c in range(CLUSTERS):
                chunk = stage[gr * CLUSTERS + c].astype(fl_type)
                for p in range(2):
                    cols = slice(c * 2 * head, (c + 1) * 2 * head)
                    left[gr * 2 + p, :, cols] = pair_block(chunk, p, head).T.astype(bf_type)
                column = chunk[head : head + 8].T
                sums[c, gr * half : (gr + 1) * half, :] = jnp.broadcast_to(column[:, 0:1], (half, 128))

    table = members(ids)
    for p in range(PAIRS):
        part = dnum[p * 2 * head : (p + 1) * 2 * head, :]
        for c in range(CLUSTERS):
            stack[p, c * 2 * head : (c + 1) * 2 * head, :] = part * table[c : c + 1, :]
        dq = dot_nn(left[p], stack[p])
        for h in range(2):
            at = slice((p * 2 + h) * head, (p * 2 + h + 1) * head)
            pick = pick_rows(sums, at, ids, rows)
            row = (p // 2) * 8 + (p % 2) * 2 + h
            full = dq[h * head : (h + 1) * head] + dden[row : row + 1, :] * pick
            dquery_out[at, :] = (full * query_slope[at, :]).astype(bf_type)


def grad_query_kernel(step, place, dquery, x, grad_query):
    @pl.when(step == 0)
    def _():
        grad_query[...] = jnp.zeros_like(grad_query)

    grad_query[...] += dot_nn(dquery[...], x[...])


def gate_back_kernel(step, place, dgate, prod, x, g, grad_gate, grad_out):
    @pl.when(step == 0)
    def _():
        grad_gate[...] = jnp.zeros_like(grad_gate)
        grad_out[...] = jnp.zeros_like(grad_out)

    grad_gate[...] += dot_nn(dgate[...], x[...])
    grad_out[...] += dot_nn(prod[...], g[...])


def out_part(grad_out, shard, z, chunk, which, span):
    lanes = grad_out.shape[1] // 4
    quarter = span // 4
    start = lax.bitwise_xor(shard, z) * span + (chunk % 2) * 2 * quarter + which * quarter
    rows = grad_out[pl.ds(pl.multiple_of(start, 8), quarter), (chunk // 2) * lanes : (chunk // 2 + 1) * lanes]
    return fold(rows, span)


def early_kernel(pieces, step, place, grad_query, grad_gate, grad_out, keep, send):
    node, shard = place[1], place[2]
    width = grad_out.shape[1]
    span = width // pieces
    tall = 2 * width // 8

    def blocks(z, chunk):
        source = grad_query if chunk < 4 else grad_gate
        top = source[(chunk % 4) * tall : (chunk % 4 + 1) * tall, z * span : (z + 1) * span]
        return jnp.concatenate([top, out_part(grad_out, shard, z, chunk, 1, span)], axis=0)

    write_pieces(pieces, node, shard, span, keep, send, blocks)


def fold(block, span):
    return jnp.concatenate(
        [block[:, i * span : (i + 1) * span] for i in range(block.shape[1] // span)], axis=0
    )


def pick_rows(sums, at, ids, rows):
    reps = rows // 128
    wide = [jnp.concatenate([sums[c, at, :]] * reps, axis=1) for c in range(CLUSTERS)]
    pick = wide[CLUSTERS - 1]
    for c in range(CLUSTERS - 1):
        pick = jnp.where(ids[...] == c, wide[c], pick)
    return pick


def output_kernel(step, place, x, prod, out_weight, result):
    result[...] = x[...].astype(fl_type) + dot_tn(prod[...], out_weight[...])


def key_back_kernel(pieces, step, place, ids, key_slope, key, value, x, grad_out, *refs):
    chunk_refs = refs[:CHUNKS]
    dkey_out, dvalue_out, norm_out, keep, send = refs[CHUNKS : CHUNKS + 5]
    stage, left_key, left_value, sums, stack, key_stack, acc = refs[CHUNKS + 5 :]
    node, shard, count = place[1], place[2], place[3]
    width, rows = value.shape
    half = width // GROUPS
    head = half // 4
    span = width // pieces

    @pl.when(step == 0)
    def _():
        place_chunks(chunk_refs, place, stage)
        for gr in range(GROUPS):
            for c in range(CLUSTERS):
                chunk = stage[gr * CLUSTERS + c].astype(fl_type)
                for p in range(2):
                    cols = slice(c * 2 * head, (c + 1) * 2 * head)
                    pair = pair_block(chunk, p, head)
                    left_value[gr * 2 + p, :, cols] = pair.astype(bf_type)
                    left_key[gr * 2 + p, :, cols] = pair.T.astype(bf_type)
                column = chunk[head : head + 8].T
                sums[c, gr * half : (gr + 1) * half, :] = jnp.broadcast_to(column[:, 0:1], (half, 128))
                if c == 0:
                    norm_out[:, gr * half : (gr + 1) * half] = chunk[head : head + 8]

    table = members(ids)
    valid = valid_row(count, step * rows, rows)
    for p in range(PAIRS):
        at = slice(p * 2 * head, (p + 1) * 2 * head)
        part = value[at, :]
        for c in range(CLUSTERS):
            stack[p % 2, c * 2 * head : (c + 1) * 2 * head, :] = part * table[c : c + 1, :]
        dk = dot_nn(left_key[p], stack[p % 2])
        for h in range(2):
            sub = slice((p * 2 + h) * head, (p * 2 + h + 1) * head)
            full = dk[h * head : (h + 1) * head] + pick_rows(sums, sub, ids, rows)
            dkey_out[sub, :] = (full * key_slope[sub, :]).astype(bf_type)
        part = key[at, :]
        for c in range(CLUSTERS):
            key_stack[p % 2, c * 2 * head : (c + 1) * 2 * head, :] = part * table[c : c + 1, :]
        dvalue_out[at, :] = dot_nn(left_value[p], key_stack[p % 2]).astype(bf_type)
    acc[0:width] = dot_nn(dkey_out[...], x[...])
    acc[width : 2 * width] = dot_nn(dvalue_out[...], x[...])

    tall = 2 * width // 8

    def blocks(z, chunk):
        top = acc[chunk * tall : (chunk + 1) * tall, z * span : (z + 1) * span]
        return jnp.concatenate([top, out_part(grad_out, shard, z, chunk, 0, span)], axis=0)

    write_pieces(pieces, node, shard, span, keep, send, blocks)


def input_kernel(steps, step, place, dquery, dkey, dvalue, dgate, full_query, full_key, full_gate, g, result, blocks, sems):
    rows, width = g.shape
    total = g[...].astype(fl_type)
    total = total + dot_tn(dquery[...], full_query[...])
    total = total + dot_tn(dkey[...], full_key[0:width, :])
    total = total + dot_tn(dvalue[...], full_key[width:, :])
    total = total + dot_tn(dgate[...], full_gate[...])
    blocks[step] = total

    def copy(i):
        at = pl.ds(pl.multiple_of(i * rows, 8), rows)
        return pltpu.make_async_copy(blocks.at[i], result.at[at, :], sems.at[i])

    copy(step).start()

    @pl.when(step == steps - 1)
    def _():
        for i in range(steps):
            copy(i).wait()


def finish_kernel(step, *refs):
    parts, sums = refs[:-1], refs[-1]
    sums[...] = tree_sum([p[...].astype(fl_type) for p in parts]).astype(bf_type)


def squares_kernel(step, *refs):
    parts, squares = refs[:-1], refs[-1]
    totals = []
    for part in parts:
        value = part[...].astype(fl_type)
        totals.append(fold_rows(value * value))
    total = jnp.sum(tree_sum(totals), axis=0, keepdims=True)
    squares[...] = jnp.broadcast_to(jnp.sum(total, axis=1, keepdims=True), squares.shape)


def assemble_kernel(step, place, *refs):
    parts, (grad_proj, grad_out, stage) = refs[:CHUNKS], refs[CHUNKS:]
    node = place[1]
    span, width = grad_out.shape
    tall = 2 * width // 8
    lanes = width // 4
    rows = span // 2
    folds = lanes // span
    for d in range(CHUNKS):
        chunk = lax.bitwise_xor(node, d)
        stage[chunk] = parts[d][...].astype(fl_type)
    rows = rows // 2
    late = tall + rows * folds
    for chunk in range(CHUNKS):
        query_at = (0 if chunk < 4 else 3 * width) + (chunk % 4) * tall
        grad_proj[:, width + chunk * tall : width + (chunk + 1) * tall] = stage[chunk, 0:tall].T
        grad_proj[:, query_at : query_at + tall] = stage[chunk, late : late + tall].T
        for which in range(2):
            for i in range(folds):
                at = slice((chunk // 2) * lanes + i * span, (chunk // 2) * lanes + (i + 1) * span)
                start = which * late + tall + i * rows
                row = (chunk % 2 * 2 + which) * rows
                grad_out[row : row + rows, at] = stage[chunk, start : start + rows]


def adam(master_w, moment_old, square_old, clipped, decay_coef, step_rate):
    moment_new = beta_one * moment_old + (1.0 - beta_one) * clipped
    square_new = beta_two * square_old + (1.0 - beta_two) * clipped * clipped
    moment_hat = moment_new * (1.0 / (1.0 - beta_one**STEP))
    square_hat = square_new * (1.0 / (1.0 - beta_two**STEP))
    master_new = master_w * (1.0 - step_rate * decay_coef) - step_rate * moment_hat / (
        jnp.sqrt(square_hat) + adam_eps
    )
    return moment_new, square_new, master_new


def update_kernel(pieces, step, place, *refs):
    squares, (gp, go, gn, pw, pm, ps, ow, om, osq, nw, nm, ns) = refs[:pieces], refs[pieces : pieces + 12]
    size, *results = refs[pieces + 12 : pieces + 25]
    p_out, o_out, n_out = results[0:4], results[4:8], results[8:12]
    new_p, new_pc, new_o, new_oc, new_n, sems = refs[pieces + 25 :]
    shard = place[2]
    span, width = ow.shape
    norm_grad = gn[1:3, :]
    norm_square = jnp.sum(norm_grad * norm_grad, axis=0, keepdims=True)
    total = tree_sum([q[0:1, 0:1] for q in squares]) + jnp.sum(norm_square, axis=1, keepdims=True)
    norm = jnp.sqrt(total)
    size[...] = norm
    clip_level = 0.5 * math.sqrt(5 * width * width + 2 * width)
    scale = jnp.minimum(1.0, clip_level / norm)
    copies = []

    def send(source, target):
        copies.append(pltpu.make_async_copy(source, target, sems.at[len(copies)]))
        copies[-1].start()

    scale = jnp.broadcast_to(scale, (1, width))

    def step_block(at, cols, w, m, s, grad, new, new_copy):
        results = adam(w[at, cols], m[at, cols], s[at, cols], grad[at, cols] * scale, decay_rate, learn_rate)
        for j, value in zip((2, 0, 1), (results[2], *results[:2])):
            new[j, at, :] = value
        new_copy[at, :] = results[2].astype(bf_type)

    blocks = [slice(r, r + 16) for r in range(0, span, 16)]
    for i in range(4):
        cols = slice(i * width, (i + 1) * width)
        for at in blocks:
            step_block(at, cols, pw, pm, ps, gp, new_p.at[:, i], new_pc.at[i])
        for j in range(3):
            send(new_p.at[j, i], p_out[j].at[:, cols])
        send(new_pc.at[i], p_out[3].at[:, cols])
    for at in blocks:
        step_block(at, slice(0, width), ow, om, osq, go, new_o, new_oc)
    for j in range(3):
        send(new_o.at[j], o_out[j])
    send(new_oc, o_out[3])
    mine = norm_grad[:, 0:span]
    for z in range(1, pieces):
        mine = jnp.where(shard == z, norm_grad[:, z * span : (z + 1) * span], mine)
    clipped = mine * scale[:, 0:span]
    for j, value in enumerate((clipped, *adam(nw[...], nm[...], ns[...], clipped, 0.0, norm_rate))):
        new_n[j] = value
        send(new_n.at[j], n_out[j])
    for copy in copies:
        copy.wait()


def make_exchange(nodes, shards):
    count = nodes * shards

    def exchange(value, node_bits, shard_bits):
        pairs = [
            (i, ((i // shards) ^ node_bits) * shards + ((i % shards) ^ shard_bits)) for i in range(count)
        ]
        return lax.ppermute(value, AXES, pairs)

    return exchange


def tree_sum(parts):
    parts = list(parts)
    while len(parts) > 1:
        pairs = [parts[i] + parts[i + 1] for i in range(0, len(parts) - 1, 2)]
        parts = pairs + parts[len(parts) - len(parts) % 2 :]
    return parts[0]


def to_float(parts):
    return [p.astype(fl_type) for p in parts]


def tie(value, *others):
    return lax.optimization_barrier((value, *others))[0]


def tie(value, *others):
    return lax.optimization_barrier((value, *others))[0]


def local(nodes, shards, *args):
    (x, g, ids, counts, pw, pm, ps, ow, om, osq, nw, nm, ns) = args
    exchange = make_exchange(nodes, shards)
    outer = nodes // 8
    rows, width = x.shape
    half = width // GROUPS
    head = width // HEADS
    span = pw.shape[0]
    block = min(1024, rows)
    steps = rows // block
    lanes = 256
    tall = 2 * width // 8
    part_rows = (3 * width + 2 + 127) // 128 * 16
    work = 2 * rows * width * width

    node = lax.axis_index("nodes").astype(jnp.int32)
    shard = lax.axis_index("shard").astype(jnp.int32)
    place = jnp.stack([lax.bitwise_and(node, 1), lax.bitwise_and(node, 7), shard, counts[0]])
    ids = ids.reshape(1, rows)
    chunk_shape = (4, head + PAD, half)

    def wide(dtype):
        return out((width, rows), dtype)

    def vmem(shape, dtype):
        return pltpu.VMEM(shape, dtype)

    message, kv_half, part, query_all = call(
        prep_kernel,
        1,
        (pw, ow, nw),
        ["hbm"] * 3,
        [
            out((width, span), bf_type),
            out((width, span), bf_type),
            out((part_rows, span), bf_type),
            out((8 * part_rows, span), bf_type),
        ],
        [None] * 4,
        [
            vmem((5, span, width), fl_type),
            vmem((2, span), fl_type),
            vmem((2, width, span), bf_type),
            pltpu.SemaphoreType.DMA((6,)),
        ],
        1e6,
        "prep",
        vmem=60,
    )
    x_turned = jnp.concatenate(
        [
            lax.dynamic_slice(x, (0, lax.bitwise_xor(shard, z) * span), (rows, span))
            for z in range(shards)
        ],
        axis=1,
    )
    mine, other = [message], [kv_half]
    for z in range(1, shards):
        late = z == 3
        mine.append(exchange(tie(message, x_turned) if late else message, 0, z))
    stack = jnp.stack([exchange(part, 0, z) for z in range(1, shards)])
    stacks = [stack] + [None] * 7
    for e in range(1, 4):
        stacks[2 * e] = exchange(stack, 2 * e, 0)
    for z in range(1, shards):
        other.append(exchange(mine[z], 1, 0))
    key_slope, key, value, keep, send = call(
        functools.partial(key_kernel, shards),
        1,
        (place, x_turned, ids, *mine, *other),
        ["smem", "row", "lane"] + [None] * (2 * shards),
        [wide(fl_type), wide(bf_type), wide(bf_type), out(chunk_shape, fl_type), out(chunk_shape, bf_type)],
        ["lane", "lane", "lane", None, None],
        [
            vmem((2 * width, width), bf_type),
            vmem((CLUSTERS * half + PAD, rows), bf_type),
            vmem((GROUPS, CLUSTERS * half + PAD, half), fl_type),
        ],
        1e3,
        "keys",
        rows,
        vmem=26,
    )

    def swap(pieces, peers, filler, cast=True):
        got = [exchange(p, *at) for p, at in zip(pieces, peers)]
        if filler is not None:
            done = filler(pieces[0])
            got = list(tie(tuple(got), done))
        return to_float(got) if cast else got

    plane = [(2 * e, 0) for e in range(1, 4)]
    along = [(0, z) for z in range(1, shards)]
    made = {}

    def reduce_chunks(keep, send, fillers):
        mine = keep + exchange(send, 1, 0).astype(fl_type)
        got = swap([mine[e].astype(bf_type) for e in range(1, 4)], plane, fillers[0])
        own = tree_sum([mine[0], *got]).astype(bf_type)
        got = swap([own] * (shards - 1), along, fillers[1])
        own = tree_sum([own.astype(fl_type), *got]).astype(bf_type)
        if outer > 1:
            got = swap([own] * (outer - 1), [(8 * o, 0) for o in range(1, outer)], None)
            own = tree_sum([own.astype(fl_type), *got]).astype(bf_type)
        return spread(own, fillers[2])

    def spread(own, filler=None):
        chunks = [own] + [None] * 7
        for e in range(1, 4):
            chunks[2 * e] = exchange(own, 2 * e, 0)
        chunks[1] = exchange(own, 1, 0)
        if filler is not None:
            done = filler(own)
            chunks[2], chunks[4], chunks[6] = tie((chunks[2], chunks[4], chunks[6]), done)
        for e in range(1, 4):
            chunks[2 * e + 1] = exchange(chunks[2 * e], 1, 0)
        return chunks

    def fill_weights(dep):
        made["weights"] = call(
            functools.partial(weights_kernel, shards),
            1,
            (tie(place, dep), query_all, *stacks),
            ["smem", None] + [None] * 8,
            [
                out((width, width), bf_type),
                out((width, width), bf_type),
                out((width, width), bf_type),
                out((width, 128), fl_type),
                out((width, 128), fl_type),
                out((width, width), bf_type),
                out((width, width), bf_type),
            ],
            [None] * 7,
            [vmem((shards, 8 * part_rows, span), bf_type)],
            1e6,
            "weights",
        )
        return made["weights"][0]

    def fill_query(dep):
        made["query"] = call(
            query_kernel,
            1,
            (tie(place, dep), x_turned, made["weights"][0]),
            ["smem", "row", None],
            [wide(fl_type), wide(bf_type)],
            ["lane"] * 2,
            [],
            work,
            "query",
            rows,
            vmem=16,
        )
        return made["query"][1], fill_gate(dep)

    def fill_gate(dep):
        gate_weight = made["weights"][1]
        made["gate"] = call(
            gate_kernel,
            1,
            (tie(place, dep), x_turned, gate_weight),
            ["smem", "row", None],
            [wide(fl_type)],
            ["lane"],
            [],
            work,
            "gate",
            rows,
            vmem=16,
        )[0]
        return made["gate"]

    def fill_grad_prod(dep):
        out_weight = made["weights"][2]
        made["grad_prod"] = call(
            grad_prod_kernel,
            1,
            (tie(place, dep), g, out_weight),
            ["smem", "row", None],
            [wide(fl_type)],
            ["lane"],
            [],
            work,
            "grad_prod",
            rows,
            vmem=16,
        )[0]
        return made["grad_prod"]

    send = tie(send, *stacks[2::2])
    for e in range(4):
        stacks[2 * e + 1] = exchange(stacks[2 * e], 1, 0)
    chunks = reduce_chunks(keep, send, (fill_weights, fill_query, fill_grad_prod))
    out_weight, gain, shift, full_query, full_gate = made["weights"][2:]
    query_slope, query = made["query"]

    parts = block // lanes
    prod, dgate, dnum, dden, keep, send = call(
        functools.partial(middle_kernel, steps, lanes),
        steps,
        (place, ids, query, made["gate"], made["grad_prod"], gain, shift, *chunks),
        ["smem", "lane", "lane", "lane", "lane", None, None] + [None] * CHUNKS,
        [
            wide(bf_type),
            wide(bf_type),
            wide(bf_type),
            out((16, rows), fl_type),
            out(chunk_shape, fl_type),
            out(chunk_shape, bf_type),
        ],
        ["lane", "lane", "lane", "lane", None, None],
        [
            vmem((CHUNKS, head + PAD, half), bf_type),
            vmem((PAIRS, 2 * head + PAD, CLUSTERS * 2 * head), bf_type),
            vmem((GROUPS, CLUSTERS * half + 32, half), fl_type),
            vmem((width, 128), fl_type),
            vmem((width, 128), fl_type),
        ]
        + [vmem((PAIRS, CLUSTERS * 2 * head, lanes), bf_type)] * parts
        + [vmem((GROUPS, CLUSTERS * half + 32, lanes), bf_type)] * parts
        + [vmem((width, lanes), fl_type)] * (3 * parts)
        + [vmem((16, lanes), fl_type)] * (2 * parts),
        6 * work,
        "middle",
        block,
    )

    short = tall + (span // 4) * (width // 4 // span)
    height = 2 * short
    early_shape = late_shape = (4, shards, short, span)

    def fill_gate_back(dep):
        made["gate_back"] = call(
            gate_back_kernel,
            1,
            (tie(place, dep), dgate, prod, x_turned, g),
            ["smem", "lane", "lane", "row", "row"],
            [out((width, width), fl_type)] * 2,
            [None] * 2,
            [],
            2 * work,
            "gate_back",
            rows,
            vmem=16,
        )
        return made["gate_back"][0]

    def fill_output(dep):
        made["output"] = call(
            output_kernel,
            steps,
            (tie(place, dep), x, prod, out_weight),
            ["smem", "row", "lane", None],
            [out((rows, width), fl_type)],
            ["row"],
            [],
            work,
            "output",
            block,
            piped=True,
        )[0]
        return made["output"]

    def fill_query_back(dep):
        made["dquery"] = call(
            query_back_kernel,
            1,
            (tie(place, dep), ids, dnum, dden, query_slope, *chunks),
            ["smem", "lane", "lane", "lane", "lane"] + [None] * CHUNKS,
            [wide(bf_type)],
            ["lane"],
            [
                vmem((CHUNKS, head + PAD, half), bf_type),
                vmem((PAIRS, 2 * head, CLUSTERS * 2 * head), bf_type),
                vmem((CLUSTERS, width, 128), fl_type),
                vmem((PAIRS, CLUSTERS * 2 * head, rows), bf_type),
            ],
            2 * work,
            "query_back",
            rows,
            vmem=26,
        )[0]
        return made["dquery"]

    def fill_grad_query(dep):
        made["grad_query"] = call(
            grad_query_kernel,
            1,
            (tie(place, dep), made["dquery"], x_turned),
            ["smem", None, None],
            [out((width, width), fl_type)],
            [None],
            [],
            work,
            "grad_query",
            vmem=12,
        )[0]
        made["early"] = call(
            functools.partial(early_kernel, shards),
            1,
            (place, made["grad_query"], *made["gate_back"]),
            ["smem"] + [None] * 3,
            [out(early_shape, fl_type), out(early_shape, bf_type)],
            [None] * 2,
            [],
            1e6,
            "early",
            vmem=8,
        )
        return made["early"][1]

    back_chunks = reduce_chunks(keep, send, (fill_gate_back, fill_query_back, fill_grad_query))
    dquery = made["dquery"]

    early_keep, early_send = made["early"]
    early_send = tie(early_send, *back_chunks[2::2])
    early_mine = early_keep + exchange(early_send, 1, 0).astype(fl_type)
    early_pieces = tie(tuple(early_mine[e].astype(bf_type) for e in range(1, 4)))
    early_got = [exchange(p, *at) for p, at in zip(early_pieces, plane)]
    dkey, dvalue, norm_grad, keep, send = call(
        functools.partial(key_back_kernel, shards),
        1,
        (place, ids, key_slope, key, value, x_turned, made["gate_back"][1], *back_chunks),
        ["smem", "lane", "lane", "lane", "lane", "row", None] + [None] * CHUNKS,
        [
            wide(bf_type),
            wide(bf_type),
            out((8, width), fl_type),
            out(late_shape, fl_type),
            out(late_shape, bf_type),
        ],
        ["lane", "lane", None, None, None],
        [
            vmem((CHUNKS, head + PAD, half), bf_type),
            vmem((PAIRS, 2 * head, CLUSTERS * 2 * head), bf_type),
            vmem((PAIRS, 2 * head, CLUSTERS * 2 * head), bf_type),
            vmem((CLUSTERS, width, 128), fl_type),
            vmem((2, CLUSTERS * 2 * head, rows), bf_type),
            vmem((2, CLUSTERS * 2 * head, rows), bf_type),
            vmem((2 * width, width), fl_type),
        ],
        6 * work,
        "key_back",
        rows,
        vmem=26,
    )

    full_key = call(
        functools.partial(key_weights_kernel, shards),
        1,
        (place, *mine, *other),
        ["smem"] + [None] * (2 * shards),
        [out((2 * width, width), bf_type)],
        [None],
        [vmem((shards, 2 * width, span), bf_type)],
        1e6,
        "key_weights",
        vmem=12,
    )[0]

    def fill_inputs(dep):
        made["inputs"] = call(
            functools.partial(input_kernel, 2),
            2,
            (tie(place, dep), dquery, dkey, dvalue, dgate, full_query, full_key, full_gate, g),
            ["smem"] + ["lane"] * 4 + [None] * 3 + ["row"],
            [out((rows, width), fl_type)],
            ["hbm"],
            [vmem((2, rows // 2, width), fl_type), pltpu.SemaphoreType.DMA((2,))],
            4 * work,
            "inputs",
            rows // 2,
        )[0]
        return made["inputs"]

    send = tie(send, *early_got)
    mine_sum = keep + exchange(send, 1, 0).astype(fl_type)
    early_sum = tree_sum([early_mine[0], *to_float(early_got)])
    pieces = tie(tuple(mine_sum[e].astype(bf_type) for e in range(1, 4)))
    got = swap(pieces, plane, fill_inputs)
    mine_sum = jnp.concatenate([tree_sum([mine_sum[0], *got]), early_sum], axis=1)
    pieces = tie(tuple(mine_sum[z].astype(bf_type) for z in range(1, shards)))
    owned_parts = [mine_sum[0], *swap(pieces, along, fill_output, cast=False)]
    if outer > 1:
        own = tree_sum(to_float(owned_parts)).astype(bf_type)
        got = [own] + [exchange(own, 8 * o, 0) for o in range(1, outer)]
        owned_parts = [tree_sum(to_float(got))] + [jnp.zeros_like(own)] * (shards - 1)

    sums = call(
        finish_kernel,
        1,
        owned_parts,
        [None] * shards,
        [out((height, span), bf_type)],
        [None],
        [],
        1e6,
        "finish",
        vmem=4,
    )[0]
    parts = spread(sums)
    squares = call(
        squares_kernel,
        1,
        parts,
        [None] * CHUNKS,
        [out((8, 128), fl_type)],
        [None],
        [],
        1e6,
        "squares",
        vmem=4,
    )[0]

    def fill_assemble(dep):
        made["grads"] = call(
            assemble_kernel,
            1,
            (tie(place, dep), *parts),
            ["smem"] + [None] * CHUNKS,
            [out((span, 4 * width), fl_type), out((span, width), fl_type)],
            [None] * 2,
            [vmem((CHUNKS, height, span), fl_type)],
            1e6,
            "assemble",
            vmem=8,
        )
        return made["grads"][0]

    squares = [squares, *swap([squares] * (shards - 1), along, fill_assemble)]
    states = (pw, pm, ps, ow, om, osq, nw, nm, ns)
    like = [pw] * 4 + [ow] * 4 + [nw] * 4
    kinds = [fl_type] * 3 + [bf_type] + [fl_type] * 3 + [bf_type] + [fl_type] * 4
    grad_size, *new = call(
        functools.partial(update_kernel, shards),
        1,
        (place, *squares, *made["grads"], norm_grad, *states),
        ["smem"] + [None] * (shards + 12),
        [out((1, 1), fl_type)] + [out(s.shape, k) for s, k in zip(like, kinds)],
        [None] + ["hbm"] * 12,
        [
            vmem((3, 4, span, width), fl_type),
            vmem((4, span, width), bf_type),
            vmem((3, span, width), fl_type),
            vmem((span, width), bf_type),
            vmem((4, 2, span), fl_type),
            pltpu.SemaphoreType.DMA((24,)),
        ],
        1e6,
        "update",
    )
    return (made["output"], made["inputs"], grad_size.reshape(1), *new)


def solution(mesh):
    nodes, shards = mesh.shape["nodes"], mesh.shape["shard"]
    by_node = P(AXES, None)
    rows = P("shard", None)
    cols = P(None, "shard")
    return jax.shard_map(
        functools.partial(local, nodes, shards),
        mesh=mesh,
        in_specs=(by_node, by_node, P(AXES), P(AXES)) + (rows,) * 6 + (cols,) * 3,
        out_specs=(by_node, by_node, P()) + (rows,) * 8 + (cols,) * 4,
        check_vma=False,
    )
```

```python
import functools
import math

import jax
import jax.numpy as jnp
from jax import lax
from jax.experimental import pallas as pl
from jax.experimental.pallas import tpu as pltpu
from jax.sharding import PartitionSpec as P

HEADS = 8
CLUSTERS = 4
STEP = 10
AXES = ("nodes", "shard")

norm_eps = 1e-05
beta_one = 0.9
beta_two = 0.999
learn_rate = 0.05
norm_rate = 0.5
decay_rate = 0.01
adam_eps = 1e-08
bf_type = jnp.bfloat16
fl_type = jnp.float32

GROUPS = 2
PAIRS = HEADS // 2
CHUNKS = GROUPS * CLUSTERS
PAD = 16


def dot_nn(a, b):
    return lax.dot_general(a, b, (((1,), (0,)), ((), ())), preferred_element_type=fl_type)


def dot_nt(a, b):
    return lax.dot_general(a, b, (((1,), (1,)), ((), ())), preferred_element_type=fl_type)


def dot_tn(a, b):
    return lax.dot_general(a, b, (((0,), (0,)), ((), ())), preferred_element_type=fl_type)


def whole(shape):
    return pl.BlockSpec(shape, lambda *_: (0,) * len(shape))


def smem():
    return pl.BlockSpec(memory_space=pltpu.SMEM)


def view(ref, kind, start, size):
    if kind == "lane":
        return ref.at[:, pl.ds(start, size)]
    if kind == "row":
        return ref.at[pl.ds(start, size), :]
    return ref


def call(kernel, steps, ins, in_kinds, outs, out_kinds, scratch, flops, name, block=0, vmem=16, piped=False):
    moved = sum(math.prod(a.shape) * a.dtype.itemsize for a in (*ins, *outs))
    arrays, kinds = [*ins, *outs], [*in_kinds, *out_kinds]

    def spec(array, kind):
        if kind == "smem":
            return smem()
        if kind == "hbm":
            return pl.BlockSpec(memory_space=pltpu.HBM)
        if isinstance(kind, pl.BlockSpec):
            return kind
        if piped and kind == "lane":
            return pl.BlockSpec((array.shape[0], block), lambda i: (0, i))
        if piped and kind == "row":
            return pl.BlockSpec((block, array.shape[1]), lambda i: (i, 0))
        return whole(array.shape)

    def body(*refs):
        if piped:
            kernel(pl.program_id(0), *refs)
            return
        if steps == 1:
            kernel(0, *refs)
            return

        def one(i, carry):
            start = pl.multiple_of(i * block, block)
            views = [view(r, k, start, block) for r, k in zip(refs, kinds)]
            kernel(i, *views, *refs[len(kinds) :])
            return carry

        lax.fori_loop(0, steps, one, 0)

    specs = [spec(a, k) for a, k in zip(arrays, kinds)]
    return pl.pallas_call(
        body,
        grid=(steps,) if piped else (),
        in_specs=specs[: len(ins)],
        out_specs=specs[len(ins) :],
        out_shape=outs,
        scratch_shapes=scratch,
        cost_estimate=pl.CostEstimate(flops=int(flops), transcendentals=0, bytes_accessed=int(moved)),
        compiler_params=pltpu.CompilerParams(vmem_limit_bytes=vmem * 1024 * 1024),
        name=name,
    )(*ins)


def out(shape, dtype):
    return jax.ShapeDtypeStruct(shape, dtype)


def fetch(copies):
    copies = [pltpu.make_async_copy(*c) for c in copies]
    for c in copies:
        c.start()
    return copies


def prep_kernel(step, wp, wo, wn, key_message, key_other, message, query_all, block, rows, stage, sems):
    core = lax.bitwise_and(lax.axis_index("nodes"), 1)
    part = lax.bitwise_and(lax.axis_index("nodes"), 7)
    shard, width = wo.shape
    columns = [wp.at[:, i * width : (i + 1) * width] for i in (1, 2, 0, 3)]
    sources = [*columns, wo]
    copies = fetch(
        [(sources[i], block.at[i], sems.at[i]) for i in range(5)] + [(wn, rows, sems.at[5])]
    )
    for i in range(2):
        copies[i].wait()
        stage[i] = block[i].T.astype(bf_type)
    key_message[...] = stage[core]
    key_other[...] = stage[1 - core]
    for i in range(3):
        copies[2 + i].wait()
        query_all[i * width : (i + 1) * width] = block[2 + i].T.astype(bf_type)
    copies[5].wait()
    rest = query_all.shape[0] - 3 * width
    tail = jnp.concatenate([rows[...], jnp.zeros((rest - 2, shard), fl_type)], axis=0)
    query_all[3 * width :] = tail.astype(bf_type)
    height = query_all.shape[0] // 8
    message[...] = query_all[pl.ds(pl.multiple_of(part * height, 16), height)]


def members(ids_ref):
    rows = ids_ref.shape[1]
    classes = lax.broadcasted_iota(jnp.int32, (PAD, rows), 0)
    return (classes == ids_ref[...]).astype(fl_type).astype(bf_type)


def valid_row(count, start, rows):
    slots = lax.broadcasted_iota(jnp.int32, (1, rows), 1) + start
    return slots < count


def put_chunks(acc, keep, send, node, extra):
    width = acc.shape[2]
    head = width // 4
    for g in range(GROUPS):
        for c in range(CLUSTERS):
            chunk = g * CLUSTERS + c
            distance = lax.bitwise_xor(node, chunk)
            slot = lax.shift_right_logical(distance, 1)
            lane_head = lax.broadcasted_iota(jnp.int32, (head, width), 1) // head
            body = jnp.zeros((head, width), fl_type)
            for h in range(4):
                rows = acc[g, c * width + h * head : c * width + (h + 1) * head, :]
                body = jnp.where(lane_head == h, rows, body)
            block = jnp.concatenate([body, extra(g, c)], axis=0)

            @pl.when(lax.bitwise_and(distance, 1) == 0)
            def _():
                keep[slot] = block

            @pl.when(lax.bitwise_and(distance, 1) == 1)
            def _():
                send[slot] = block.astype(bf_type)


def key_kernel(pieces, step, place, x, ids, *refs):
    mine, other = refs[:pieces], refs[pieces : 2 * pieces]
    key_slope, key_out, value_out, keep, send, weights, masked, acc = refs[2 * pieces :]
    core, node, count = place[0], place[1], place[3]
    width = x.shape[1]
    rows = x.shape[0]
    half = width // GROUPS

    span = mine[0].shape[1]
    for d in range(pieces):
        cols = slice(d * span, (d + 1) * span)
        weights[pl.ds(pl.multiple_of(core * width, 16), width), cols] = mine[d][...]
        weights[pl.ds(pl.multiple_of((1 - core) * width, 16), width), cols] = other[d][...]

    table = members(ids)
    valid = valid_row(count, step * rows, rows)
    for g in range(GROUPS):
        sig = jax.nn.sigmoid(dot_nt(weights[g * half : (g + 1) * half, :], x[...]))
        kept = jnp.where(valid, sig, 0.0)
        key_slope[g * half : (g + 1) * half, :] = kept * (1.0 - sig)
        keys = kept.astype(bf_type)
        key_out[g * half : (g + 1) * half, :] = keys
        value = dot_nt(weights[width + g * half : width + (g + 1) * half, :], x[...]).astype(bf_type)
        value_out[g * half : (g + 1) * half, :] = value
        for c in range(CLUSTERS):
            masked[c * half : (c + 1) * half, :] = value * table[c : c + 1, :]
        masked[CLUSTERS * half :, :] = table
        acc[g] = dot_nt(masked[...], keys)

    def extra(g, c):
        row = acc[g, CLUSTERS * half + c : CLUSTERS * half + c + 1, :]
        return jnp.concatenate([row, jnp.zeros((PAD - 1, half), fl_type)], axis=0)

    put_chunks(acc, keep, send, node, extra)


def weights_kernel(pieces, step, place, own, *refs):
    stacks = refs[:8]
    query_weight, gate_weight, out_weight, gain, shift, full_query, full_gate, stage = refs[8:]
    node, shard = place[1], place[2]
    width = out_weight.shape[0]
    span = own.shape[1]
    height = own.shape[0] // 8
    stage[0] = own[...]
    for position in range(8):
        where = pl.multiple_of(lax.bitwise_xor(node, position) * height, 16)
        for d in range(1, pieces):
            stage[d, pl.ds(where, height), :] = stacks[position][d - 1]
    norm_rows = []
    for z in range(pieces):
        where = lax.bitwise_xor(shard, z)
        cols = slice(z * span, (z + 1) * span)
        query_weight[:, cols] = stage[z, 0:width, :]
        gate_weight[:, cols] = stage[z, width : 2 * width, :]
        full_query[:, cols] = stage[where, 0:width, :]
        full_gate[:, cols] = stage[where, width : 2 * width, :]
        out_weight[cols, :] = stage[where, 2 * width : 3 * width, :].T
        norm_rows.append(stage[where, 3 * width : 3 * width + 16, :])
    turned = jnp.concatenate(norm_rows, axis=1).astype(fl_type).T
    gain[...] = jnp.broadcast_to(turned[:, 0:1], gain.shape)
    shift[...] = jnp.broadcast_to(turned[:, 1:2], shift.shape)


def key_weights_kernel(pieces, step, place, *refs):
    mine, other = refs[:pieces], refs[pieces : 2 * pieces]
    full, stage = refs[2 * pieces :]
    core = place[0]
    width, span = full.shape[1], mine[0].shape[1]
    for d in range(pieces):
        stage[d, pl.ds(pl.multiple_of(core * width, 16), width), :] = mine[d][0:width]
        stage[d, pl.ds(pl.multiple_of((1 - core) * width, 16), width), :] = other[d][0:width]
    for z in range(pieces):
        full[:, z * span : (z + 1) * span] = stage[lax.bitwise_xor(place[2], z)]


def query_kernel(step, place, x, weight, query_slope, query):
    sig = jax.nn.sigmoid(dot_nt(weight[...], x[...]))
    query_slope[...] = sig * (1.0 - sig)
    query[...] = sig.astype(bf_type)


def gate_kernel(step, place, x, weight, gate):
    rows = x.shape[0]
    valid = valid_row(place[3], step * rows, rows)
    gate[...] = jnp.where(valid, dot_nt(weight[...], x[...]), 0.0)


def grad_prod_kernel(step, place, g, out_weight, grad_prod):
    rows = g.shape[0]
    valid = valid_row(place[3], step * rows, rows)
    grad_prod[...] = jnp.where(valid, dot_nt(out_weight[...], g[...]), 0.0)


def place_chunks(chunk_refs, place, stage):
    node = place[1]
    for d in range(CHUNKS):
        stage[lax.bitwise_xor(node, d)] = chunk_refs[d][...]


def pair_rows(h, value):
    lane_head = lax.broadcasted_iota(jnp.int32, (1, value.shape[1]), 1) // (value.shape[1] // 2)
    return jnp.where(lane_head == h, value, jnp.zeros_like(value))


def pair_block(chunk, p, head):
    mine = chunk[:head, p * 2 * head : (p + 1) * 2 * head]
    return jnp.concatenate([pair_rows(0, mine), pair_rows(1, mine)], axis=0)


def head_rows(width, h, value):
    lane_head = lax.broadcasted_iota(jnp.int32, (1, width), 1) // (width // 4)
    return jnp.where(lane_head == h, value, jnp.zeros_like(value))


def middle_kernel(steps, lanes, step, place, ids, query, gate, grad_prod, gain, shift, *refs):
    chunk_refs = refs[:CHUNKS]
    prod_out, dgate_out, dnum_out, dden_out, keep, send = refs[CHUNKS : CHUNKS + 6]
    rest = refs[CHUNKS + 6 :]
    width, rows = query.shape
    parts = rows // lanes
    stage, left, acc, dgain, dshift = rest[:5]
    stacks, back_stacks, nums, normeds, dnormeds, dens, ddens = (
        rest[5 + i * parts : 5 + (i + 1) * parts] for i in range(7)
    )
    node, count = place[1], place[3]
    half = width // GROUPS
    head = half // 4

    @pl.when(step == 0)
    def _():
        place_chunks(chunk_refs, place, stage)
        for g in range(GROUPS):
            for c in range(CLUSTERS):
                chunk = stage[g * CLUSTERS + c].astype(fl_type)
                cols = slice(c * 2 * head, (c + 1) * 2 * head)
                for p in range(2):
                    mine = chunk[:, p * 2 * head : (p + 1) * 2 * head]
                    for h in range(2):
                        at = slice(h * head, (h + 1) * head)
                        left[g * 2 + p, at, cols] = pair_rows(h, mine[:head]).astype(bf_type)
                    sums = [pair_rows(h, mine[head : head + 1]) for h in range(2)]
                    sums.append(jnp.zeros((PAD - 2, 2 * head), fl_type))
                    left[g * 2 + p, 2 * head :, cols] = jnp.concatenate(sums, axis=0).astype(bf_type)
        acc[...] = jnp.zeros_like(acc)
        dgain[...] = jnp.zeros_like(dgain)
        dshift[...] = jnp.zeros_like(dshift)

    def forward(part):
        cols = slice(part * lanes, (part + 1) * lanes)
        table = members(ids.at[:, cols])
        stack, num, den = stacks[part], nums[part], dens[part]
        for p in range(PAIRS):
            at = slice(p * 2 * head, (p + 1) * 2 * head)
            mine = query[at, cols]
            for c in range(CLUSTERS):
                stack[p, c * 2 * head : (c + 1) * 2 * head, :] = mine * table[c : c + 1, :]
            both = dot_nn(left[p], stack[p])
            num[at, :] = both[: 2 * head]
            row = (p // 2) * 8 + (p % 2) * 2
            den[row : row + 2, :] = 1.0 / both[2 * head : 2 * head + 2]

    def norm(part):
        cols = slice(part * lanes, (part + 1) * lanes)
        num, dnormed, den, dden = nums[part], dnormeds[part], dens[part], ddens[part]
        spans = [slice(h * head, (h + 1) * head) for h in range(HEADS)]
        inverse = [den[(h // 4) * 8 + h % 4 : (h // 4) * 8 + h % 4 + 1, :] for h in range(HEADS)]

        def mean_of(blocks):
            return jnp.sum(tree_sum(blocks), axis=0, keepdims=True) * (1.0 / width)

        mean = mean_of([fold_rows(num[spans[h], :]) * inverse[h] for h in range(HEADS)])
        squares = []
        for h in range(HEADS):
            centered = num[spans[h], :] * inverse[h] - mean
            num[spans[h], :] = centered
            squares.append(fold_rows(centered * centered))
        scale = lax.rsqrt(mean_of(squares) + norm_eps)
        first, second = [], []
        for h in range(HEADS):
            span = spans[h]
            ah = num[span, :] * scale
            num[span, :] = ah
            gamma = jnp.concatenate([gain[span, :]] * (lanes // 128), axis=1)
            beta = jnp.concatenate([shift[span, :]] * (lanes // 128), axis=1)
            u = ah * gamma + beta
            zg = gate[span, cols]
            dp = grad_prod[span, cols]
            prod_out[span, cols] = (u * zg).astype(bf_type)
            du = dp * zg
            dgate_out[span, cols] = (dp * u).astype(bf_type)
            du_ah = du * ah
            dgain[span, :] += fold_lanes(du_ah)
            dshift[span, :] += fold_lanes(du)
            dah = gamma * du
            first.append(fold_rows(dah))
            second.append(fold_rows(gamma * du_ah))
            dnormed[span, :] = dah
        first = mean_of(first)
        second = mean_of(second)
        shifted = mean * scale
        for h in range(HEADS):
            span = spans[h]
            ah = num[span, :]
            rest = dnormed[span, :] - ah * second - first
            dnum_out[span, cols] = (rest * (scale * inverse[h])).astype(bf_type)
            inner = fold_rows(rest * ah) + shifted * fold_rows(rest)
            row = (h // 4) * 8 + h % 4
            dden[row : row + 1, :] = -jnp.sum(inner, axis=0, keepdims=True) * inverse[h]
        dden_out[:, cols] = dden[...]

    def backward(part):
        cols = slice(part * lanes, (part + 1) * lanes)
        table = members(ids.at[:, cols])
        stack, dden = back_stacks[part], ddens[part]
        for g in range(GROUPS):
            mine = dnum_out[g * half : (g + 1) * half, cols]
            for c in range(CLUSTERS):
                stack[g, c * half : (c + 1) * half, :] = mine * table[c : c + 1, :]
            den_rows = dden[g * 8 : g * 8 + 4, :]
            high = den_rows.astype(bf_type)
            low = (den_rows - high.astype(fl_type)).astype(bf_type)
            four_high = jnp.concatenate([high * table[c : c + 1, :] for c in range(CLUSTERS)], axis=0)
            four_low = jnp.concatenate([low * table[c : c + 1, :] for c in range(CLUSTERS)], axis=0)
            stack[g, CLUSTERS * half :, :] = jnp.concatenate([four_high, four_low], axis=0)
            acc[g] += dot_nt(stack[g], query[g * half : (g + 1) * half, cols])

    for part in range(parts):
        forward(part)
    for part in range(parts):
        norm(part)
        backward(part)

    @pl.when(step == steps - 1)
    def _():
        gain_row = jnp.sum(dgain[...].T, axis=0, keepdims=True)
        shift_row = jnp.sum(dshift[...].T, axis=0, keepdims=True)

        def extra(g, c):
            base = CLUSTERS * half
            row = jnp.zeros((1, half), fl_type)
            for h in range(4):
                at = base + c * 4 + h
                row = row + head_rows(half, h, acc[g, at : at + 1, :] + acc[g, at + 16 : at + 17, :])
            cols = slice(g * half, (g + 1) * half)
            tail = [row]
            if c == 0:
                tail += [gain_row[:, cols], shift_row[:, cols]]
            tail.append(jnp.zeros((PAD - len(tail), half), fl_type))
            return jnp.concatenate(tail, axis=0)

        put_chunks(acc, keep, send, node, extra)


def fold_rows(block):
    return tree_sum([block[i * 8 : (i + 1) * 8] for i in range(block.shape[0] // 8)])


def fold_lanes(block):
    return tree_sum([block[:, i * 128 : (i + 1) * 128] for i in range(block.shape[1] // 128)])


def write_pieces(pieces, node, shard, span, keep, send, blocks):
    for chunk in range(8):
        distance = lax.bitwise_xor(node, chunk)
        slot = lax.shift_right_logical(distance, 1)
        even = lax.bitwise_and(distance, 1) == 0
        for z in range(pieces):
            block = blocks(z, chunk)

            @pl.when(even)
            def _():
                keep[slot, z] = block

            @pl.when(jnp.logical_not(even))
            def _():
                send[slot, z] = block.astype(bf_type)


def query_back_kernel(step, place, ids, dnum, dden, query_slope, *refs):
    chunk_refs = refs[:CHUNKS]
    dquery_out = refs[CHUNKS]
    stage, left, sums, stack = refs[CHUNKS + 1 :]
    width, rows = dnum.shape
    half = width // GROUPS
    head = half // 4

    @pl.when(step == 0)
    def _():
        place_chunks(chunk_refs, place, stage)
        for gr in range(GROUPS):
            for c in range(CLUSTERS):
                chunk = stage[gr * CLUSTERS + c].astype(fl_type)
                for p in range(2):
                    cols = slice(c * 2 * head, (c + 1) * 2 * head)
                    left[gr * 2 + p, :, cols] = pair_block(chunk, p, head).T.astype(bf_type)
                column = chunk[head : head + 8].T
                sums[c, gr * half : (gr + 1) * half, :] = jnp.broadcast_to(column[:, 0:1], (half, 128))

    table = members(ids)
    for p in range(PAIRS):
        part = dnum[p * 2 * head : (p + 1) * 2 * head, :]
        for c in range(CLUSTERS):
            stack[p, c * 2 * head : (c + 1) * 2 * head, :] = part * table[c : c + 1, :]
        dq = dot_nn(left[p], stack[p])
        for h in range(2):
            at = slice((p * 2 + h) * head, (p * 2 + h + 1) * head)
            pick = pick_rows(sums, at, ids, rows)
            row = (p // 2) * 8 + (p % 2) * 2 + h
            full = dq[h * head : (h + 1) * head] + dden[row : row + 1, :] * pick
            dquery_out[at, :] = (full * query_slope[at, :]).astype(bf_type)


def grad_query_kernel(step, place, dquery, x, grad_query):
    @pl.when(step == 0)
    def _():
        grad_query[...] = jnp.zeros_like(grad_query)

    grad_query[...] += dot_nn(dquery[...], x[...])


def gate_back_kernel(step, place, dgate, prod, x, g, grad_gate, grad_out):
    @pl.when(step == 0)
    def _():
        grad_gate[...] = jnp.zeros_like(grad_gate)
        grad_out[...] = jnp.zeros_like(grad_out)

    grad_gate[...] += dot_nn(dgate[...], x[...])
    grad_out[...] += dot_nn(prod[...], g[...])


def out_part(grad_out, shard, z, chunk, which, span):
    lanes = grad_out.shape[1] // 4
    quarter = span // 4
    start = lax.bitwise_xor(shard, z) * span + (chunk % 2) * 2 * quarter + which * quarter
    rows = grad_out[pl.ds(pl.multiple_of(start, 8), quarter), (chunk // 2) * lanes : (chunk // 2 + 1) * lanes]
    return fold(rows, span)


def early_kernel(pieces, step, place, grad_query, grad_gate, grad_out, keep, send):
    node, shard = place[1], place[2]
    width = grad_out.shape[1]
    span = width // pieces
    tall = 2 * width // 8

    def blocks(z, chunk):
        source = grad_query if chunk < 4 else grad_gate
        top = source[(chunk % 4) * tall : (chunk % 4 + 1) * tall, z * span : (z + 1) * span]
        return jnp.concatenate([top, out_part(grad_out, shard, z, chunk, 1, span)], axis=0)

    write_pieces(pieces, node, shard, span, keep, send, blocks)


def fold(block, span):
    return jnp.concatenate(
        [block[:, i * span : (i + 1) * span] for i in range(block.shape[1] // span)], axis=0
    )


def pick_rows(sums, at, ids, rows):
    reps = rows // 128
    wide = [jnp.concatenate([sums[c, at, :]] * reps, axis=1) for c in range(CLUSTERS)]
    pick = wide[CLUSTERS - 1]
    for c in range(CLUSTERS - 1):
        pick = jnp.where(ids[...] == c, wide[c], pick)
    return pick


def output_kernel(step, place, x, prod, out_weight, result):
    result[...] = x[...].astype(fl_type) + dot_tn(prod[...], out_weight[...])


def key_back_kernel(pieces, step, place, ids, key_slope, key, value, x, grad_out, *refs):
    chunk_refs = refs[:CHUNKS]
    dkey_out, dvalue_out, norm_out, keep, send = refs[CHUNKS : CHUNKS + 5]
    stage, left_key, left_value, sums, stack, key_stack, acc = refs[CHUNKS + 5 :]
    node, shard, count = place[1], place[2], place[3]
    width, rows = value.shape
    half = width // GROUPS
    head = half // 4
    span = width // pieces

    @pl.when(step == 0)
    def _():
        place_chunks(chunk_refs, place, stage)
        for gr in range(GROUPS):
            for c in range(CLUSTERS):
                chunk = stage[gr * CLUSTERS + c].astype(fl_type)
                for p in range(2):
                    cols = slice(c * 2 * head, (c + 1) * 2 * head)
                    pair = pair_block(chunk, p, head)
                    left_value[gr * 2 + p, :, cols] = pair.astype(bf_type)
                    left_key[gr * 2 + p, :, cols] = pair.T.astype(bf_type)
                column = chunk[head : head + 8].T
                sums[c, gr * half : (gr + 1) * half, :] = jnp.broadcast_to(column[:, 0:1], (half, 128))
                if c == 0:
                    norm_out[:, gr * half : (gr + 1) * half] = chunk[head : head + 8]

    table = members(ids)
    valid = valid_row(count, step * rows, rows)
    for p in range(PAIRS):
        at = slice(p * 2 * head, (p + 1) * 2 * head)
        part = value[at, :]
        for c in range(CLUSTERS):
            stack[p % 2, c * 2 * head : (c + 1) * 2 * head, :] = part * table[c : c + 1, :]
        dk = dot_nn(left_key[p], stack[p % 2])
        for h in range(2):
            sub = slice((p * 2 + h) * head, (p * 2 + h + 1) * head)
            full = dk[h * head : (h + 1) * head] + pick_rows(sums, sub, ids, rows)
            dkey_out[sub, :] = (full * key_slope[sub, :]).astype(bf_type)
        part = key[at, :]
        for c in range(CLUSTERS):
            key_stack[p % 2, c * 2 * head : (c + 1) * 2 * head, :] = part * table[c : c + 1, :]
        dvalue_out[at, :] = dot_nn(left_value[p], key_stack[p % 2]).astype(bf_type)
    acc[0:width] = dot_nn(dkey_out[...], x[...])
    acc[width : 2 * width] = dot_nn(dvalue_out[...], x[...])

    tall = 2 * width // 8

    def blocks(z, chunk):
        top = acc[chunk * tall : (chunk + 1) * tall, z * span : (z + 1) * span]
        return jnp.concatenate([top, out_part(grad_out, shard, z, chunk, 0, span)], axis=0)

    write_pieces(pieces, node, shard, span, keep, send, blocks)


def input_kernel(steps, step, place, dquery, dkey, dvalue, dgate, full_query, full_key, full_gate, g, result, blocks, sems):
    rows, width = g.shape
    total = g[...].astype(fl_type)
    total = total + dot_tn(dquery[...], full_query[...])
    total = total + dot_tn(dkey[...], full_key[0:width, :])
    total = total + dot_tn(dvalue[...], full_key[width:, :])
    total = total + dot_tn(dgate[...], full_gate[...])
    blocks[step] = total

    def copy(i):
        at = pl.ds(pl.multiple_of(i * rows, 8), rows)
        return pltpu.make_async_copy(blocks.at[i], result.at[at, :], sems.at[i])

    copy(step).start()

    @pl.when(step == steps - 1)
    def _():
        for i in range(steps):
            copy(i).wait()


def finish_kernel(step, *refs):
    parts, sums = refs[:-1], refs[-1]
    sums[...] = tree_sum([p[...].astype(fl_type) for p in parts]).astype(bf_type)


def squares_kernel(step, *refs):
    parts, squares = refs[:-1], refs[-1]
    totals = []
    for part in parts:
        value = part[...].astype(fl_type)
        totals.append(fold_rows(value * value))
    total = jnp.sum(tree_sum(totals), axis=0, keepdims=True)
    squares[...] = jnp.broadcast_to(jnp.sum(total, axis=1, keepdims=True), squares.shape)


def assemble_kernel(step, place, *refs):
    parts, (grad_proj, grad_out, stage) = refs[:CHUNKS], refs[CHUNKS:]
    node = place[1]
    span, width = grad_out.shape
    tall = 2 * width // 8
    lanes = width // 4
    rows = span // 2
    folds = lanes // span
    for d in range(CHUNKS):
        chunk = lax.bitwise_xor(node, d)
        stage[chunk] = parts[d][...].astype(fl_type)
    rows = rows // 2
    late = tall + rows * folds
    for chunk in range(CHUNKS):
        query_at = (0 if chunk < 4 else 3 * width) + (chunk % 4) * tall
        grad_proj[:, width + chunk * tall : width + (chunk + 1) * tall] = stage[chunk, 0:tall].T
        grad_proj[:, query_at : query_at + tall] = stage[chunk, late : late + tall].T
        for which in range(2):
            for i in range(folds):
                at = slice((chunk // 2) * lanes + i * span, (chunk // 2) * lanes + (i + 1) * span)
                start = which * late + tall + i * rows
                row = (chunk % 2 * 2 + which) * rows
                grad_out[row : row + rows, at] = stage[chunk, start : start + rows]


def adam(master_w, moment_old, square_old, clipped, decay_coef, step_rate):
    moment_new = beta_one * moment_old + (1.0 - beta_one) * clipped
    square_new = beta_two * square_old + (1.0 - beta_two) * clipped * clipped
    moment_hat = moment_new * (1.0 / (1.0 - beta_one**STEP))
    square_hat = square_new * (1.0 / (1.0 - beta_two**STEP))
    master_new = master_w * (1.0 - step_rate * decay_coef) - step_rate * moment_hat / (
        jnp.sqrt(square_hat) + adam_eps
    )
    return moment_new, square_new, master_new


def update_kernel(pieces, step, place, *refs):
    squares, (gp, go, gn, pw, pm, ps, ow, om, osq, nw, nm, ns) = refs[:pieces], refs[pieces : pieces + 12]
    size, *results = refs[pieces + 12 : pieces + 25]
    p_out, o_out, n_out = results[0:4], results[4:8], results[8:12]
    new_p, new_pc, new_o, new_oc, new_n, sems = refs[pieces + 25 :]
    shard = place[2]
    span, width = ow.shape
    norm_grad = gn[1:3, :]
    norm_square = jnp.sum(norm_grad * norm_grad, axis=0, keepdims=True)
    total = tree_sum([q[0:1, 0:1] for q in squares]) + jnp.sum(norm_square, axis=1, keepdims=True)
    norm = jnp.sqrt(total)
    size[...] = norm
    clip_level = 0.5 * math.sqrt(5 * width * width + 2 * width)
    scale = jnp.minimum(1.0, clip_level / norm)
    copies = []

    def send(source, target):
        copies.append(pltpu.make_async_copy(source, target, sems.at[len(copies)]))
        copies[-1].start()

    scale = jnp.broadcast_to(scale, (1, width))

    def step_block(at, cols, w, m, s, grad, new, new_copy):
        results = adam(w[at, cols], m[at, cols], s[at, cols], grad[at, cols] * scale, decay_rate, learn_rate)
        for j, value in zip((2, 0, 1), (results[2], *results[:2])):
            new[j, at, :] = value
        new_copy[at, :] = results[2].astype(bf_type)

    blocks = [slice(r, r + 16) for r in range(0, span, 16)]
    for i in range(4):
        cols = slice(i * width, (i + 1) * width)
        for at in blocks:
            step_block(at, cols, pw, pm, ps, gp, new_p.at[:, i], new_pc.at[i])
        for j in range(3):
            send(new_p.at[j, i], p_out[j].at[:, cols])
        send(new_pc.at[i], p_out[3].at[:, cols])
    for at in blocks:
        step_block(at, slice(0, width), ow, om, osq, go, new_o, new_oc)
    for j in range(3):
        send(new_o.at[j], o_out[j])
    send(new_oc, o_out[3])
    mine = norm_grad[:, 0:span]
    for z in range(1, pieces):
        mine = jnp.where(shard == z, norm_grad[:, z * span : (z + 1) * span], mine)
    clipped = mine * scale[:, 0:span]
    for j, value in enumerate((clipped, *adam(nw[...], nm[...], ns[...], clipped, 0.0, norm_rate))):
        new_n[j] = value
        send(new_n.at[j], n_out[j])
    for copy in copies:
        copy.wait()


def make_exchange(nodes, shards):
    count = nodes * shards

    def exchange(value, node_bits, shard_bits):
        pairs = [
            (i, ((i // shards) ^ node_bits) * shards + ((i % shards) ^ shard_bits)) for i in range(count)
        ]
        return lax.ppermute(value, AXES, pairs)

    return exchange


def tree_sum(parts):
    parts = list(parts)
    while len(parts) > 1:
        pairs = [parts[i] + parts[i + 1] for i in range(0, len(parts) - 1, 2)]
        parts = pairs + parts[len(parts) - len(parts) % 2 :]
    return parts[0]


def to_float(parts):
    return [p.astype(fl_type) for p in parts]


def tie(value, *others):
    return lax.optimization_barrier((value, *others))[0]


def tie(value, *others):
    return lax.optimization_barrier((value, *others))[0]


def local(nodes, shards, *args):
    (x, g, ids, counts, pw, pm, ps, ow, om, osq, nw, nm, ns) = args
    exchange = make_exchange(nodes, shards)
    outer = nodes // 8
    rows, width = x.shape
    half = width // GROUPS
    head = width // HEADS
    span = pw.shape[0]
    block = min(1024, rows)
    steps = rows // block
    lanes = 256
    tall = 2 * width // 8
    part_rows = (3 * width + 2 + 127) // 128 * 16
    work = 2 * rows * width * width

    node = lax.axis_index("nodes").astype(jnp.int32)
    shard = lax.axis_index("shard").astype(jnp.int32)
    place = jnp.stack([lax.bitwise_and(node, 1), lax.bitwise_and(node, 7), shard, counts[0]])
    ids = ids.reshape(1, rows)
    chunk_shape = (4, head + PAD, half)

    def wide(dtype):
        return out((width, rows), dtype)

    def vmem(shape, dtype):
        return pltpu.VMEM(shape, dtype)

    message, kv_half, part, query_all = call(
        prep_kernel,
        1,
        (pw, ow, nw),
        ["hbm"] * 3,
        [
            out((width, span), bf_type),
            out((width, span), bf_type),
            out((part_rows, span), bf_type),
            out((8 * part_rows, span), bf_type),
        ],
        [None] * 4,
        [
            vmem((5, span, width), fl_type),
            vmem((2, span), fl_type),
            vmem((2, width, span), bf_type),
            pltpu.SemaphoreType.DMA((6,)),
        ],
        1e6,
        "prep",
        vmem=60,
    )
    x_turned = jnp.concatenate(
        [
            lax.dynamic_slice(x, (0, lax.bitwise_xor(shard, z) * span), (rows, span))
            for z in range(shards)
        ],
        axis=1,
    )
    mine, other = [message], [kv_half]
    for z in range(1, shards):
        late = z == 3
        mine.append(exchange(tie(message, x_turned) if late else message, 0, z))
    stack = jnp.stack([exchange(part, 0, z) for z in range(1, shards)])
    stacks = [stack] + [None] * 7
    for e in range(1, 4):
        stacks[2 * e] = exchange(stack, 2 * e, 0)
    for z in range(1, shards):
        other.append(exchange(mine[z], 1, 0))
    key_slope, key, value, keep, send = call(
        functools.partial(key_kernel, shards),
        1,
        (place, x_turned, ids, *mine, *other),
        ["smem", "row", "lane"] + [None] * (2 * shards),
        [wide(fl_type), wide(bf_type), wide(bf_type), out(chunk_shape, fl_type), out(chunk_shape, bf_type)],
        ["lane", "lane", "lane", None, None],
        [
            vmem((2 * width, width), bf_type),
            vmem((CLUSTERS * half + PAD, rows), bf_type),
            vmem((GROUPS, CLUSTERS * half + PAD, half), fl_type),
        ],
        1e3,
        "keys",
        rows,
        vmem=26,
    )

    def swap(pieces, peers, filler, cast=True):
        got = [exchange(p, *at) for p, at in zip(pieces, peers)]
        if filler is not None:
            done = filler(pieces[0])
            got = list(tie(tuple(got), done))
        return to_float(got) if cast else got

    plane = [(2 * e, 0) for e in range(1, 4)]
    along = [(0, z) for z in range(1, shards)]
    made = {}

    def reduce_chunks(keep, send, fillers):
        mine = keep + exchange(send, 1, 0).astype(fl_type)
        got = swap([mine[e].astype(bf_type) for e in range(1, 4)], plane, fillers[0])
        own = tree_sum([mine[0], *got]).astype(bf_type)
        got = swap([own] * (shards - 1), along, fillers[1])
        own = tree_sum([own.astype(fl_type), *got]).astype(bf_type)
        if outer > 1:
            got = swap([own] * (outer - 1), [(8 * o, 0) for o in range(1, outer)], None)
            own = tree_sum([own.astype(fl_type), *got]).astype(bf_type)
        return spread(own, fillers[2])

    def spread(own, filler=None):
        chunks = [own] + [None] * 7
        for e in range(1, 4):
            chunks[2 * e] = exchange(own, 2 * e, 0)
        chunks[1] = exchange(own, 1, 0)
        if filler is not None:
            done = filler(own)
            chunks[2], chunks[4], chunks[6] = tie((chunks[2], chunks[4], chunks[6]), done)
        for e in range(1, 4):
            chunks[2 * e + 1] = exchange(chunks[2 * e], 1, 0)
        return chunks

    def fill_weights(dep):
        made["weights"] = call(
            functools.partial(weights_kernel, shards),
            1,
            (tie(place, dep), query_all, *stacks),
            ["smem", None] + [None] * 8,
            [
                out((width, width), bf_type),
                out((width, width), bf_type),
                out((width, width), bf_type),
                out((width, 128), fl_type),
                out((width, 128), fl_type),
                out((width, width), bf_type),
                out((width, width), bf_type),
            ],
            [None] * 7,
            [vmem((shards, 8 * part_rows, span), bf_type)],
            1e6,
            "weights",
        )
        return fill_query(dep)

    def fill_query(dep):
        made["query"] = call(
            query_kernel,
            1,
            (tie(place, dep), x_turned, made["weights"][0]),
            ["smem", "row", None],
            [wide(fl_type), wide(bf_type)],
            ["lane"] * 2,
            [],
            work,
            "query",
            rows,
            vmem=16,
        )
        return made["query"][1]

    def fill_gate(dep):
        gate_weight = made["weights"][1]
        made["gate"] = call(
            gate_kernel,
            1,
            (tie(place, dep), x_turned, gate_weight),
            ["smem", "row", None],
            [wide(fl_type)],
            ["lane"],
            [],
            work,
            "gate",
            rows,
            vmem=16,
        )[0]
        return made["gate"]

    def fill_grad_prod(dep):
        out_weight = made["weights"][2]
        made["grad_prod"] = call(
            grad_prod_kernel,
            1,
            (tie(place, dep), g, out_weight),
            ["smem", "row", None],
            [wide(fl_type)],
            ["lane"],
            [],
            work,
            "grad_prod",
            rows,
            vmem=16,
        )[0]
        return made["grad_prod"]

    send = tie(send, *stacks[2::2])
    for e in range(4):
        stacks[2 * e + 1] = exchange(stacks[2 * e], 1, 0)
    chunks = reduce_chunks(keep, send, (fill_weights, fill_gate, fill_grad_prod))
    out_weight, gain, shift, full_query, full_gate = made["weights"][2:]
    query_slope, query = made["query"]

    parts = block // lanes
    prod, dgate, dnum, dden, keep, send = call(
        functools.partial(middle_kernel, steps, lanes),
        steps,
        (place, ids, query, made["gate"], made["grad_prod"], gain, shift, *chunks),
        ["smem", "lane", "lane", "lane", "lane", None, None] + [None] * CHUNKS,
        [
            wide(bf_type),
            wide(bf_type),
            wide(bf_type),
            out((16, rows), fl_type),
            out(chunk_shape, fl_type),
            out(chunk_shape, bf_type),
        ],
        ["lane", "lane", "lane", "lane", None, None],
        [
            vmem((CHUNKS, head + PAD, half), bf_type),
            vmem((PAIRS, 2 * head + PAD, CLUSTERS * 2 * head), bf_type),
            vmem((GROUPS, CLUSTERS * half + 32, half), fl_type),
            vmem((width, 128), fl_type),
            vmem((width, 128), fl_type),
        ]
        + [vmem((PAIRS, CLUSTERS * 2 * head, lanes), bf_type)] * parts
        + [vmem((GROUPS, CLUSTERS * half + 32, lanes), bf_type)] * parts
        + [vmem((width, lanes), fl_type)] * (3 * parts)
        + [vmem((16, lanes), fl_type)] * (2 * parts),
        6 * work,
        "middle",
        block,
    )

    short = tall + (span // 4) * (width // 4 // span)
    height = 2 * short
    early_shape = late_shape = (4, shards, short, span)

    def fill_gate_back(dep):
        made["gate_back"] = call(
            gate_back_kernel,
            1,
            (tie(place, dep), dgate, prod, x_turned, g),
            ["smem", "lane", "lane", "row", "row"],
            [out((width, width), fl_type)] * 2,
            [None] * 2,
            [],
            2 * work,
            "gate_back",
            rows,
            vmem=16,
        )
        return made["gate_back"][0]

    def fill_output(dep):
        made["output"] = call(
            output_kernel,
            steps,
            (tie(place, dep), x, prod, out_weight),
            ["smem", "row", "lane", None],
            [out((rows, width), fl_type)],
            ["row"],
            [],
            work,
            "output",
            block,
            piped=True,
        )[0]
        return made["output"]

    def fill_query_back(dep):
        made["dquery"] = call(
            query_back_kernel,
            1,
            (tie(place, dep), ids, dnum, dden, query_slope, *chunks),
            ["smem", "lane", "lane", "lane", "lane"] + [None] * CHUNKS,
            [wide(bf_type)],
            ["lane"],
            [
                vmem((CHUNKS, head + PAD, half), bf_type),
                vmem((PAIRS, 2 * head, CLUSTERS * 2 * head), bf_type),
                vmem((CLUSTERS, width, 128), fl_type),
                vmem((PAIRS, CLUSTERS * 2 * head, rows), bf_type),
            ],
            2 * work,
            "query_back",
            rows,
            vmem=26,
        )[0]
        return made["dquery"]

    def fill_grad_query(dep):
        made["grad_query"] = call(
            grad_query_kernel,
            1,
            (tie(place, dep), made["dquery"], x_turned),
            ["smem", None, None],
            [out((width, width), fl_type)],
            [None],
            [],
            work,
            "grad_query",
            vmem=12,
        )[0]
        made["early"] = call(
            functools.partial(early_kernel, shards),
            1,
            (place, made["grad_query"], *made["gate_back"]),
            ["smem"] + [None] * 3,
            [out(early_shape, fl_type), out(early_shape, bf_type)],
            [None] * 2,
            [],
            1e6,
            "early",
            vmem=8,
        )
        return made["early"][1]

    back_chunks = reduce_chunks(keep, send, (fill_gate_back, fill_query_back, fill_grad_query))
    dquery = made["dquery"]

    early_keep, early_send = made["early"]
    early_send = tie(early_send, *back_chunks[2::2])
    early_mine = early_keep + exchange(early_send, 1, 0).astype(fl_type)
    early_pieces = tie(tuple(early_mine[e].astype(bf_type) for e in range(1, 4)))
    early_got = [exchange(p, *at) for p, at in zip(early_pieces, plane)]
    dkey, dvalue, norm_grad, keep, send = call(
        functools.partial(key_back_kernel, shards),
        1,
        (place, ids, key_slope, key, value, x_turned, made["gate_back"][1], *back_chunks),
        ["smem", "lane", "lane", "lane", "lane", "row", None] + [None] * CHUNKS,
        [
            wide(bf_type),
            wide(bf_type),
            out((8, width), fl_type),
            out(late_shape, fl_type),
            out(late_shape, bf_type),
        ],
        ["lane", "lane", None, None, None],
        [
            vmem((CHUNKS, head + PAD, half), bf_type),
            vmem((PAIRS, 2 * head, CLUSTERS * 2 * head), bf_type),
            vmem((PAIRS, 2 * head, CLUSTERS * 2 * head), bf_type),
            vmem((CLUSTERS, width, 128), fl_type),
            vmem((2, CLUSTERS * 2 * head, rows), bf_type),
            vmem((2, CLUSTERS * 2 * head, rows), bf_type),
            vmem((2 * width, width), fl_type),
        ],
        6 * work,
        "key_back",
        rows,
        vmem=26,
    )

    full_key = call(
        functools.partial(key_weights_kernel, shards),
        1,
        (place, *mine, *other),
        ["smem"] + [None] * (2 * shards),
        [out((2 * width, width), bf_type)],
        [None],
        [vmem((shards, 2 * width, span), bf_type)],
        1e6,
        "key_weights",
        vmem=12,
    )[0]

    def fill_inputs(dep):
        made["inputs"] = call(
            functools.partial(input_kernel, 2),
            2,
            (tie(place, dep), dquery, dkey, dvalue, dgate, full_query, full_key, full_gate, g),
            ["smem"] + ["lane"] * 4 + [None] * 3 + ["row"],
            [out((rows, width), fl_type)],
            ["hbm"],
            [vmem((2, rows // 2, width), fl_type), pltpu.SemaphoreType.DMA((2,))],
            4 * work,
            "inputs",
            rows // 2,
        )[0]
        return made["inputs"]

    send = tie(send, *early_got)
    mine_sum = keep + exchange(send, 1, 0).astype(fl_type)
    early_sum = tree_sum([early_mine[0], *to_float(early_got)])
    pieces = tie(tuple(mine_sum[e].astype(bf_type) for e in range(1, 4)))
    got = swap(pieces, plane, fill_inputs)
    mine_sum = jnp.concatenate([tree_sum([mine_sum[0], *got]), early_sum], axis=1)
    pieces = tie(tuple(mine_sum[z].astype(bf_type) for z in range(1, shards)))
    owned_parts = [mine_sum[0], *swap(pieces, along, fill_output, cast=False)]
    if outer > 1:
        own = tree_sum(to_float(owned_parts)).astype(bf_type)
        got = [own] + [exchange(own, 8 * o, 0) for o in range(1, outer)]
        owned_parts = [tree_sum(to_float(got))] + [jnp.zeros_like(own)] * (shards - 1)

    sums = call(
        finish_kernel,
        1,
        owned_parts,
        [None] * shards,
        [out((height, span), bf_type)],
        [None],
        [],
        1e6,
        "finish",
        vmem=4,
    )[0]
    parts = spread(sums)
    squares = call(
        squares_kernel,
        1,
        parts,
        [None] * CHUNKS,
        [out((8, 128), fl_type)],
        [None],
        [],
        1e6,
        "squares",
        vmem=4,
    )[0]

    def fill_assemble(dep):
        made["grads"] = call(
            assemble_kernel,
            1,
            (tie(place, dep), *parts),
            ["smem"] + [None] * CHUNKS,
            [out((span, 4 * width), fl_type), out((span, width), fl_type)],
            [None] * 2,
            [vmem((CHUNKS, height, span), fl_type)],
            1e6,
            "assemble",
            vmem=8,
        )
        return made["grads"][0]

    squares = [squares, *swap([squares] * (shards - 1), along, fill_assemble)]
    states = (pw, pm, ps, ow, om, osq, nw, nm, ns)
    like = [pw] * 4 + [ow] * 4 + [nw] * 4
    kinds = [fl_type] * 3 + [bf_type] + [fl_type] * 3 + [bf_type] + [fl_type] * 4
    grad_size, *new = call(
        functools.partial(update_kernel, shards),
        1,
        (place, *squares, *made["grads"], norm_grad, *states),
        ["smem"] + [None] * (shards + 12),
        [out((1, 1), fl_type)] + [out(s.shape, k) for s, k in zip(like, kinds)],
        [None] + ["hbm"] * 12,
        [
            vmem((3, 4, span, width), fl_type),
            vmem((4, span, width), bf_type),
            vmem((3, span, width), fl_type),
            vmem((span, width), bf_type),
            vmem((4, 2, span), fl_type),
            pltpu.SemaphoreType.DMA((24,)),
        ],
        1e6,
        "update",
    )
    return (made["output"], made["inputs"], grad_size.reshape(1), *new)


def solution(mesh):
    nodes, shards = mesh.shape["nodes"], mesh.shape["shard"]
    by_node = P(AXES, None)
    rows = P("shard", None)
    cols = P(None, "shard")
    return jax.shard_map(
        functools.partial(local, nodes, shards),
        mesh=mesh,
        in_specs=(by_node, by_node, P(AXES), P(AXES)) + (rows,) * 6 + (cols,) * 3,
        out_specs=(by_node, by_node, P()) + (rows,) * 8 + (cols,) * 4,
        check_vma=False,
    )
```
